512 devices in a mesh: adapter: 64 (over z, y), tensor: 8 (over x, core).
Axes of the slice: x: 4, y: 8, z: 8, core: 2. Of those that a mesh axis runs over, the one named last changes fastest.
Arguments:
- tokens: bfloat16 [49152, 8192], P('adapter', 'tensor'), may hold values from -6 to 6
- value_weight: bfloat16 [8192, 1024], P('tensor'), may hold values from -0.0625 to 0.0625
- adapter_down: bfloat16 [512, 64, 8192], P('adapter', None, 'tensor'), may hold values from -0.0625 to 0.0625
- adapter_up_weight: bfloat16 [512, 64, 1024], P('adapter', None, 'tensor'), may hold values from -0.75 to 0.75
- adapter_ids: int32 [49152, 1], P('adapter'), may hold values from 0 to 511, as said below
Outputs:
- values: bfloat16 [49152, 1024], P('adapter', 'tensor')
The draws below stay inside these ranges and needn't reach their ends.
Inputs may be any that keep to these rules, and one draw needn't show every extreme that they name: `adapter_ids`: adapter e is held by index e // 8 of adapter. Among the 768 tokens of one index of adapter (aligned blocks), no adapter id appears more than 3 times; in every block, all 8 adapters held by some one index of adapter each appear exactly 3 times; every adapter is used by some token.
All inputs are finite; a program needn't handle non-finite values.
Results may differ from the reference program's by a relative error of at most 0.017.
Values may be sent and summed in bfloat16 or wider, within the bound.
No kernel may reach another device: no remote copies, remote signals or barrier semaphores. Data moves between devices by JAX's collectives and lax.ppermute only.
A program may use at most 64 MiB of HBM per device.

```python
import jax
import jax.numpy as jnp
from jax import lax

D = 8192
KV = 1024
R = 64
EXP_DEV = 8
TOK_DEV = 768
ADAPTERS = 512
MOST = 3
TOKENS = 49152
N_ADAPTER = 64
N_TENSOR = 8


def draw_adapter_ids(key, part):
    blocks = TOKENS // TOK_DEV
    others = ADAPTERS - EXP_DEV
    rest = TOK_DEV - EXP_DEV * MOST
    owner_key, pool_key, place_key = jax.random.split(jax.random.fold_in(key, 7), 3)
    full_owner = jax.random.permutation(owner_key, blocks).astype(jnp.int32)
    pool_keys = jax.random.split(pool_key, blocks)
    place_keys = jax.random.split(place_key, blocks)

    def one_block(owner, pick_key, spot_key):
        heavy = owner * EXP_DEV + jnp.arange(EXP_DEV * MOST, dtype=jnp.int32) // MOST
        shuffled = jax.random.permutation(pick_key, others).astype(jnp.int32)
        picks = shuffled[jnp.arange(rest, dtype=jnp.int32) % others]
        light = picks + EXP_DEV * (picks >= owner * EXP_DEV).astype(jnp.int32)
        joined = jnp.concatenate([heavy, light])
        return joined[jax.random.permutation(spot_key, TOK_DEV)]
    drawn = jax.vmap(one_block)(full_owner, pool_keys, place_keys)
    return drawn.reshape(TOKENS, 1).astype(jnp.int32)


def steps_of(rng, extent, pieces, smallest, largest):
    def one(dim, shards_of):
        heights = jax.random.uniform(jax.random.fold_in(jax.random.fold_in(rng, 6), dim), (shards_of,), jnp.float32, smallest / len(pieces), largest / len(pieces))
        return jnp.repeat(jnp.exp(heights), extent[dim] // shards_of).reshape((-1,) + (1,) * (len(extent) - dim - 1))

    factor_of = one(*pieces[0])
    for cut in pieces[1:]:
        factor_of = factor_of * one(*cut)
    return factor_of


def bell_draw(own_key, extent, deviation, bound, cuts=(), held_as=jnp.bfloat16):
    gain = steps_of(own_key, extent, cuts, -0.22, 0.18) if cuts else 1.0
    entries = jax.random.normal(own_key, extent, jnp.float32) * deviation * gain
    return jnp.minimum(jnp.maximum(entries, -bound), bound).astype(held_as)


def setup_inputs(seed: int = 0) -> dict:
    keys = jax.random.split(jax.random.key(seed), 6)
    return {
        "tokens": bell_draw(keys[0], (TOKENS, D), 1.0, 6.0, ((0, 64), (1, 8))),
        "value_weight": bell_draw(keys[1], (D, KV), D ** -0.5, 0.0625, ((0, 8),)),
        "adapter_down": bell_draw(keys[2], (ADAPTERS, R, D), D ** -0.5, 0.0625, ((0, 64), (2, 8))),
        "adapter_up_weight": bell_draw(keys[3], (ADAPTERS, R, KV), R ** -0.5, 0.75, ((0, 64), (2, 8))),
        "adapter_ids": draw_adapter_ids(jax.random.fold_in(keys[5], 71), 0),
    }


adapter_output_scale = 2.0


def reference(tokens, value_weight, adapter_down, adapter_up_weight, adapter_ids):
    group = D // N_TENSOR
    base = jnp.zeros((TOKENS, KV), jnp.float32)
    for g in range(N_TENSOR):
        part = jnp.dot(tokens[:, g * group:(g + 1) * group], value_weight[g * group:(g + 1) * group, :], preferred_element_type=jnp.float32)
        part = lax.optimization_barrier(part.astype(jnp.bfloat16))
        base = base + part.astype(jnp.float32)
    ids = adapter_ids[:, 0].astype(jnp.int32)
    order = jnp.argsort(ids, stable=True).astype(jnp.int32)
    sorted_ids = ids[order]
    first = jnp.searchsorted(sorted_ids, sorted_ids, side="left").astype(jnp.int32)
    rank_sorted = jnp.arange(TOKENS, dtype=jnp.int32) - first
    rank = jnp.zeros((TOKENS,), jnp.int32).at[order].set(rank_sorted)
    capacity = N_ADAPTER * MOST
    table = jnp.full((ADAPTERS, capacity), TOKENS, jnp.int32).at[ids, rank].set(jnp.arange(TOKENS, dtype=jnp.int32))
    padded = jnp.concatenate([tokens, jnp.zeros((1, D), tokens.dtype)], axis=0)

    def one_adapter(selected_adapter):
        rows = padded[table[selected_adapter]]
        rank_activations = jnp.dot(rows, adapter_down[selected_adapter].T, preferred_element_type=jnp.float32).astype(jnp.bfloat16)
        adapter_contribution = adapter_output_scale * jnp.dot(rank_activations, adapter_up_weight[selected_adapter], preferred_element_type=jnp.float32)
        return adapter_contribution.astype(jnp.bfloat16)

    stacked = lax.map(one_adapter, jnp.arange(ADAPTERS, dtype=jnp.int32))
    delta = stacked[ids, rank]
    return (base + delta.astype(jnp.float32)).astype(jnp.bfloat16)
```

```python
import jax
import jax.numpy as jnp
from jax import lax
from jax.experimental import pallas as pl
from jax.experimental.pallas import tpu as pltpu
from jax.sharding import Mesh
from jax.sharding import PartitionSpec as P

TENSOR = ("tensor_0", "tensor_1")
MOST = 3

adapter_output_scale = 2.0


def swap(x, axes):
    return lax.all_to_all(x, axes, split_axis=0, concat_axis=0, tiled=True)


def place_rows(ids_row, ids_col, tokens, slots):
    rows, width = tokens.shape
    tile = 256

    def kernel(row_ref, col_ref, tok_ref, out_ref, at_col_ref, at_row_ref):
        @pl.when(pl.program_id(0) == 0)
        def _():
            row = row_ref[...]
            col = col_ref[...]
            same = row == col
            i = lax.broadcasted_iota(jnp.int32, (rows, rows), 0)
            j = lax.broadcasted_iota(jnp.int32, (rows, rows), 1)
            before_row = jnp.sum(jnp.where(same & (i < j), 1, 0), axis=0, keepdims=True)
            before_col = jnp.sum(jnp.where(same & (j < i), 1, 0), axis=1, keepdims=True)
            at_row_ref[...] = row * MOST + before_row
            at_col_ref[...] = col * MOST + before_col

        first = pl.program_id(0) * tile
        slot = lax.broadcasted_iota(jnp.int32, (tile, rows), 0) + first
        pick = jnp.where(slot == at_row_ref[...], 1.0, 0.0).astype(jnp.bfloat16)
        out_ref[...] = jnp.dot(pick, tok_ref[...], preferred_element_type=jnp.float32).astype(
            jnp.bfloat16
        )

    return pl.pallas_call(
        kernel,
        grid=(slots // tile,),
        in_specs=[
            pl.BlockSpec((1, rows), lambda i: (0, 0)),
            pl.BlockSpec((rows, 1), lambda i: (0, 0)),
            pl.BlockSpec((rows, width), lambda i: (0, 0)),
        ],
        out_specs=[
            pl.BlockSpec((tile, width), lambda i: (i, 0)),
            pl.BlockSpec((rows, 1), lambda i: (0, 0)),
        ],
        out_shape=[
            jax.ShapeDtypeStruct((slots, width), tokens.dtype),
            jax.ShapeDtypeStruct((rows, 1), jnp.int32),
        ],
        scratch_shapes=[pltpu.VMEM((1, rows), jnp.int32)],
        name="place_rows",
    )(ids_row, ids_col, tokens)


def value_pieces(tokens, weight, pieces):
    rows, width = tokens.shape
    cols = weight.shape[1] // pieces
    step = 2

    def kernel(tok_ref, w_ref, out_ref):
        part = jnp.dot(tok_ref[...], w_ref[...], preferred_element_type=jnp.float32)
        part = part.astype(jnp.bfloat16)
        for k in range(step):
            out_ref[k] = part[:, k * cols : (k + 1) * cols]

    return pl.pallas_call(
        kernel,
        grid=(pieces // step,),
        in_specs=[
            pl.BlockSpec((rows, width), lambda i: (0, 0)),
            pl.BlockSpec((width, step * cols), lambda i: (0, i)),
        ],
        out_specs=pl.BlockSpec((step, rows, cols), lambda i: (i, 0, 0)),
        out_shape=jax.ShapeDtypeStruct((pieces, rows, cols), jnp.bfloat16),
        name="value_pieces",
    )(tokens, weight)


def adapter_of(shape, first, group):
    slot = lax.broadcasted_iota(jnp.int32, shape, 0) + first
    return slot % group // MOST


def down_rows(arrived, down):
    slots, width = arrived.shape
    here, rank, _ = down.shape
    group = here * MOST
    half = slots // 2
    tile = 192
    pair = 2 * rank

    def kernel(lo_ref, hi_ref, down_ref, out_ref):
        weight = down_ref[...].reshape(here * rank, width)
        lane = lax.broadcasted_iota(jnp.int32, (tile, pair), 1)

        def rows_of(ref):
            full = lax.dot_general(
                ref[...], weight, (((1,), (1,)), ((), ())), preferred_element_type=jnp.float32
            )
            mine = adapter_of((tile, pair), 0, group)
            kept = jnp.zeros((tile, pair), jnp.float32)
            for k in range(here // 2):
                holder = jnp.where(lane < rank, 2 * k, 2 * k + 1)
                kept = kept + jnp.where(mine == holder, full[:, k * pair : (k + 1) * pair], 0.0)
            return kept + pltpu.roll(kept, rank, 1)

        out_ref[...] = jnp.where(lane < rank, rows_of(lo_ref), rows_of(hi_ref)).astype(
            jnp.bfloat16
        )

    steps = half // tile
    return pl.pallas_call(
        kernel,
        grid=(steps,),
        in_specs=[
            pl.BlockSpec((tile, width), lambda i: (i, 0)),
            pl.BlockSpec((tile, width), lambda i: (i + steps, 0)),
            pl.BlockSpec((here, rank, width), lambda i: (0, 0, 0)),
        ],
        out_specs=pl.BlockSpec((tile, pair), lambda i: (i, 0)),
        out_shape=jax.ShapeDtypeStruct((half, pair), jnp.bfloat16),
        name="down_rows",
    )(arrived, arrived, down)


def up_rows(low, up):
    half, pair = low.shape
    here, rank, cols = up.shape
    group = here * MOST

    def kernel(low_ref, up_ref, out_ref):
        weight = up_ref[...].reshape(here * rank, cols)
        low_wide = low_ref[...].astype(jnp.float32)
        turned = pltpu.roll(low_wide, rank, 1)
        lane = lax.broadcasted_iota(jnp.int32, (half, pair), 1)
        mine = adapter_of((half, pair), 0, group)
        for h in range(2):
            own = (lane < rank) == (h == 0)
            both = jnp.where(own, low_wide, turned)
            spread = []
            for k in range(here // 2):
                holder = jnp.where(lane < rank, 2 * k, 2 * k + 1)
                spread.append(jnp.where(mine == holder, both, 0.0).astype(jnp.bfloat16))
            acc = jnp.dot(
                jnp.concatenate(spread, axis=1), weight, preferred_element_type=jnp.float32
            )
            out_ref[h * half : (h + 1) * half, :] = (adapter_output_scale * acc).astype(
                jnp.bfloat16
            )

    return pl.pallas_call(
        kernel,
        out_shape=jax.ShapeDtypeStruct((2 * half, cols), jnp.bfloat16),
        name="up_rows",
    )(low, up)


def take_rows(at_col, back, base):
    rows, cols = base.shape
    slots = back.shape[0]

    def kernel(at_ref, back_ref, base_ref, out_ref):
        slot = lax.broadcasted_iota(jnp.int32, (rows, slots), 1)
        pick = jnp.where(slot == at_ref[...], 1.0, 0.0).astype(jnp.bfloat16)
        mine = jnp.dot(pick, back_ref[...], preferred_element_type=jnp.float32)
        out_ref[...] = (base_ref[...] + mine).astype(jnp.bfloat16)

    return pl.pallas_call(
        kernel,
        out_shape=jax.ShapeDtypeStruct((rows, cols), jnp.bfloat16),
        name="take_rows",
    )(at_col, back, base)


def per_device(tokens, value_weight, adapter_down, adapter_up_weight, adapter_ids):
    owners = lax.axis_size("adapter")
    groups = lax.axis_size(TENSOR)
    here, rank, _ = adapter_down.shape
    rows, width = tokens.shape
    cols = adapter_up_weight.shape[2]
    share = here * MOST
    slots = owners * share

    placed, at_col = place_rows(adapter_ids.reshape(1, rows), adapter_ids, tokens, slots)
    pieces = value_pieces(tokens, value_weight, groups)
    arrived_base = swap(pieces, TENSOR)
    arrived = swap(placed.reshape(owners, share, width), "adapter").reshape(slots, width)

    low_part = down_rows(arrived, adapter_down)
    low_sum = swap(low_part.reshape(groups, -1, 2 * rank), TENSOR)
    low_share = low_sum.astype(jnp.float32).sum(axis=0).astype(jnp.bfloat16)
    low = lax.all_gather(low_share, TENSOR[1], axis=0, tiled=True)
    low = lax.all_gather(low, TENSOR[0], axis=0, tiled=True)

    delta = up_rows(low, adapter_up_weight)
    back = swap(delta.reshape(owners, share, cols), "adapter").reshape(slots, cols)
    base = arrived_base.astype(jnp.float32).sum(axis=0)
    return take_rows(at_col, back, base)


def solution(mesh):
    torus = Mesh(
        mesh.devices.reshape(mesh.shape["adapter"], 4, 2), ("adapter", "tensor_0", "tensor_1")
    )
    return jax.shard_map(
        per_device,
        mesh=torus,
        in_specs=(
            P("adapter", TENSOR),
            P(TENSOR, None),
            P("adapter", None, TENSOR),
            P("adapter", None, TENSOR),
            P("adapter", None),
        ),
        out_specs=P("adapter", TENSOR),
        check_vma=False,
    )
```

```python
import jax
import jax.numpy as jnp
from jax import lax
from jax.experimental import pallas as pl
from jax.experimental.pallas import tpu as pltpu
from jax.sharding import Mesh
from jax.sharding import PartitionSpec as P


TENSOR = ("tensor_0", "tensor_1")
MOST = 3
GRANT = pltpu.CompilerParams(vmem_limit_bytes=16 * 2**20)

adapter_output_scale = 2.0


def swap(x, axes):
    return lax.all_to_all(x, axes, split_axis=0, concat_axis=0, tiled=True)


def place_rows(ids_row, tokens, slots):
    rows, width = tokens.shape
    tile = 256

    def kernel(row_ref, tok_ref, out_ref, at_col_ref, at_row_ref):
        @pl.when(pl.program_id(0) == 0)
        def _():
            row = row_ref[...]
            col = jnp.broadcast_to(row, (128, rows)).T[:, :1]
            same = row == col
            i = lax.broadcasted_iota(jnp.int32, (rows, rows), 0)
            j = lax.broadcasted_iota(jnp.int32, (rows, rows), 1)
            before_row = jnp.sum(jnp.where(same & (i < j), 1, 0), axis=0, keepdims=True)
            before_col = jnp.sum(jnp.where(same & (j < i), 1, 0), axis=1, keepdims=True)
            at_row_ref[...] = row * MOST + before_row
            at_col_ref[...] = col * MOST + before_col

        first = pl.program_id(0) * tile
        slot = lax.broadcasted_iota(jnp.int32, (tile, rows), 0) + first
        pick = jnp.where(slot == at_row_ref[...], 1.0, 0.0).astype(jnp.bfloat16)
        out_ref[...] = jnp.dot(pick, tok_ref[...], preferred_element_type=jnp.float32).astype(
            jnp.bfloat16
        )

    return pl.pallas_call(
        kernel,
        grid=(slots // tile,),
        in_specs=[
            pl.BlockSpec((1, rows), lambda i: (0, 0)),
            pl.BlockSpec((rows, width), lambda i: (0, 0)),
        ],
        out_specs=[
            pl.BlockSpec((tile, width), lambda i: (i, 0)),
            pl.BlockSpec((rows, 1), lambda i: (0, 0)),
        ],
        out_shape=[
            jax.ShapeDtypeStruct((slots, width), tokens.dtype),
            jax.ShapeDtypeStruct((rows, 1), jnp.int32),
        ],
        scratch_shapes=[pltpu.VMEM((1, rows), jnp.int32)],
        compiler_params=GRANT,
        name="place_rows",
    )(ids_row, tokens)


def value_pieces(tokens, weight, at, pieces):
    rows, width = tokens.shape
    cols = weight.shape[1] // pieces
    step = 2

    def kernel(at_ref, tok_ref, w_ref, *refs):
        out_refs, part_ref = refs[:-1], refs[-1]
        for first in range(0, pieces, step):
            part = jnp.dot(
                tok_ref[...],
                w_ref[:, first * cols : (first + step) * cols],
                preferred_element_type=jnp.float32,
            ).astype(jnp.bfloat16)
            for k in range(step):
                part_ref[first + k] = part[:, k * cols : (k + 1) * cols]
        for k in range(pieces):
            out_refs[k][...] = part_ref[at_ref[0] ^ k]

    return pl.pallas_call(
        kernel,
        in_specs=[
            pl.BlockSpec(memory_space=pltpu.SMEM),
            pl.BlockSpec((rows, width), lambda: (0, 0)),
            pl.BlockSpec(weight.shape, lambda: (0, 0)),
        ],
        out_shape=[jax.ShapeDtypeStruct((rows, cols), jnp.bfloat16)] * pieces,
        scratch_shapes=[pltpu.VMEM((pieces, rows, cols), jnp.bfloat16)],
        compiler_params=GRANT,
        name="value_pieces",
    )(at, tokens, weight)


def base_sum(parts):
    def kernel(*refs):
        total = refs[0][...].astype(jnp.float32)
        for ref in refs[1:-1]:
            total = total + ref[...].astype(jnp.float32)
        refs[-1][...] = total

    return pl.pallas_call(
        kernel,
        out_shape=jax.ShapeDtypeStruct(parts[0].shape, jnp.float32),
        compiler_params=GRANT,
        name="base_sum",
    )(*parts)


def adapter_of(shape, first, group):
    slot = lax.broadcasted_iota(jnp.int32, shape, 0) + first
    return slot % group // MOST


def down_rows(arrived, down):
    slots, width = arrived.shape
    here, rank, _ = down.shape
    group = here * MOST
    half = slots // 2
    tile = 192
    pair = 2 * rank

    def kernel(lo_ref, hi_ref, down_ref, out_ref):
        weight = down_ref[...].reshape(here * rank, width)
        lane = lax.broadcasted_iota(jnp.int32, (tile, pair), 1)

        def rows_of(ref):
            full = lax.dot_general(
                ref[...], weight, (((1,), (1,)), ((), ())), preferred_element_type=jnp.float32
            )
            mine = adapter_of((tile, pair), 0, group)
            kept = jnp.zeros((tile, pair), jnp.float32)
            for k in range(here // 2):
                holder = jnp.where(lane < rank, 2 * k, 2 * k + 1)
                kept = kept + jnp.where(mine == holder, full[:, k * pair : (k + 1) * pair], 0.0)
            return kept + pltpu.roll(kept, rank, 1)

        out_ref[...] = jnp.where(lane < rank, rows_of(lo_ref), rows_of(hi_ref)).astype(
            jnp.bfloat16
        )

    steps = half // tile
    return pl.pallas_call(
        kernel,
        grid=(steps,),
        in_specs=[
            pl.BlockSpec((tile, width), lambda i: (i, 0)),
            pl.BlockSpec((tile, width), lambda i: (i + steps, 0)),
            pl.BlockSpec((here, rank, width), lambda i: (0, 0, 0)),
        ],
        out_specs=pl.BlockSpec((tile, pair), lambda i: (i, 0)),
        out_shape=jax.ShapeDtypeStruct((half, pair), jnp.bfloat16),
        compiler_params=GRANT,
        name="down_rows",
    )(arrived, arrived, down)


def up_rows(low, up):
    half, pair = low.shape
    here, rank, cols = up.shape
    group = here * MOST

    def kernel(low_ref, up_ref, out_ref):
        weight = up_ref[...].reshape(here * rank, cols)
        low_wide = low_ref[...].astype(jnp.float32)
        turned = pltpu.roll(low_wide, rank, 1)
        lane = lax.broadcasted_iota(jnp.int32, (half, pair), 1)
        mine = adapter_of((half, pair), 0, group)
        for h in range(2):
            own = (lane < rank) == (h == 0)
            both = jnp.where(own, low_wide, turned)
            spread = []
            for k in range(here // 2):
                holder = jnp.where(lane < rank, 2 * k, 2 * k + 1)
                spread.append(jnp.where(mine == holder, both, 0.0).astype(jnp.bfloat16))
            acc = jnp.dot(
                jnp.concatenate(spread, axis=1), weight, preferred_element_type=jnp.float32
            )
            out_ref[h * half : (h + 1) * half, :] = (adapter_output_scale * acc).astype(
                jnp.bfloat16
            )

    return pl.pallas_call(
        kernel,
        out_shape=jax.ShapeDtypeStruct((2 * half, cols), jnp.bfloat16),
        compiler_params=GRANT,
        name="up_rows",
    )(low, up)


def take_rows(at_col, back, base):
    rows, cols = base.shape
    slots = back.shape[0]

    def kernel(at_ref, back_ref, base_ref, out_ref):
        slot = lax.broadcasted_iota(jnp.int32, (rows, slots), 1)
        pick = jnp.where(slot == at_ref[...], 1.0, 0.0).astype(jnp.bfloat16)
        mine = jnp.dot(pick, back_ref[...], preferred_element_type=jnp.float32)
        out_ref[...] = (base_ref[...] + mine).astype(jnp.bfloat16)

    return pl.pallas_call(
        kernel,
        out_shape=jax.ShapeDtypeStruct((rows, cols), jnp.bfloat16),
        compiler_params=GRANT,
        name="take_rows",
    )(at_col, back, base)


def layer(tokens, value_weight, adapter_down, adapter_up_weight, adapter_ids):
    owners = lax.axis_size("adapter")
    groups = lax.axis_size(TENSOR)
    here, rank, _ = adapter_down.shape
    rows, width = tokens.shape
    cols = adapter_up_weight.shape[2]
    share = here * MOST
    slots = owners * share

    placed, at_col = place_rows(adapter_ids.reshape(1, rows), tokens, slots)
    arrived = swap(placed.reshape(owners, share, width), "adapter")
    arrived = arrived.reshape(slots, width)
    at = lax.axis_index(TENSOR).astype(jnp.int32).reshape(1)
    pieces = value_pieces(tokens, value_weight, at, groups)
    parts = [pieces[0]]
    for k in range(1, groups):
        parts.append(lax.ppermute(pieces[k], TENSOR, [(i, i ^ k) for i in range(groups)]))
    base = base_sum(parts)

    low_part = down_rows(arrived, adapter_down)
    low_sum = swap(low_part.reshape(groups, -1, 2 * rank), TENSOR)
    low_share = low_sum.astype(jnp.float32).sum(axis=0).astype(jnp.bfloat16)
    copies = jnp.broadcast_to(low_share[None], (groups, *low_share.shape))
    low = swap(copies, TENSOR).reshape(slots // 2, 2 * rank)

    delta = up_rows(low, adapter_up_weight)
    back = swap(delta.reshape(owners, share, cols), "adapter").reshape(slots, cols)
    return take_rows(at_col, back, base)


def solution(mesh):
    torus = Mesh(
        mesh.devices.reshape(mesh.shape["adapter"], 4, 2), ("adapter", "tensor_0", "tensor_1")
    )
    return jax.shard_map(
        layer,
        mesh=torus,
        in_specs=(
            P("adapter", TENSOR),
            P(TENSOR, None),
            P("adapter", None, TENSOR),
            P("adapter", None, TENSOR),
            P("adapter", None),
        ),
        out_specs=P("adapter", TENSOR),
        check_vma=False,
    )
```

```python
import jax
import jax.numpy as jnp
from jax import lax
from jax.experimental import pallas as pl
from jax.experimental.pallas import tpu as pltpu
from jax.sharding import Mesh
from jax.sharding import PartitionSpec as P


TENSOR = ("tensor_0", "tensor_1")
ADAPTER = ("z", "y")
HERE = 8
MOST = 3
MAIN = 2
SIDE = 16
LOST = 3e38
GRANT = pltpu.CompilerParams(vmem_limit_bytes=16 * 2**20)

adapter_output_scale = 2.0


def swap(x, axes):
    return lax.all_to_all(x, axes, split_axis=0, concat_axis=0, tiled=True)


def full_place(ids_row, tokens, slots):
    rows, width = tokens.shape
    tile = 256

    def kernel(row_ref, tok_ref, out_ref, at_col_ref, at_row_ref):
        @pl.when(pl.program_id(0) == 0)
        def _():
            row = row_ref[...]
            col = jnp.broadcast_to(row, (128, rows)).T[:, :1]
            same = row == col
            i = lax.broadcasted_iota(jnp.int32, (rows, rows), 0)
            j = lax.broadcasted_iota(jnp.int32, (rows, rows), 1)
            before_row = jnp.sum(jnp.where(same & (i < j), 1, 0), axis=0, keepdims=True)
            before_col = jnp.sum(jnp.where(same & (j < i), 1, 0), axis=1, keepdims=True)
            at_row_ref[...] = row * MOST + before_row
            at_col_ref[...] = col * MOST + before_col

        first = pl.program_id(0) * tile
        slot = lax.broadcasted_iota(jnp.int32, (tile, rows), 0) + first
        pick = jnp.where(slot == at_row_ref[...], 1.0, 0.0).astype(jnp.bfloat16)
        out_ref[...] = jnp.dot(pick, tok_ref[...], preferred_element_type=jnp.float32).astype(
            jnp.bfloat16
        )

    return pl.pallas_call(
        kernel,
        grid=(slots // tile,),
        in_specs=[
            pl.BlockSpec((1, rows), lambda i: (0, 0)),
            pl.BlockSpec((rows, width), lambda i: (0, 0)),
        ],
        out_specs=[
            pl.BlockSpec((tile, width), lambda i: (i, 0)),
            pl.BlockSpec((rows, 1), lambda i: (0, 0)),
        ],
        out_shape=[
            jax.ShapeDtypeStruct((slots, width), tokens.dtype),
            jax.ShapeDtypeStruct((rows, 1), jnp.int32),
        ],
        scratch_shapes=[pltpu.VMEM((1, rows), jnp.int32)],
        compiler_params=GRANT,
        name="full_place",
    )(ids_row, tokens)


def value_pieces(tokens, weight, at, pieces):
    rows, width = tokens.shape
    cols = weight.shape[1] // pieces
    step = 2

    def kernel(at_ref, tok_ref, w_ref, *refs):
        out_refs, part_ref = refs[:-1], refs[-1]
        for first in range(0, pieces, step):
            part = jnp.dot(
                tok_ref[...],
                w_ref[:, first * cols : (first + step) * cols],
                preferred_element_type=jnp.float32,
            ).astype(jnp.bfloat16)
            for k in range(step):
                part_ref[first + k] = part[:, k * cols : (k + 1) * cols]
        for k in range(pieces):
            out_refs[k][...] = part_ref[at_ref[0] ^ k]

    return pl.pallas_call(
        kernel,
        in_specs=[
            pl.BlockSpec(memory_space=pltpu.SMEM),
            pl.BlockSpec((rows, width), lambda: (0, 0)),
            pl.BlockSpec(weight.shape, lambda: (0, 0)),
        ],
        out_shape=[jax.ShapeDtypeStruct((rows, cols), jnp.bfloat16)] * pieces,
        scratch_shapes=[pltpu.VMEM((pieces, rows, cols), jnp.bfloat16)],
        compiler_params=GRANT,
        name="value_pieces",
    )(at, tokens, weight)


def base_sum(parts):
    def kernel(*refs):
        total = refs[0][...].astype(jnp.float32)
        for ref in refs[1:-1]:
            total = total + ref[...].astype(jnp.float32)
        refs[-1][...] = total

    return pl.pallas_call(
        kernel,
        out_shape=jax.ShapeDtypeStruct(parts[0].shape, jnp.float32),
        compiler_params=GRANT,
        name="base_sum",
    )(*parts)


def adapter_of(shape, first, group):
    slot = lax.broadcasted_iota(jnp.int32, shape, 0) + first
    return slot % group // MOST


def full_down(arrived, down):
    slots, width = arrived.shape
    here, rank, _ = down.shape
    group = here * MOST
    half = slots // 2
    tile = 192
    pair = 2 * rank

    def kernel(lo_ref, hi_ref, down_ref, out_ref):
        weight = down_ref[...].reshape(here * rank, width)
        lane = lax.broadcasted_iota(jnp.int32, (tile, pair), 1)

        def rows_of(ref):
            full = lax.dot_general(
                ref[...], weight, (((1,), (1,)), ((), ())), preferred_element_type=jnp.float32
            )
            mine = adapter_of((tile, pair), 0, group)
            kept = jnp.zeros((tile, pair), jnp.float32)
            for k in range(here // 2):
                holder = jnp.where(lane < rank, 2 * k, 2 * k + 1)
                kept = kept + jnp.where(mine == holder, full[:, k * pair : (k + 1) * pair], 0.0)
            return kept + pltpu.roll(kept, rank, 1)

        out_ref[...] = jnp.where(lane < rank, rows_of(lo_ref), rows_of(hi_ref)).astype(
            jnp.bfloat16
        )

    steps = half // tile
    return pl.pallas_call(
        kernel,
        grid=(steps,),
        in_specs=[
            pl.BlockSpec((tile, width), lambda i: (i, 0)),
            pl.BlockSpec((tile, width), lambda i: (i + steps, 0)),
            pl.BlockSpec((here, rank, width), lambda i: (0, 0, 0)),
        ],
        out_specs=pl.BlockSpec((tile, pair), lambda i: (i, 0)),
        out_shape=jax.ShapeDtypeStruct((half, pair), jnp.bfloat16),
        compiler_params=GRANT,
        name="full_down",
    )(arrived, arrived, down)


def full_up(low, up):
    half, pair = low.shape
    here, rank, cols = up.shape
    group = here * MOST

    def kernel(low_ref, up_ref, out_ref):
        weight = up_ref[...].reshape(here * rank, cols)
        low_wide = low_ref[...].astype(jnp.float32)
        turned = pltpu.roll(low_wide, rank, 1)
        lane = lax.broadcasted_iota(jnp.int32, (half, pair), 1)
        mine = adapter_of((half, pair), 0, group)
        for h in range(2):
            own = (lane < rank) == (h == 0)
            both = jnp.where(own, low_wide, turned)
            spread = []
            for k in range(here // 2):
                holder = jnp.where(lane < rank, 2 * k, 2 * k + 1)
                spread.append(jnp.where(mine == holder, both, 0.0).astype(jnp.bfloat16))
            acc = jnp.dot(
                jnp.concatenate(spread, axis=1), weight, preferred_element_type=jnp.float32
            )
            out_ref[h * half : (h + 1) * half, :] = (adapter_output_scale * acc).astype(
                jnp.bfloat16
            )

    return pl.pallas_call(
        kernel,
        out_shape=jax.ShapeDtypeStruct((2 * half, cols), jnp.bfloat16),
        compiler_params=GRANT,
        name="full_up",
    )(low, up)


def full_take(at_col, back, base):
    rows, cols = base.shape
    slots = back.shape[0]

    def kernel(at_ref, back_ref, base_ref, out_ref):
        slot = lax.broadcasted_iota(jnp.int32, (rows, slots), 1)
        pick = jnp.where(slot == at_ref[...], 1.0, 0.0).astype(jnp.bfloat16)
        mine = jnp.dot(pick, back_ref[...], preferred_element_type=jnp.float32)
        out_ref[...] = (base_ref[...] + mine).astype(jnp.bfloat16)

    return pl.pallas_call(
        kernel,
        out_shape=jax.ShapeDtypeStruct((rows, cols), jnp.bfloat16),
        compiler_params=GRANT,
        name="full_take",
    )(at_col, back, base)


def scalar_spec():
    return pl.BlockSpec(memory_space=pltpu.SMEM)


def count_before(row, col, also_col=None):
    n = row.shape[1]
    j = lax.broadcasted_iota(jnp.int32, (n, n), 0)
    i = lax.broadcasted_iota(jnp.int32, (n, n), 1)
    hit = (row == col) & (j < i)
    if also_col is not None:
        hit = hit & also_col
    return jnp.sum(jnp.where(hit, 1, 0), axis=0, keepdims=True)


def to_col(row):
    return jnp.broadcast_to(row, (128, row.shape[1])).T[:, :1]


def pick_rows(at_row, slots, first=0):
    n = at_row.shape[1]
    slot = lax.broadcasted_iota(jnp.int32, (slots, n), 0) + first
    return jnp.where(slot == at_row, 1.0, 0.0).astype(jnp.bfloat16)


def place_main(ids_row, tokens, slots):
    rows, width = tokens.shape
    tile = 256

    def kernel(row_ref, tok_ref, out_ref, seen_ref, at_col_ref):
        @pl.when(pl.program_id(0) == 0)
        def _():
            row = row_ref[...]
            seen = count_before(row, to_col(row))
            seen_ref[...] = seen
            spot = row % HERE
            back = row // HERE * (HERE * MOST) + jnp.where(
                seen < MAIN, spot * MAIN + seen, HERE * MAIN + spot
            )
            at_col_ref[...] = to_col(back)

        at_row = jnp.where(seen_ref[...] < MAIN, row_ref[...] * MAIN + seen_ref[...], -1)
        pick = pick_rows(at_row, tile, pl.program_id(0) * tile)
        out_ref[...] = jnp.dot(pick, tok_ref[...], preferred_element_type=jnp.float32).astype(
            jnp.bfloat16
        )

    return pl.pallas_call(
        kernel,
        grid=(slots // tile,),
        in_specs=[
            pl.BlockSpec((1, rows), lambda i: (0, 0)),
            pl.BlockSpec((rows, width), lambda i: (0, 0)),
        ],
        out_specs=[
            pl.BlockSpec((tile, width), lambda i: (i, 0)),
            pl.BlockSpec((1, rows), lambda i: (0, 0)),
            pl.BlockSpec((rows, 1), lambda i: (0, 0)),
        ],
        out_shape=[
            jax.ShapeDtypeStruct((slots, width), tokens.dtype),
            jax.ShapeDtypeStruct((1, rows), jnp.int32),
            jax.ShapeDtypeStruct((rows, 1), jnp.int32),
        ],
        compiler_params=GRANT,
        name="place_main",
    )(ids_row, tokens)


def bucket(rows_of, key, key_col, code, valid, valid_col, flag, out_refs, block_ref, at):
    n = key.shape[1]
    width = rows_of.shape[1]
    q = count_before(key, key_col, valid_col)
    fits = valid & (q < SIDE - 1)
    lost = jnp.max(jnp.where(valid & (q >= SIDE - 1), 1.0, 0.0), axis=1, keepdims=True)
    flag = jnp.maximum(flag, lost)
    pick = pick_rows(jnp.where(fits, key * SIDE + q, -1), 8 * SIDE)
    data = jnp.dot(pick, rows_of, preferred_element_type=jnp.float32)
    which = lax.broadcasted_iota(jnp.int32, (8, n), 0)
    owned = jnp.where(fits & (which == key), (code + 1).astype(jnp.float32), 0.0)
    place = lax.broadcasted_iota(jnp.int32, (128, n), 0)
    there = jnp.where(place == q, 1.0, 0.0)
    codes = lax.dot_general(
        owned.astype(jnp.bfloat16),
        there.astype(jnp.bfloat16),
        (((1,), (1,)), ((), ())),
        preferred_element_type=jnp.float32,
    )
    lane = lax.broadcasted_iota(jnp.int32, (8, 128), 1)
    codes = jnp.where(lane == 127, flag, codes)
    wide = jnp.concatenate([codes, jnp.zeros((8, width - 128), jnp.float32)], axis=1)
    row = lax.broadcasted_iota(jnp.int32, (SIDE, width), 0)
    for k in range(8):
        note = jnp.broadcast_to(wide[k : k + 1], (SIDE, width))
        block_ref[k] = jnp.where(
            row == SIDE - 1, note, data[k * SIDE : (k + 1) * SIDE]
        ).astype(jnp.bfloat16)
    for k in range(8):
        out_refs[k][...] = block_ref[at ^ k]


def read_codes(in_refs):
    n = 8 * SIDE
    lane = lax.broadcasted_iota(jnp.int32, (8, n), 1)
    codes = jnp.zeros((8, n), jnp.float32)
    flag = jnp.zeros((1, 1), jnp.float32)
    for k in range(8):
        block = in_refs[k][...].astype(jnp.float32)
        note = block[SIDE - 1 : SIDE, :n]
        flag = jnp.maximum(flag, note[:, 127:128])
        own = jnp.where(lane < SIDE - 1, jnp.broadcast_to(note, (8, n)), 0.0)
        codes = codes + (pltpu.roll(own, k * SIDE, 1) if k else own)
    return codes[:1].astype(jnp.int32) - 1, flag


def side_first(at, seen, ids_row, tokens):
    _, width = tokens.shape

    def kernel(at_ref, seen_ref, row_ref, tok_ref, *refs):
        row = row_ref[...]
        third = seen_ref[...] >= MAIN
        home = row // HERE
        key = home % 8
        marked = jnp.where(third, key, -1)
        bucket(
            tok_ref[...], key, to_col(marked), home // 8 * 8 + row % HERE, third, None,
            jnp.zeros((1, 1), jnp.float32), refs[:8], refs[8], at_ref[0],
        )

    return pl.pallas_call(
        kernel,
        in_specs=[scalar_spec()] + [pl.BlockSpec(memory_space=pltpu.VMEM)] * 3,
        out_shape=[jax.ShapeDtypeStruct((SIDE, width), jnp.bfloat16)] * 8,
        scratch_shapes=[pltpu.VMEM((8, SIDE, width), jnp.bfloat16)],
        compiler_params=GRANT,
        name="side_first",
    )(at, seen, ids_row, tokens)


def side_second(at, blocks):
    width = blocks[0].shape[1]
    n = 8 * SIDE

    def kernel(at_ref, *refs):
        code, flag = read_codes(refs[:8])
        valid = code >= 0
        key = jnp.where(valid, code // 8, -1)
        from_y = (lax.broadcasted_iota(jnp.int32, (1, n), 1) // SIDE) ^ at_ref[1]
        rows_of = jnp.concatenate([ref[...] for ref in refs[:8]], axis=0)
        bucket(
            rows_of, key, to_col(key), from_y * 8 + code % 8, valid, None,
            flag, refs[8:16], refs[16], at_ref[0],
        )

    return pl.pallas_call(
        kernel,
        in_specs=[scalar_spec()] + [pl.BlockSpec(memory_space=pltpu.VMEM)] * 8,
        out_shape=[jax.ShapeDtypeStruct((SIDE, width), jnp.bfloat16)] * 8,
        scratch_shapes=[pltpu.VMEM((8, SIDE, width), jnp.bfloat16)],
        compiler_params=GRANT,
        name="side_second",
    )(at, *blocks)


def fold(full, mine, rank):
    pair = 2 * rank
    lane = lax.broadcasted_iota(jnp.int32, (full.shape[0], pair), 1)
    kept = jnp.zeros((full.shape[0], pair), jnp.float32)
    for k in range(HERE // 2):
        holder = jnp.where(lane < rank, 2 * k, 2 * k + 1)
        kept = kept + jnp.where(mine == holder, full[:, k * pair : (k + 1) * pair], 0.0)
    return kept + pltpu.roll(kept, rank, 1)


def contract_last(x, y):
    return lax.dot_general(x, y, (((1,), (1,)), ((), ())), preferred_element_type=jnp.float32)


def side_low(at, blocks, down):
    here, rank, width = down.shape
    n = 8 * SIDE
    thirds = 64 * here
    pair = 2 * rank

    def kernel(at_ref, *refs):
        down_ref, out_ref, flag_ref = refs[8:]
        code, flag = read_codes(refs[:8])
        from_z = (lax.broadcasted_iota(jnp.int32, (1, n), 1) // SIDE) ^ at_ref[0]
        slot = jnp.where(code >= 0, from_z * 64 + code, -1)
        rows_of = jnp.concatenate([ref[...] for ref in refs[:8]], axis=0)
        full = contract_last(rows_of, down_ref[...].reshape(here * rank, width))
        mine = to_col(jnp.where(code >= 0, code % 8, -1))
        low = fold(full, mine, rank).astype(jnp.bfloat16)
        spread = jnp.dot(pick_rows(slot, thirds), low, preferred_element_type=jnp.float32)
        lane = lax.broadcasted_iota(jnp.int32, (thirds // 2, pair), 1)
        out_ref[...] = jnp.where(
            lane < rank, spread[: thirds // 2], spread[thirds // 2 :]
        ).astype(jnp.bfloat16)
        flag_ref[...] = jnp.broadcast_to(flag, (8, 128))

    return pl.pallas_call(
        kernel,
        in_specs=[scalar_spec()] + [pl.BlockSpec(memory_space=pltpu.VMEM)] * 9,
        out_shape=[
            jax.ShapeDtypeStruct((thirds // 2, pair), jnp.bfloat16),
            jax.ShapeDtypeStruct((8, 128), jnp.float32),
        ],
        compiler_params=GRANT,
        name="side_low",
    )(at, *blocks, down)


def down_main(arrived, thirds, down):
    slots, width = arrived.shape
    here, rank, _ = down.shape
    half = slots // 2
    tile = 256
    pair = 2 * rank

    def kernel(in_ref, thirds_ref, down_ref, out_ref):
        weight = down_ref[...].reshape(here * rank, width)
        lane = lax.broadcasted_iota(jnp.int32, (tile, pair), 1)
        slot = lax.broadcasted_iota(jnp.int32, (tile, pair), 0)
        mine = slot % (HERE * MAIN) // MAIN
        for first in range(0, half, tile):
            lo = fold(contract_last(in_ref[first : first + tile, :], weight), mine, rank)
            hi = fold(
                contract_last(in_ref[half + first : half + first + tile, :], weight), mine, rank
            )
            out_ref[first : first + tile, :] = jnp.where(lane < rank, lo, hi).astype(jnp.bfloat16)
        out_ref[half:, :] = thirds_ref[...]

    return pl.pallas_call(
        kernel,
        out_shape=jax.ShapeDtypeStruct((half + thirds.shape[0], pair), jnp.bfloat16),
        compiler_params=GRANT,
        name="down_main",
    )(arrived, thirds, down)


def up_main(low, flag, up):
    here, rank, cols = up.shape
    owners = 2 * low.shape[0] // (here * MOST)
    half = owners * here * MAIN // 2

    def kernel(low_ref, flag_ref, up_ref, out_ref):
        weight = up_ref[...].reshape(here * rank, cols)

        def mapped(part, per):
            wide = part.astype(jnp.float32)
            turned = pltpu.roll(wide, rank, 1)
            lane = lax.broadcasted_iota(jnp.int32, wide.shape, 1)
            slot = lax.broadcasted_iota(jnp.int32, wide.shape, 0)
            mine = slot % (here * per) // per
            halves = []
            for h in range(2):
                both = jnp.where((lane < rank) == (h == 0), wide, turned)
                spread = []
                for k in range(here // 2):
                    holder = jnp.where(lane < rank, 2 * k, 2 * k + 1)
                    spread.append(jnp.where(mine == holder, both, 0.0).astype(jnp.bfloat16))
                halves.append(
                    jnp.dot(
                        jnp.concatenate(spread, axis=1), weight, preferred_element_type=jnp.float32
                    )
                )
            acc = jnp.concatenate(halves, axis=0) * adapter_output_scale
            return acc.reshape(owners, here * per, cols)

        main = mapped(low_ref[:half, :], MAIN)
        thirds = mapped(low_ref[half:, :], MOST - MAIN)
        both = jnp.concatenate([main, thirds], axis=1).reshape(owners * here * MOST, cols)
        out_ref[...] = jnp.where(flag_ref[:1, :1] > 0.0, LOST, both).astype(jnp.bfloat16)

    return pl.pallas_call(
        kernel,
        out_shape=jax.ShapeDtypeStruct((owners * here * MOST, cols), jnp.bfloat16),
        compiler_params=GRANT,
        name="up_main",
    )(low, flag, up)


def take_main(at_col, back, base):
    rows, cols = base.shape
    slots = back.shape[0]

    def kernel(at_ref, back_ref, base_ref, out_ref, lost_ref):
        slot = lax.broadcasted_iota(jnp.int32, (rows, slots), 1)
        pick = jnp.where(slot == at_ref[...], 1.0, 0.0).astype(jnp.bfloat16)
        mine = jnp.dot(pick, back_ref[...], preferred_element_type=jnp.float32)
        out_ref[...] = (base_ref[...] + mine).astype(jnp.bfloat16)
        lost_ref[0] = (jnp.max(back_ref[...].astype(jnp.float32)) > LOST / 2).astype(jnp.int32)

    return pl.pallas_call(
        kernel,
        out_specs=[pl.BlockSpec(memory_space=pltpu.VMEM), pl.BlockSpec(memory_space=pltpu.SMEM)],
        out_shape=[
            jax.ShapeDtypeStruct((rows, cols), jnp.bfloat16),
            jax.ShapeDtypeStruct((1,), jnp.int32),
        ],
        compiler_params=GRANT,
        name="take_main",
    )(at_col, back, base)


def low_of_all(low_part, groups):
    rows, pair = low_part.shape
    parts = swap(low_part.reshape(groups, rows // groups, pair), TENSOR)
    share = parts.astype(jnp.float32).sum(axis=0).astype(jnp.bfloat16)
    copies = jnp.broadcast_to(share[None], (groups, *share.shape))
    return swap(copies, TENSOR).reshape(rows, pair)


def whole_exchange(tokens, adapter_down, adapter_up_weight, adapter_ids, base):
    rows, width = tokens.shape
    cols = adapter_up_weight.shape[2]
    share = HERE * MOST
    slots = 64 * share
    placed, at_col = full_place(adapter_ids.reshape(1, rows), tokens, slots)
    arrived = swap(placed.reshape(64, share, width), ADAPTER).reshape(slots, width)
    low = low_of_all(full_down(arrived, adapter_down), lax.axis_size(TENSOR))
    delta = full_up(low, adapter_up_weight)
    back = swap(delta.reshape(64, share, cols), ADAPTER).reshape(slots, cols)
    return full_take(at_col, back, base)


def layer(tokens, value_weight, adapter_down, adapter_up_weight, adapter_ids):
    groups = lax.axis_size(TENSOR)
    rows, width = tokens.shape
    cols = adapter_up_weight.shape[2]
    ids_row = adapter_ids.reshape(1, rows)
    at_z = lax.axis_index("z").astype(jnp.int32)
    at_y = lax.axis_index("y").astype(jnp.int32)

    placed, seen, at_col = place_main(ids_row, tokens, 64 * HERE * MAIN)
    arrived = swap(placed.reshape(64, HERE * MAIN, width), ADAPTER)
    arrived = arrived.reshape(64 * HERE * MAIN, width)

    blocks = side_first(at_y.reshape(1), seen, ids_row, tokens)
    blocks = xor_sends(blocks, "y")
    blocks = side_second(jnp.stack([at_z, at_y]), blocks)
    blocks = xor_sends(blocks, "z")
    thirds, flag = side_low(at_z.reshape(1), blocks, adapter_down)

    at = lax.axis_index(TENSOR).astype(jnp.int32).reshape(1)
    pieces = value_pieces(tokens, value_weight, at, groups)
    pieces = xor_sends(pieces, TENSOR)
    base = base_sum(pieces)

    low = low_of_all(down_main(arrived, thirds, adapter_down), groups)
    delta = up_main(low, flag, adapter_up_weight)
    back = swap(delta.reshape(64, HERE * MOST, cols), ADAPTER).reshape(64 * HERE * MOST, cols)
    values, lost = take_main(at_col, back, base)
    return lax.cond(
        lost[0] > 0,
        lambda: whole_exchange(tokens, adapter_down, adapter_up_weight, adapter_ids, base),
        lambda: values,
    )


def xor_sends(pieces, axis):
    size = lax.axis_size(axis)
    parts = [pieces[0]]
    for k in range(1, size):
        parts.append(lax.ppermute(pieces[k], axis, [(i, i ^ k) for i in range(size)]))
    return parts


def solution(mesh):
    torus = Mesh(mesh.devices.reshape(8, 8, 4, 2), (*ADAPTER, *TENSOR))
    return jax.shard_map(
        layer,
        mesh=torus,
        in_specs=(
            P(ADAPTER, TENSOR),
            P(TENSOR, None),
            P(ADAPTER, None, TENSOR),
            P(ADAPTER, None, TENSOR),
            P(ADAPTER, None),
        ),
        out_specs=P(ADAPTER, TENSOR),
        check_vma=False,
    )
```

```python
import jax
import jax.numpy as jnp
from jax import lax
from jax.experimental import pallas as pl
from jax.experimental.pallas import tpu as pltpu
from jax.sharding import Mesh
from jax.sharding import PartitionSpec as P


TENSOR = ("tensor_0", "tensor_1")
ADAPTER = ("z", "y")
HERE = 8
MOST = 3
MAIN = 2
SIDE = 16
STAY = (0, 4, 2, 6)
LEAVE = (1, 5, 3, 7)
LOST = 3e38
GRANT = pltpu.CompilerParams(vmem_limit_bytes=16 * 2**20)

adapter_output_scale = 2.0


def swap(x, axes):
    return lax.all_to_all(x, axes, split_axis=0, concat_axis=0, tiled=True)


def full_place(ids_row, tokens, slots):
    rows, width = tokens.shape
    tile = 256

    def kernel(row_ref, tok_ref, out_ref, at_col_ref, at_row_ref):
        @pl.when(pl.program_id(0) == 0)
        def _():
            row = row_ref[...]
            col = jnp.broadcast_to(row, (128, rows)).T[:, :1]
            same = row == col
            i = lax.broadcasted_iota(jnp.int32, (rows, rows), 0)
            j = lax.broadcasted_iota(jnp.int32, (rows, rows), 1)
            before_row = jnp.sum(jnp.where(same & (i < j), 1, 0), axis=0, keepdims=True)
            before_col = jnp.sum(jnp.where(same & (j < i), 1, 0), axis=1, keepdims=True)
            at_row_ref[...] = row * MOST + before_row
            at_col_ref[...] = col * MOST + before_col

        first = pl.program_id(0) * tile
        slot = lax.broadcasted_iota(jnp.int32, (tile, rows), 0) + first
        pick = jnp.where(slot == at_row_ref[...], 1.0, 0.0).astype(jnp.bfloat16)
        out_ref[...] = jnp.dot(pick, tok_ref[...], preferred_element_type=jnp.float32).astype(
            jnp.bfloat16
        )

    return pl.pallas_call(
        kernel,
        grid=(slots // tile,),
        in_specs=[
            pl.BlockSpec((1, rows), lambda i: (0, 0)),
            pl.BlockSpec((rows, width), lambda i: (0, 0)),
        ],
        out_specs=[
            pl.BlockSpec((tile, width), lambda i: (i, 0)),
            pl.BlockSpec((rows, 1), lambda i: (0, 0)),
        ],
        out_shape=[
            jax.ShapeDtypeStruct((slots, width), tokens.dtype),
            jax.ShapeDtypeStruct((rows, 1), jnp.int32),
        ],
        scratch_shapes=[pltpu.VMEM((1, rows), jnp.int32)],
        compiler_params=GRANT,
        name="full_place",
    )(ids_row, tokens)


def value_pieces(tokens, weight, at, pieces):
    rows, width = tokens.shape
    cols = weight.shape[1] // pieces
    step = 2

    def kernel(at_ref, tok_ref, w_ref, own_ref, other_ref, part_ref):
        for first in range(0, pieces, step):
            part = jnp.dot(
                tok_ref[...],
                w_ref[:, first * cols : (first + step) * cols],
                preferred_element_type=jnp.float32,
            ).astype(jnp.bfloat16)
            for k in range(step):
                part_ref[first + k] = part[:, k * cols : (k + 1) * cols]
        for k in range(pieces // 2):
            own_ref[k] = part_ref[at_ref[0] ^ (2 * k)]
            other_ref[k] = part_ref[at_ref[0] ^ (2 * k + 1)]

    return pl.pallas_call(
        kernel,
        in_specs=[
            pl.BlockSpec(memory_space=pltpu.SMEM),
            pl.BlockSpec((rows, width), lambda: (0, 0)),
            pl.BlockSpec(weight.shape, lambda: (0, 0)),
        ],
        out_shape=[jax.ShapeDtypeStruct((pieces // 2, rows, cols), jnp.bfloat16)] * 2,
        scratch_shapes=[pltpu.VMEM((pieces, rows, cols), jnp.bfloat16)],
        compiler_params=GRANT,
        name="value_pieces",
    )(at, tokens, weight)


def pair_sum(own, other):
    count, rows, cols = own.shape

    def kernel(own_ref, other_ref, *out_refs):
        for k in range(1, count):
            total = own_ref[k].astype(jnp.float32) + other_ref[k].astype(jnp.float32)
            out_refs[k - 1][...] = total.astype(jnp.bfloat16)

    return pl.pallas_call(
        kernel,
        out_shape=[jax.ShapeDtypeStruct((rows, cols), jnp.bfloat16)] * (count - 1),
        compiler_params=GRANT,
        name="pair_sum",
    )(own, other)


def base_sum(own, other, parts):
    def kernel(own_ref, other_ref, *refs):
        total = own_ref[0].astype(jnp.float32) + other_ref[0].astype(jnp.float32)
        for ref in refs[:-1]:
            total = total + ref[...].astype(jnp.float32)
        refs[-1][...] = total

    return pl.pallas_call(
        kernel,
        out_shape=jax.ShapeDtypeStruct(parts[0].shape, jnp.float32),
        compiler_params=GRANT,
        name="base_sum",
    )(own, other, *parts)


def adapter_of(shape, first, group):
    slot = lax.broadcasted_iota(jnp.int32, shape, 0) + first
    return slot % group // MOST


def full_down(arrived, down):
    slots, width = arrived.shape
    here, rank, _ = down.shape
    group = here * MOST
    half = slots // 2
    tile = 192
    pair = 2 * rank

    def kernel(lo_ref, hi_ref, down_ref, out_ref):
        weight = down_ref[...].reshape(here * rank, width)
        lane = lax.broadcasted_iota(jnp.int32, (tile, pair), 1)

        def rows_of(ref):
            full = lax.dot_general(
                ref[...], weight, (((1,), (1,)), ((), ())), preferred_element_type=jnp.float32
            )
            mine = adapter_of((tile, pair), 0, group)
            kept = jnp.zeros((tile, pair), jnp.float32)
            for k in range(here // 2):
                holder = jnp.where(lane < rank, 2 * k, 2 * k + 1)
                kept = kept + jnp.where(mine == holder, full[:, k * pair : (k + 1) * pair], 0.0)
            return kept + pltpu.roll(kept, rank, 1)

        out_ref[...] = jnp.where(lane < rank, rows_of(lo_ref), rows_of(hi_ref)).astype(
            jnp.bfloat16
        )

    steps = half // tile
    return pl.pallas_call(
        kernel,
        grid=(steps,),
        in_specs=[
            pl.BlockSpec((tile, width), lambda i: (i, 0)),
            pl.BlockSpec((tile, width), lambda i: (i + steps, 0)),
            pl.BlockSpec((here, rank, width), lambda i: (0, 0, 0)),
        ],
        out_specs=pl.BlockSpec((tile, pair), lambda i: (i, 0)),
        out_shape=jax.ShapeDtypeStruct((half, pair), jnp.bfloat16),
        compiler_params=GRANT,
        name="full_down",
    )(arrived, arrived, down)


def full_up(low, up):
    half, pair = low.shape
    here, rank, cols = up.shape
    group = here * MOST

    def kernel(low_ref, up_ref, out_ref):
        weight = up_ref[...].reshape(here * rank, cols)
        low_wide = low_ref[...].astype(jnp.float32)
        turned = pltpu.roll(low_wide, rank, 1)
        lane = lax.broadcasted_iota(jnp.int32, (half, pair), 1)
        mine = adapter_of((half, pair), 0, group)
        for h in range(2):
            own = (lane < rank) == (h == 0)
            both = jnp.where(own, low_wide, turned)
            spread = []
            for k in range(here // 2):
                holder = jnp.where(lane < rank, 2 * k, 2 * k + 1)
                spread.append(jnp.where(mine == holder, both, 0.0).astype(jnp.bfloat16))
            acc = jnp.dot(
                jnp.concatenate(spread, axis=1), weight, preferred_element_type=jnp.float32
            )
            out_ref[h * half : (h + 1) * half, :] = (adapter_output_scale * acc).astype(
                jnp.bfloat16
            )

    return pl.pallas_call(
        kernel,
        out_shape=jax.ShapeDtypeStruct((2 * half, cols), jnp.bfloat16),
        compiler_params=GRANT,
        name="full_up",
    )(low, up)


def full_take(at_col, back, base):
    rows, cols = base.shape
    slots = back.shape[0]

    def kernel(at_ref, back_ref, base_ref, out_ref):
        slot = lax.broadcasted_iota(jnp.int32, (rows, slots), 1)
        pick = jnp.where(slot == at_ref[...], 1.0, 0.0).astype(jnp.bfloat16)
        mine = jnp.dot(pick, back_ref[...], preferred_element_type=jnp.float32)
        out_ref[...] = (base_ref[...] + mine).astype(jnp.bfloat16)

    return pl.pallas_call(
        kernel,
        out_shape=jax.ShapeDtypeStruct((rows, cols), jnp.bfloat16),
        compiler_params=GRANT,
        name="full_take",
    )(at_col, back, base)


def scalar_spec():
    return pl.BlockSpec(memory_space=pltpu.SMEM)


def count_before(row, col, also_col=None):
    n = row.shape[1]
    j = lax.broadcasted_iota(jnp.int32, (n, n), 0)
    i = lax.broadcasted_iota(jnp.int32, (n, n), 1)
    hit = (row == col) & (j < i)
    if also_col is not None:
        hit = hit & also_col
    return jnp.sum(jnp.where(hit, 1, 0), axis=0, keepdims=True)


def to_col(row):
    return jnp.broadcast_to(row, (128, row.shape[1])).T[:, :1]


def pick_rows(at_row, slots, first=0):
    n = at_row.shape[1]
    slot = lax.broadcasted_iota(jnp.int32, (slots, n), 0) + first
    return jnp.where(slot == at_row, 1.0, 0.0).astype(jnp.bfloat16)


def place_main(ids_row, tokens, slots):
    rows, width = tokens.shape
    tile = 256

    def kernel(row_ref, tok_ref, out_ref, seen_ref, at_col_ref):
        @pl.when(pl.program_id(0) == 0)
        def _():
            row = row_ref[...]
            seen = count_before(row, to_col(row))
            seen_ref[...] = seen
            spot = row % HERE
            back = row // HERE * (HERE * MOST) + jnp.where(
                seen < MAIN, spot * MAIN + seen, HERE * MAIN + spot
            )
            at_col_ref[...] = to_col(back)

        at_row = jnp.where(seen_ref[...] < MAIN, row_ref[...] * MAIN + seen_ref[...], -1)
        pick = pick_rows(at_row, tile, pl.program_id(0) * tile)
        out_ref[...] = jnp.dot(pick, tok_ref[...], preferred_element_type=jnp.float32).astype(
            jnp.bfloat16
        )

    return pl.pallas_call(
        kernel,
        grid=(slots // tile,),
        in_specs=[
            pl.BlockSpec((1, rows), lambda i: (0, 0)),
            pl.BlockSpec((rows, width), lambda i: (0, 0)),
        ],
        out_specs=[
            pl.BlockSpec((tile, width), lambda i: (i, 0)),
            pl.BlockSpec((1, rows), lambda i: (0, 0)),
            pl.BlockSpec((rows, 1), lambda i: (0, 0)),
        ],
        out_shape=[
            jax.ShapeDtypeStruct((slots, width), tokens.dtype),
            jax.ShapeDtypeStruct((1, rows), jnp.int32),
            jax.ShapeDtypeStruct((rows, 1), jnp.int32),
        ],
        compiler_params=GRANT,
        name="place_main",
    )(ids_row, tokens)


def bucket(rows_of, key, key_col, code, valid, valid_col, flag, out_refs, block_ref, at):
    n = key.shape[1]
    width = rows_of.shape[1]
    q = count_before(key, key_col, valid_col)
    fits = valid & (q < SIDE - 1)
    lost = jnp.max(jnp.where(valid & (q >= SIDE - 1), 1.0, 0.0), axis=1, keepdims=True)
    flag = jnp.maximum(flag, lost)
    pick = pick_rows(jnp.where(fits, key * SIDE + q, -1), 8 * SIDE)
    data = jnp.dot(pick, rows_of, preferred_element_type=jnp.float32)
    which = lax.broadcasted_iota(jnp.int32, (8, n), 0)
    owned = jnp.where(fits & (which == key), (code + 1).astype(jnp.float32), 0.0)
    place = lax.broadcasted_iota(jnp.int32, (128, n), 0)
    there = jnp.where(place == q, 1.0, 0.0)
    codes = lax.dot_general(
        owned.astype(jnp.bfloat16),
        there.astype(jnp.bfloat16),
        (((1,), (1,)), ((), ())),
        preferred_element_type=jnp.float32,
    )
    lane = lax.broadcasted_iota(jnp.int32, (8, 128), 1)
    codes = jnp.where(lane == 127, flag, codes)
    wide = jnp.concatenate([codes, jnp.zeros((8, width - 128), jnp.float32)], axis=1)
    row = lax.broadcasted_iota(jnp.int32, (SIDE, width), 0)
    for k in range(8):
        note = jnp.broadcast_to(wide[k : k + 1], (SIDE, width))
        block_ref[k] = jnp.where(
            row == SIDE - 1, note, data[k * SIDE : (k + 1) * SIDE]
        ).astype(jnp.bfloat16)
    for ref, order in zip(out_refs, (STAY, LEAVE)):
        for i, k in enumerate(order):
            ref[i * SIDE : (i + 1) * SIDE, :] = block_ref[at ^ k]


def arrived_blocks(refs):
    stay, first, second, third = refs
    spots = [(stay, 0), (first, 0), (second, 0), (second, 2)] + [(third, i) for i in range(4)]
    return [ref[i * SIDE : (i + 1) * SIDE, :] for ref, i in spots]


def halving_sends(stay, leave, axis):
    size = lax.axis_size(axis)

    def send(x, step):
        return lax.ppermute(x, axis, [(i, i ^ step) for i in range(size)])

    half = 2 * SIDE
    first = send(leave, 1)
    second = send(jnp.concatenate([stay[half:], first[half:]]), 2)
    last = [x[i * SIDE : (i + 1) * SIDE] for x, i in ((stay, 1), (first, 1), (second, 1), (second, 3))]
    third = send(jnp.concatenate(last), 4)
    return stay, first, second, third


def read_codes(blocks):
    n = 8 * SIDE
    lane = lax.broadcasted_iota(jnp.int32, (8, n), 1)
    codes = jnp.zeros((8, n), jnp.float32)
    flag = jnp.zeros((1, 1), jnp.float32)
    for k in range(8):
        note = blocks[k].astype(jnp.float32)[SIDE - 1 : SIDE, :n]
        flag = jnp.maximum(flag, note[:, 127:128])
        own = jnp.where(lane < SIDE - 1, jnp.broadcast_to(note, (8, n)), 0.0)
        codes = codes + (pltpu.roll(own, k * SIDE, 1) if k else own)
    return codes[:1].astype(jnp.int32) - 1, flag


def side_first(at, seen, ids_row, tokens):
    _, width = tokens.shape

    def kernel(at_ref, seen_ref, row_ref, tok_ref, *refs):
        row = row_ref[...]
        third = seen_ref[...] >= MAIN
        home = row // HERE
        key = home % 8
        marked = jnp.where(third, key, -1)
        bucket(
            tok_ref[...], key, to_col(marked), home // 8 * 8 + row % HERE, third, None,
            jnp.zeros((1, 1), jnp.float32), refs[:2], refs[2], at_ref[0],
        )

    return pl.pallas_call(
        kernel,
        in_specs=[scalar_spec()] + [pl.BlockSpec(memory_space=pltpu.VMEM)] * 3,
        out_shape=[jax.ShapeDtypeStruct((4 * SIDE, width), jnp.bfloat16)] * 2,
        scratch_shapes=[pltpu.VMEM((8, SIDE, width), jnp.bfloat16)],
        compiler_params=GRANT,
        name="side_first",
    )(at, seen, ids_row, tokens)


def side_second(at, blocks):
    width = blocks[0].shape[1]
    n = 8 * SIDE

    def kernel(at_ref, *refs):
        blocks = arrived_blocks(refs[:4])
        code, flag = read_codes(blocks)
        valid = code >= 0
        key = jnp.where(valid, code // 8, -1)
        from_y = (lax.broadcasted_iota(jnp.int32, (1, n), 1) // SIDE) ^ at_ref[1]
        rows_of = jnp.concatenate(blocks, axis=0)
        bucket(
            rows_of, key, to_col(key), from_y * 8 + code % 8, valid, None,
            flag, refs[4:6], refs[6], at_ref[0],
        )

    return pl.pallas_call(
        kernel,
        in_specs=[scalar_spec()] + [pl.BlockSpec(memory_space=pltpu.VMEM)] * 4,
        out_shape=[jax.ShapeDtypeStruct((4 * SIDE, width), jnp.bfloat16)] * 2,
        scratch_shapes=[pltpu.VMEM((8, SIDE, width), jnp.bfloat16)],
        compiler_params=GRANT,
        name="side_second",
    )(at, *blocks)


def fold(full, mine, rank):
    pair = 2 * rank
    lane = lax.broadcasted_iota(jnp.int32, (full.shape[0], pair), 1)
    kept = jnp.zeros((full.shape[0], pair), jnp.float32)
    for k in range(HERE // 2):
        holder = jnp.where(lane < rank, 2 * k, 2 * k + 1)
        kept = kept + jnp.where(mine == holder, full[:, k * pair : (k + 1) * pair], 0.0)
    return kept + pltpu.roll(kept, rank, 1)


def contract_last(x, y):
    return lax.dot_general(x, y, (((1,), (1,)), ((), ())), preferred_element_type=jnp.float32)


def side_low(at, blocks, down):
    here, rank, width = down.shape
    n = 8 * SIDE
    thirds = 64 * here
    pair = 2 * rank

    def kernel(at_ref, *refs):
        down_ref, out_ref, flag_ref = refs[4:]
        blocks = arrived_blocks(refs[:4])
        code, flag = read_codes(blocks)
        from_z = (lax.broadcasted_iota(jnp.int32, (1, n), 1) // SIDE) ^ at_ref[0]
        slot = jnp.where(code >= 0, from_z * 64 + code, -1)
        rows_of = jnp.concatenate(blocks, axis=0)
        full = contract_last(rows_of, down_ref[...].reshape(here * rank, width))
        mine = to_col(jnp.where(code >= 0, code % 8, -1))
        low = fold(full, mine, rank).astype(jnp.bfloat16)
        spread = jnp.dot(pick_rows(slot, thirds), low, preferred_element_type=jnp.float32)
        lane = lax.broadcasted_iota(jnp.int32, (thirds // 2, pair), 1)
        out_ref[...] = jnp.where(
            lane < rank, spread[: thirds // 2], spread[thirds // 2 :]
        ).astype(jnp.bfloat16)
        flag_ref[...] = jnp.broadcast_to(flag, (8, 128))

    return pl.pallas_call(
        kernel,
        in_specs=[scalar_spec()] + [pl.BlockSpec(memory_space=pltpu.VMEM)] * 5,
        out_shape=[
            jax.ShapeDtypeStruct((thirds // 2, pair), jnp.bfloat16),
            jax.ShapeDtypeStruct((8, 128), jnp.float32),
        ],
        compiler_params=GRANT,
        name="side_low",
    )(at, *blocks, down)


def down_main(arrived, thirds, down):
    slots, width = arrived.shape
    here, rank, _ = down.shape
    half = slots // 2
    tile = 256
    pair = 2 * rank

    def kernel(in_ref, thirds_ref, down_ref, out_ref):
        weight = down_ref[...].reshape(here * rank, width)
        lane = lax.broadcasted_iota(jnp.int32, (tile, pair), 1)
        slot = lax.broadcasted_iota(jnp.int32, (tile, pair), 0)
        mine = slot % (HERE * MAIN) // MAIN
        for first in range(0, half, tile):
            lo = fold(contract_last(in_ref[first : first + tile, :], weight), mine, rank)
            hi = fold(
                contract_last(in_ref[half + first : half + first + tile, :], weight), mine, rank
            )
            out_ref[first : first + tile, :] = jnp.where(lane < rank, lo, hi).astype(jnp.bfloat16)
        out_ref[half:, :] = thirds_ref[...]

    return pl.pallas_call(
        kernel,
        out_shape=jax.ShapeDtypeStruct((half + thirds.shape[0], pair), jnp.bfloat16),
        compiler_params=GRANT,
        name="down_main",
    )(arrived, thirds, down)


def up_main(low, flag, up):
    here, rank, cols = up.shape
    owners = 2 * low.shape[0] // (here * MOST)
    half = owners * here * MAIN // 2

    def kernel(low_ref, flag_ref, up_ref, out_ref):
        weight = up_ref[...].reshape(here * rank, cols)

        def mapped(part, per):
            wide = part.astype(jnp.float32)
            turned = pltpu.roll(wide, rank, 1)
            lane = lax.broadcasted_iota(jnp.int32, wide.shape, 1)
            slot = lax.broadcasted_iota(jnp.int32, wide.shape, 0)
            mine = slot % (here * per) // per
            halves = []
            for h in range(2):
                both = jnp.where((lane < rank) == (h == 0), wide, turned)
                spread = []
                for k in range(here // 2):
                    holder = jnp.where(lane < rank, 2 * k, 2 * k + 1)
                    spread.append(jnp.where(mine == holder, both, 0.0).astype(jnp.bfloat16))
                halves.append(
                    jnp.dot(
                        jnp.concatenate(spread, axis=1), weight, preferred_element_type=jnp.float32
                    )
                )
            acc = jnp.concatenate(halves, axis=0) * adapter_output_scale
            return acc.reshape(owners, here * per, cols)

        main = mapped(low_ref[:half, :], MAIN)
        thirds = mapped(low_ref[half:, :], MOST - MAIN)
        both = jnp.concatenate([main, thirds], axis=1).reshape(owners * here * MOST, cols)
        out_ref[...] = jnp.where(flag_ref[:1, :1] > 0.0, LOST, both).astype(jnp.bfloat16)

    return pl.pallas_call(
        kernel,
        out_shape=jax.ShapeDtypeStruct((owners * here * MOST, cols), jnp.bfloat16),
        compiler_params=GRANT,
        name="up_main",
    )(low, flag, up)


def take_main(at_col, back, base):
    rows, cols = base.shape
    slots = back.shape[0]

    def kernel(at_ref, back_ref, base_ref, out_ref, lost_ref):
        slot = lax.broadcasted_iota(jnp.int32, (rows, slots), 1)
        pick = jnp.where(slot == at_ref[...], 1.0, 0.0).astype(jnp.bfloat16)
        mine = jnp.dot(pick, back_ref[...], preferred_element_type=jnp.float32)
        out_ref[...] = (base_ref[...] + mine).astype(jnp.bfloat16)
        lost_ref[0] = (jnp.max(back_ref[...].astype(jnp.float32)) > LOST / 2).astype(jnp.int32)

    return pl.pallas_call(
        kernel,
        out_specs=[pl.BlockSpec(memory_space=pltpu.VMEM), pl.BlockSpec(memory_space=pltpu.SMEM)],
        out_shape=[
            jax.ShapeDtypeStruct((rows, cols), jnp.bfloat16),
            jax.ShapeDtypeStruct((1,), jnp.int32),
        ],
        compiler_params=GRANT,
        name="take_main",
    )(at_col, back, base)


def low_of_all(low_part, groups):
    rows, pair = low_part.shape
    parts = swap(low_part.reshape(groups, rows // groups, pair), TENSOR)
    share = parts.astype(jnp.float32).sum(axis=0).astype(jnp.bfloat16)
    copies = jnp.broadcast_to(share[None], (groups, *share.shape))
    return swap(copies, TENSOR).reshape(rows, pair)


def whole_exchange(tokens, adapter_down, adapter_up_weight, adapter_ids, base):
    rows, width = tokens.shape
    cols = adapter_up_weight.shape[2]
    share = HERE * MOST
    slots = 64 * share
    placed, at_col = full_place(adapter_ids.reshape(1, rows), tokens, slots)
    arrived = swap(placed.reshape(64, share, width), ADAPTER).reshape(slots, width)
    low = low_of_all(full_down(arrived, adapter_down), lax.axis_size(TENSOR))
    delta = full_up(low, adapter_up_weight)
    back = swap(delta.reshape(64, share, cols), ADAPTER).reshape(slots, cols)
    return full_take(at_col, back, base)


def layer(tokens, value_weight, adapter_down, adapter_up_weight, adapter_ids):
    groups = lax.axis_size(TENSOR)
    rows, width = tokens.shape
    cols = adapter_up_weight.shape[2]
    ids_row = adapter_ids.reshape(1, rows)
    at_z = lax.axis_index("z").astype(jnp.int32)
    at_y = lax.axis_index("y").astype(jnp.int32)

    placed, seen, at_col = place_main(ids_row, tokens, 64 * HERE * MAIN)
    arrived = swap(placed.reshape(64, HERE * MAIN, width), ADAPTER)
    arrived = arrived.reshape(64 * HERE * MAIN, width)

    blocks = side_first(at_y.reshape(1), seen, ids_row, tokens)
    blocks = halving_sends(*blocks, "y")
    blocks = side_second(jnp.stack([at_z, at_y]), blocks)
    blocks = halving_sends(*blocks, "z")
    thirds, flag = side_low(at_z.reshape(1), blocks, adapter_down)

    at = lax.axis_index(TENSOR).astype(jnp.int32).reshape(1)
    own, other = value_pieces(tokens, value_weight, at, groups)
    other = lax.ppermute(other, TENSOR[1], [(0, 1), (1, 0)])
    pairs = pair_sum(own, other)
    base = base_sum(own, other, xor_sends(pairs, TENSOR[0]))

    low = low_of_all(down_main(arrived, thirds, adapter_down), groups)
    delta = up_main(low, flag, adapter_up_weight)
    back = swap(delta.reshape(64, HERE * MOST, cols), ADAPTER).reshape(64 * HERE * MOST, cols)
    values, lost = take_main(at_col, back, base)
    return lax.cond(
        lost[0] > 0,
        lambda: whole_exchange(tokens, adapter_down, adapter_up_weight, adapter_ids, base),
        lambda: values,
    )


def xor_sends(pieces, axis):
    size = lax.axis_size(axis)
    parts = []
    for k in range(1, size):
        parts.append(lax.ppermute(pieces[k - 1], axis, [(i, i ^ k) for i in range(size)]))
    return parts


def solution(mesh):
    torus = Mesh(mesh.devices.reshape(8, 8, 4, 2), (*ADAPTER, *TENSOR))
    return jax.shard_map(
        layer,
        mesh=torus,
        in_specs=(
            P(ADAPTER, TENSOR),
            P(TENSOR, None),
            P(ADAPTER, None, TENSOR),
            P(ADAPTER, None, TENSOR),
            P(ADAPTER, None),
        ),
        out_specs=P(ADAPTER, TENSOR),
        check_vma=False,
    )
```

```python
import jax
import jax.numpy as jnp
from jax import lax
from jax.experimental import pallas as pl
from jax.experimental.pallas import tpu as pltpu
from jax.sharding import Mesh
from jax.sharding import PartitionSpec as P


TENSOR = ("tensor_0", "tensor_1")
ADAPTER = ("z", "y")
HERE = 8
MOST = 3
MAIN = 2
SIDE = 16
STAY = (0, 4, 2, 6)
LEAVE = (1, 5, 3, 7)
LOST = 3e38
GRANT = pltpu.CompilerParams(vmem_limit_bytes=16 * 2**20)

adapter_output_scale = 2.0


def swap(x, axes):
    return lax.all_to_all(x, axes, split_axis=0, concat_axis=0, tiled=True)


def full_place(ids_row, tokens, slots):
    rows, width = tokens.shape
    tile = 256

    def kernel(row_ref, tok_ref, out_ref, at_col_ref, at_row_ref):
        @pl.when(pl.program_id(0) == 0)
        def _():
            row = row_ref[...]
            col = jnp.broadcast_to(row, (128, rows)).T[:, :1]
            same = row == col
            i = lax.broadcasted_iota(jnp.int32, (rows, rows), 0)
            j = lax.broadcasted_iota(jnp.int32, (rows, rows), 1)
            before_row = jnp.sum(jnp.where(same & (i < j), 1, 0), axis=0, keepdims=True)
            before_col = jnp.sum(jnp.where(same & (j < i), 1, 0), axis=1, keepdims=True)
            at_row_ref[...] = row * MOST + before_row
            at_col_ref[...] = col * MOST + before_col

        first = pl.program_id(0) * tile
        slot = lax.broadcasted_iota(jnp.int32, (tile, rows), 0) + first
        pick = jnp.where(slot == at_row_ref[...], 1.0, 0.0).astype(jnp.bfloat16)
        out_ref[...] = jnp.dot(pick, tok_ref[...], preferred_element_type=jnp.float32).astype(
            jnp.bfloat16
        )

    return pl.pallas_call(
        kernel,
        grid=(slots // tile,),
        in_specs=[
            pl.BlockSpec((1, rows), lambda i: (0, 0)),
            pl.BlockSpec((rows, width), lambda i: (0, 0)),
        ],
        out_specs=[
            pl.BlockSpec((tile, width), lambda i: (i, 0)),
            pl.BlockSpec((rows, 1), lambda i: (0, 0)),
        ],
        out_shape=[
            jax.ShapeDtypeStruct((slots, width), tokens.dtype),
            jax.ShapeDtypeStruct((rows, 1), jnp.int32),
        ],
        scratch_shapes=[pltpu.VMEM((1, rows), jnp.int32)],
        compiler_params=GRANT,
        name="full_place",
    )(ids_row, tokens)


def value_pieces(tokens, weight, at, pieces):
    rows, width = tokens.shape
    cols = weight.shape[1] // pieces
    step = 2

    def kernel(at_ref, tok_ref, w_ref, own_ref, other_ref, part_ref):
        for first in range(0, pieces, step):
            part = jnp.dot(
                tok_ref[...],
                w_ref[:, first * cols : (first + step) * cols],
                preferred_element_type=jnp.float32,
            ).astype(jnp.bfloat16)
            for k in range(step):
                part_ref[first + k] = part[:, k * cols : (k + 1) * cols]
        for k in range(pieces // 2):
            own_ref[k] = part_ref[at_ref[0] ^ (2 * k)]
            other_ref[k] = part_ref[at_ref[0] ^ (2 * k + 1)]

    return pl.pallas_call(
        kernel,
        in_specs=[
            pl.BlockSpec(memory_space=pltpu.SMEM),
            pl.BlockSpec((rows, width), lambda: (0, 0)),
            pl.BlockSpec(weight.shape, lambda: (0, 0)),
        ],
        out_shape=[jax.ShapeDtypeStruct((pieces // 2, rows, cols), jnp.bfloat16)] * 2,
        scratch_shapes=[pltpu.VMEM((pieces, rows, cols), jnp.bfloat16)],
        compiler_params=GRANT,
        name="value_pieces",
    )(at, tokens, weight)


def pair_sum(own, other):
    count, rows, cols = own.shape

    def kernel(own_ref, other_ref, *out_refs):
        for k in range(1, count):
            total = own_ref[k].astype(jnp.float32) + other_ref[k].astype(jnp.float32)
            out_refs[k - 1][...] = total.astype(jnp.bfloat16)

    return pl.pallas_call(
        kernel,
        out_shape=[jax.ShapeDtypeStruct((rows, cols), jnp.bfloat16)] * (count - 1),
        compiler_params=GRANT,
        name="pair_sum",
    )(own, other)


def base_sum(own, other, parts):
    def kernel(own_ref, other_ref, *refs):
        total = own_ref[0].astype(jnp.float32) + other_ref[0].astype(jnp.float32)
        for ref in refs[:-1]:
            total = total + ref[...].astype(jnp.float32)
        refs[-1][...] = total

    return pl.pallas_call(
        kernel,
        out_shape=jax.ShapeDtypeStruct(parts[0].shape, jnp.float32),
        compiler_params=GRANT,
        name="base_sum",
    )(own, other, *parts)


def adapter_of(shape, first, group):
    slot = lax.broadcasted_iota(jnp.int32, shape, 0) + first
    return slot % group // MOST


def full_down(arrived, down):
    slots, width = arrived.shape
    here, rank, _ = down.shape
    group = here * MOST
    half = slots // 2
    tile = 192
    pair = 2 * rank

    def kernel(lo_ref, hi_ref, down_ref, out_ref):
        weight = down_ref[...].reshape(here * rank, width)
        lane = lax.broadcasted_iota(jnp.int32, (tile, pair), 1)

        def rows_of(ref):
            full = lax.dot_general(
                ref[...], weight, (((1,), (1,)), ((), ())), preferred_element_type=jnp.float32
            )
            mine = adapter_of((tile, pair), 0, group)
            kept = jnp.zeros((tile, pair), jnp.float32)
            for k in range(here // 2):
                holder = jnp.where(lane < rank, 2 * k, 2 * k + 1)
                kept = kept + jnp.where(mine == holder, full[:, k * pair : (k + 1) * pair], 0.0)
            return kept + pltpu.roll(kept, rank, 1)

        out_ref[...] = jnp.where(lane < rank, rows_of(lo_ref), rows_of(hi_ref)).astype(
            jnp.bfloat16
        )

    steps = half // tile
    return pl.pallas_call(
        kernel,
        grid=(steps,),
        in_specs=[
            pl.BlockSpec((tile, width), lambda i: (i, 0)),
            pl.BlockSpec((tile, width), lambda i: (i + steps, 0)),
            pl.BlockSpec((here, rank, width), lambda i: (0, 0, 0)),
        ],
        out_specs=pl.BlockSpec((tile, pair), lambda i: (i, 0)),
        out_shape=jax.ShapeDtypeStruct((half, pair), jnp.bfloat16),
        compiler_params=GRANT,
        name="full_down",
    )(arrived, arrived, down)


def full_up(low, up):
    half, pair = low.shape
    here, rank, cols = up.shape
    group = here * MOST

    def kernel(low_ref, up_ref, out_ref):
        weight = up_ref[...].reshape(here * rank, cols)
        low_wide = low_ref[...].astype(jnp.float32)
        turned = pltpu.roll(low_wide, rank, 1)
        lane = lax.broadcasted_iota(jnp.int32, (half, pair), 1)
        mine = adapter_of((half, pair), 0, group)
        for h in range(2):
            own = (lane < rank) == (h == 0)
            both = jnp.where(own, low_wide, turned)
            spread = []
            for k in range(here // 2):
                holder = jnp.where(lane < rank, 2 * k, 2 * k + 1)
                spread.append(jnp.where(mine == holder, both, 0.0).astype(jnp.bfloat16))
            acc = jnp.dot(
                jnp.concatenate(spread, axis=1), weight, preferred_element_type=jnp.float32
            )
            out_ref[h * half : (h + 1) * half, :] = (adapter_output_scale * acc).astype(
                jnp.bfloat16
            )

    return pl.pallas_call(
        kernel,
        out_shape=jax.ShapeDtypeStruct((2 * half, cols), jnp.bfloat16),
        compiler_params=GRANT,
        name="full_up",
    )(low, up)


def full_take(at_col, back, base):
    rows, cols = base.shape
    slots = back.shape[0]

    def kernel(at_ref, back_ref, base_ref, out_ref):
        slot = lax.broadcasted_iota(jnp.int32, (rows, slots), 1)
        pick = jnp.where(slot == at_ref[...], 1.0, 0.0).astype(jnp.bfloat16)
        mine = jnp.dot(pick, back_ref[...], preferred_element_type=jnp.float32)
        out_ref[...] = (base_ref[...] + mine).astype(jnp.bfloat16)

    return pl.pallas_call(
        kernel,
        out_shape=jax.ShapeDtypeStruct((rows, cols), jnp.bfloat16),
        compiler_params=GRANT,
        name="full_take",
    )(at_col, back, base)


def scalar_spec():
    return pl.BlockSpec(memory_space=pltpu.SMEM)


def count_before(row, col):
    n = row.shape[1]
    j = lax.broadcasted_iota(jnp.int32, (n, n), 0)
    i = lax.broadcasted_iota(jnp.int32, (n, n), 1)
    return jnp.sum(jnp.where((row == col) & (j < i), 1, 0), axis=0, keepdims=True)


def to_col(row):
    return jnp.broadcast_to(row, (128, row.shape[1])).T[:, :1]


def pick_rows(at_row, slots, first=0):
    n = at_row.shape[1]
    slot = lax.broadcasted_iota(jnp.int32, (slots, n), 0) + first
    return jnp.where(slot == at_row, 1.0, 0.0).astype(jnp.bfloat16)


def place_main(ids_row, seen, tokens, slots):
    rows, width = tokens.shape
    tile = 256

    def kernel(row_ref, seen_ref, tok_ref, out_ref):
        at_row = jnp.where(seen_ref[...] < MAIN, row_ref[...] * MAIN + seen_ref[...], -1)
        pick = pick_rows(at_row, tile, pl.program_id(0) * tile)
        out_ref[...] = jnp.dot(pick, tok_ref[...], preferred_element_type=jnp.float32).astype(
            jnp.bfloat16
        )

    return pl.pallas_call(
        kernel,
        grid=(slots // tile,),
        in_specs=[
            pl.BlockSpec((1, rows), lambda i: (0, 0)),
            pl.BlockSpec((1, rows), lambda i: (0, 0)),
            pl.BlockSpec((rows, width), lambda i: (0, 0)),
        ],
        out_specs=pl.BlockSpec((tile, width), lambda i: (i, 0)),
        out_shape=jax.ShapeDtypeStruct((slots, width), tokens.dtype),
        compiler_params=GRANT,
        name="place_main",
    )(ids_row, seen, tokens)


def bucket(rows_of, key, key_col, code, valid, flag, store):
    n = key.shape[1]
    width = rows_of.shape[1]
    q = count_before(key, key_col)
    fits = valid & (q < SIDE - 1)
    lost = jnp.max(jnp.where(valid & (q >= SIDE - 1), 1.0, 0.0), axis=1, keepdims=True)
    flag = jnp.maximum(flag, lost)
    pick = pick_rows(jnp.where(fits, key * SIDE + q, -1), 8 * SIDE)
    data = jnp.dot(pick, rows_of, preferred_element_type=jnp.float32)
    which = lax.broadcasted_iota(jnp.int32, (8, n), 0)
    owned = jnp.where(fits & (which == key), (code + 1).astype(jnp.float32), 0.0)
    place = lax.broadcasted_iota(jnp.int32, (128, n), 0)
    there = jnp.where(place == q, 1.0, 0.0)
    codes = lax.dot_general(
        owned.astype(jnp.bfloat16),
        there.astype(jnp.bfloat16),
        (((1,), (1,)), ((), ())),
        preferred_element_type=jnp.float32,
    )
    lane = lax.broadcasted_iota(jnp.int32, (8, 128), 1)
    codes = jnp.where(lane == 127, flag, codes)
    wide = jnp.concatenate([codes, jnp.zeros((8, width - 128), jnp.float32)], axis=1)
    row = lax.broadcasted_iota(jnp.int32, (SIDE, width), 0)
    for k in range(8):
        note = jnp.broadcast_to(wide[k : k + 1], (SIDE, width))
        block = jnp.where(row == SIDE - 1, note, data[k * SIDE : (k + 1) * SIDE])
        store(k, block.astype(jnp.bfloat16))


def arrived_blocks(refs):
    stay, first, second, third = refs
    spots = [(stay, 0), (first, 0), (second, 0), (second, 2)] + [(third, i) for i in range(4)]
    return [ref[i * SIDE : (i + 1) * SIDE, :] for ref, i in spots]


def halving_sends(stay, leave, axis):
    size = lax.axis_size(axis)

    def send(x, step):
        return lax.ppermute(x, axis, [(i, i ^ step) for i in range(size)])

    half = 2 * SIDE
    first = send(leave, 1)
    second = send(jnp.concatenate([stay[half:], first[half:]]), 2)
    last = [x[i * SIDE : (i + 1) * SIDE] for x, i in ((stay, 1), (first, 1), (second, 1), (second, 3))]
    third = send(jnp.concatenate(last), 4)
    return stay, first, second, third


def read_codes(blocks):
    n = 8 * SIDE
    lane = lax.broadcasted_iota(jnp.int32, (8, n), 1)
    codes = jnp.zeros((8, n), jnp.float32)
    flag = jnp.zeros((1, 1), jnp.float32)
    for k in range(8):
        note = blocks[k].astype(jnp.float32)[SIDE - 1 : SIDE, :n]
        flag = jnp.maximum(flag, note[:, 127:128])
        own = jnp.where(lane < SIDE - 1, jnp.broadcast_to(note, (8, n)), 0.0)
        codes = codes + (pltpu.roll(own, k * SIDE, 1) if k else own)
    return codes[:1].astype(jnp.int32) - 1, flag


def side_first(ids_row, tokens):
    rows, width = tokens.shape

    def kernel(row_ref, tok_ref, out_ref, seen_ref, at_col_ref):
        row = row_ref[...]
        seen = count_before(row, to_col(row))
        seen_ref[...] = seen
        home = row // HERE
        spot = row % HERE
        back = home * (HERE * MOST) + jnp.where(
            seen < MAIN, spot * MAIN + seen, HERE * MAIN + spot
        )
        at_col_ref[...] = to_col(back)
        third = seen >= MAIN
        key = home % 8

        def store(k, block):
            out_ref[k * SIDE : (k + 1) * SIDE, :] = block

        bucket(
            tok_ref[...], key, to_col(jnp.where(third, key, -1)), home // 8 * 8 + spot, third,
            jnp.zeros((1, 1), jnp.float32), store,
        )

    return pl.pallas_call(
        kernel,
        out_shape=[
            jax.ShapeDtypeStruct((8 * SIDE, width), jnp.bfloat16),
            jax.ShapeDtypeStruct((1, rows), jnp.int32),
            jax.ShapeDtypeStruct((rows, 1), jnp.int32),
        ],
        compiler_params=GRANT,
        name="side_first",
    )(ids_row, tokens)


def side_second(at, arrived):
    n, width = arrived.shape

    def kernel(at_ref, in_ref, stay_ref, leave_ref, block_ref):
        blocks = [in_ref[k * SIDE : (k + 1) * SIDE, :] for k in range(8)]
        code, flag = read_codes(blocks)
        valid = code >= 0
        key = jnp.where(valid, code // 8, -1)
        from_y = lax.broadcasted_iota(jnp.int32, (1, n), 1) // SIDE

        def store(k, block):
            block_ref[k] = block

        bucket(in_ref[...], key, to_col(key), from_y * 8 + code % 8, valid, flag, store)
        for ref, order in ((stay_ref, STAY), (leave_ref, LEAVE)):
            for i, k in enumerate(order):
                ref[i * SIDE : (i + 1) * SIDE, :] = block_ref[at_ref[0] ^ k]

    return pl.pallas_call(
        kernel,
        in_specs=[scalar_spec(), pl.BlockSpec(memory_space=pltpu.VMEM)],
        out_shape=[jax.ShapeDtypeStruct((4 * SIDE, width), jnp.bfloat16)] * 2,
        scratch_shapes=[pltpu.VMEM((8, SIDE, width), jnp.bfloat16)],
        compiler_params=GRANT,
        name="side_second",
    )(at, arrived)


def fold(full, mine, rank):
    pair = 2 * rank
    lane = lax.broadcasted_iota(jnp.int32, (full.shape[0], pair), 1)
    kept = jnp.zeros((full.shape[0], pair), jnp.float32)
    for k in range(HERE // 2):
        holder = jnp.where(lane < rank, 2 * k, 2 * k + 1)
        kept = kept + jnp.where(mine == holder, full[:, k * pair : (k + 1) * pair], 0.0)
    return kept + pltpu.roll(kept, rank, 1)


def contract_last(x, y):
    return lax.dot_general(x, y, (((1,), (1,)), ((), ())), preferred_element_type=jnp.float32)


def side_low(at, blocks, down):
    here, rank, width = down.shape
    n = 8 * SIDE
    thirds = 64 * here
    pair = 2 * rank

    def kernel(at_ref, *refs):
        down_ref, out_ref, flag_ref = refs[4:]
        blocks = arrived_blocks(refs[:4])
        code, flag = read_codes(blocks)
        from_z = (lax.broadcasted_iota(jnp.int32, (1, n), 1) // SIDE) ^ at_ref[0]
        slot = jnp.where(code >= 0, from_z * 64 + code, -1)
        rows_of = jnp.concatenate(blocks, axis=0)
        full = contract_last(rows_of, down_ref[...].reshape(here * rank, width))
        mine = to_col(jnp.where(code >= 0, code % 8, -1))
        low = fold(full, mine, rank).astype(jnp.bfloat16)
        spread = jnp.dot(pick_rows(slot, thirds), low, preferred_element_type=jnp.float32)
        lane = lax.broadcasted_iota(jnp.int32, (thirds // 2, pair), 1)
        out_ref[...] = jnp.where(
            lane < rank, spread[: thirds // 2], spread[thirds // 2 :]
        ).astype(jnp.bfloat16)
        flag_ref[...] = jnp.broadcast_to(flag, (8, 128))

    return pl.pallas_call(
        kernel,
        in_specs=[scalar_spec()] + [pl.BlockSpec(memory_space=pltpu.VMEM)] * 5,
        out_shape=[
            jax.ShapeDtypeStruct((thirds // 2, pair), jnp.bfloat16),
            jax.ShapeDtypeStruct((8, 128), jnp.float32),
        ],
        compiler_params=GRANT,
        name="side_low",
    )(at, *blocks, down)


def down_main(arrived, thirds, down):
    slots, width = arrived.shape
    here, rank, _ = down.shape
    half = slots // 2
    tile = 256
    pair = 2 * rank

    def kernel(in_ref, thirds_ref, down_ref, out_ref):
        weight = down_ref[...].reshape(here * rank, width)
        lane = lax.broadcasted_iota(jnp.int32, (tile, pair), 1)
        slot = lax.broadcasted_iota(jnp.int32, (tile, pair), 0)
        mine = slot % (HERE * MAIN) // MAIN
        for first in range(0, half, tile):
            lo = fold(contract_last(in_ref[first : first + tile, :], weight), mine, rank)
            hi = fold(
                contract_last(in_ref[half + first : half + first + tile, :], weight), mine, rank
            )
            out_ref[first : first + tile, :] = jnp.where(lane < rank, lo, hi).astype(jnp.bfloat16)
        out_ref[half:, :] = thirds_ref[...]

    return pl.pallas_call(
        kernel,
        out_shape=jax.ShapeDtypeStruct((half + thirds.shape[0], pair), jnp.bfloat16),
        compiler_params=GRANT,
        name="down_main",
    )(arrived, thirds, down)


def up_main(low, flag, up):
    here, rank, cols = up.shape
    owners = 2 * low.shape[0] // (here * MOST)
    half = owners * here * MAIN // 2

    def kernel(low_ref, flag_ref, up_ref, out_ref):
        weight = up_ref[...].reshape(here * rank, cols)

        def mapped(part, per):
            wide = part.astype(jnp.float32)
            turned = pltpu.roll(wide, rank, 1)
            lane = lax.broadcasted_iota(jnp.int32, wide.shape, 1)
            slot = lax.broadcasted_iota(jnp.int32, wide.shape, 0)
            mine = slot % (here * per) // per
            halves = []
            for h in range(2):
                both = jnp.where((lane < rank) == (h == 0), wide, turned)
                spread = []
                for k in range(here // 2):
                    holder = jnp.where(lane < rank, 2 * k, 2 * k + 1)
                    spread.append(jnp.where(mine == holder, both, 0.0).astype(jnp.bfloat16))
                halves.append(
                    jnp.dot(
                        jnp.concatenate(spread, axis=1), weight, preferred_element_type=jnp.float32
                    )
                )
            acc = jnp.concatenate(halves, axis=0) * adapter_output_scale
            return acc.reshape(owners, here * per, cols)

        main = mapped(low_ref[:half, :], MAIN)
        thirds = mapped(low_ref[half:, :], MOST - MAIN)
        both = jnp.concatenate([main, thirds], axis=1).reshape(owners * here * MOST, cols)
        out_ref[...] = jnp.where(flag_ref[:1, :1] > 0.0, LOST, both).astype(jnp.bfloat16)

    return pl.pallas_call(
        kernel,
        out_shape=jax.ShapeDtypeStruct((owners * here * MOST, cols), jnp.bfloat16),
        compiler_params=GRANT,
        name="up_main",
    )(low, flag, up)


def take_main(at_col, back, base):
    rows, cols = base.shape
    slots = back.shape[0]

    def kernel(at_ref, back_ref, base_ref, out_ref, lost_ref):
        slot = lax.broadcasted_iota(jnp.int32, (rows, slots), 1)
        pick = jnp.where(slot == at_ref[...], 1.0, 0.0).astype(jnp.bfloat16)
        mine = jnp.dot(pick, back_ref[...], preferred_element_type=jnp.float32)
        out_ref[...] = (base_ref[...] + mine).astype(jnp.bfloat16)
        lost_ref[0] = (jnp.max(back_ref[...].astype(jnp.float32)) > LOST / 2).astype(jnp.int32)

    return pl.pallas_call(
        kernel,
        out_specs=[pl.BlockSpec(memory_space=pltpu.VMEM), pl.BlockSpec(memory_space=pltpu.SMEM)],
        out_shape=[
            jax.ShapeDtypeStruct((rows, cols), jnp.bfloat16),
            jax.ShapeDtypeStruct((1,), jnp.int32),
        ],
        compiler_params=GRANT,
        name="take_main",
    )(at_col, back, base)


def low_of_all(low_part, groups):
    rows, pair = low_part.shape
    parts = swap(low_part.reshape(groups, rows // groups, pair), TENSOR)
    share = parts.astype(jnp.float32).sum(axis=0).astype(jnp.bfloat16)
    copies = jnp.broadcast_to(share[None], (groups, *share.shape))
    return swap(copies, TENSOR).reshape(rows, pair)


def whole_exchange(tokens, adapter_down, adapter_up_weight, adapter_ids, base):
    rows, width = tokens.shape
    cols = adapter_up_weight.shape[2]
    share = HERE * MOST
    slots = 64 * share
    placed, at_col = full_place(adapter_ids.reshape(1, rows), tokens, slots)
    arrived = swap(placed.reshape(64, share, width), ADAPTER).reshape(slots, width)
    low = low_of_all(full_down(arrived, adapter_down), lax.axis_size(TENSOR))
    delta = full_up(low, adapter_up_weight)
    back = swap(delta.reshape(64, share, cols), ADAPTER).reshape(slots, cols)
    return full_take(at_col, back, base)


def layer(tokens, value_weight, adapter_down, adapter_up_weight, adapter_ids):
    groups = lax.axis_size(TENSOR)
    rows, width = tokens.shape
    cols = adapter_up_weight.shape[2]
    ids_row = adapter_ids.reshape(1, rows)
    at_z = lax.axis_index("z").astype(jnp.int32)

    blocks, seen, at_col = side_first(ids_row, tokens)
    blocks = swap(blocks.reshape(8, SIDE, width), "y").reshape(8 * SIDE, width)
    placed = place_main(ids_row, seen, tokens, 64 * HERE * MAIN)
    arrived = swap(placed.reshape(64, HERE * MAIN, width), ADAPTER)
    arrived = arrived.reshape(64 * HERE * MAIN, width)

    blocks = side_second(at_z.reshape(1), blocks)
    blocks = halving_sends(*blocks, "z")
    thirds, flag = side_low(at_z.reshape(1), blocks, adapter_down)

    at = lax.axis_index(TENSOR).astype(jnp.int32).reshape(1)
    own, other = value_pieces(tokens, value_weight, at, groups)
    other = lax.ppermute(other, TENSOR[1], [(0, 1), (1, 0)])
    pairs = pair_sum(own, other)
    base = base_sum(own, other, xor_sends(pairs, TENSOR[0]))

    low = low_of_all(down_main(arrived, thirds, adapter_down), groups)
    delta = up_main(low, flag, adapter_up_weight)
    back = swap(delta.reshape(64, HERE * MOST, cols), ADAPTER).reshape(64 * HERE * MOST, cols)
    values, lost = take_main(at_col, back, base)
    return lax.cond(
        lost[0] > 0,
        lambda: whole_exchange(tokens, adapter_down, adapter_up_weight, adapter_ids, base),
        lambda: values,
    )


def xor_sends(pieces, axis):
    size = lax.axis_size(axis)
    parts = []
    for k in range(1, size):
        parts.append(lax.ppermute(pieces[k - 1], axis, [(i, i ^ k) for i in range(size)]))
    return parts


def solution(mesh):
    torus = Mesh(mesh.devices.reshape(8, 8, 4, 2), (*ADAPTER, *TENSOR))
    return jax.shard_map(
        layer,
        mesh=torus,
        in_specs=(
            P(ADAPTER, TENSOR),
            P(TENSOR, None),
            P(ADAPTER, None, TENSOR),
            P(ADAPTER, None, TENSOR),
            P(ADAPTER, None),
        ),
        out_specs=P(ADAPTER, TENSOR),
        check_vma=False,
    )
```

```python
import jax
import jax.numpy as jnp
from jax import lax
from jax.experimental import pallas as pl
from jax.experimental.pallas import tpu as pltpu
from jax.sharding import Mesh
from jax.sharding import PartitionSpec as P


TENSOR = ("tensor_0", "tensor_1")
ADAPTER = ("z", "y")
HERE = 8
MOST = 3
MAIN = 2
SIDE = 16
LOST = 3e38
GRANT = pltpu.CompilerParams(vmem_limit_bytes=16 * 2**20)

adapter_output_scale = 2.0


def swap(x, axes):
    return lax.all_to_all(x, axes, split_axis=0, concat_axis=0, tiled=True)


def full_place(ids_row, tokens, slots):
    rows, width = tokens.shape
    tile = 256

    def kernel(row_ref, tok_ref, out_ref, at_col_ref, at_row_ref):
        @pl.when(pl.program_id(0) == 0)
        def _():
            row = row_ref[...]
            col = jnp.broadcast_to(row, (128, rows)).T[:, :1]
            same = row == col
            i = lax.broadcasted_iota(jnp.int32, (rows, rows), 0)
            j = lax.broadcasted_iota(jnp.int32, (rows, rows), 1)
            before_row = jnp.sum(jnp.where(same & (i < j), 1, 0), axis=0, keepdims=True)
            before_col = jnp.sum(jnp.where(same & (j < i), 1, 0), axis=1, keepdims=True)
            at_row_ref[...] = row * MOST + before_row
            at_col_ref[...] = col * MOST + before_col

        first = pl.program_id(0) * tile
        slot = lax.broadcasted_iota(jnp.int32, (tile, rows), 0) + first
        pick = jnp.where(slot == at_row_ref[...], 1.0, 0.0).astype(jnp.bfloat16)
        out_ref[...] = jnp.dot(pick, tok_ref[...], preferred_element_type=jnp.float32).astype(
            jnp.bfloat16
        )

    return pl.pallas_call(
        kernel,
        grid=(slots // tile,),
        in_specs=[
            pl.BlockSpec((1, rows), lambda i: (0, 0)),
            pl.BlockSpec((rows, width), lambda i: (0, 0)),
        ],
        out_specs=[
            pl.BlockSpec((tile, width), lambda i: (i, 0)),
            pl.BlockSpec((rows, 1), lambda i: (0, 0)),
        ],
        out_shape=[
            jax.ShapeDtypeStruct((slots, width), tokens.dtype),
            jax.ShapeDtypeStruct((rows, 1), jnp.int32),
        ],
        scratch_shapes=[pltpu.VMEM((1, rows), jnp.int32)],
        compiler_params=GRANT,
        name="full_place",
    )(ids_row, tokens)


def value_pieces(tokens, weight, at, pieces):
    rows, width = tokens.shape
    cols = weight.shape[1] // pieces
    step = 2

    def kernel(at_ref, tok_ref, w_ref, own_ref, other_ref, part_ref):
        for first in range(0, pieces, step):
            part = jnp.dot(
                tok_ref[...],
                w_ref[:, first * cols : (first + step) * cols],
                preferred_element_type=jnp.float32,
            ).astype(jnp.bfloat16)
            for k in range(step):
                part_ref[first + k] = part[:, k * cols : (k + 1) * cols]
        for k in range(pieces // 2):
            own_ref[k] = part_ref[at_ref[0] ^ (2 * k)]
            other_ref[k] = part_ref[at_ref[0] ^ (2 * k + 1)]

    return pl.pallas_call(
        kernel,
        in_specs=[
            pl.BlockSpec(memory_space=pltpu.SMEM),
            pl.BlockSpec((rows, width), lambda: (0, 0)),
            pl.BlockSpec(weight.shape, lambda: (0, 0)),
        ],
        out_shape=[jax.ShapeDtypeStruct((pieces // 2, rows, cols), jnp.bfloat16)] * 2,
        scratch_shapes=[pltpu.VMEM((pieces, rows, cols), jnp.bfloat16)],
        compiler_params=GRANT,
        name="value_pieces",
    )(at, tokens, weight)


def pair_sum(own, other):
    count, rows, cols = own.shape

    def kernel(own_ref, other_ref, *out_refs):
        for k in range(1, count):
            total = own_ref[k].astype(jnp.float32) + other_ref[k].astype(jnp.float32)
            out_refs[k - 1][...] = total.astype(jnp.bfloat16)

    return pl.pallas_call(
        kernel,
        out_shape=[jax.ShapeDtypeStruct((rows, cols), jnp.bfloat16)] * (count - 1),
        compiler_params=GRANT,
        name="pair_sum",
    )(own, other)


def base_sum(own, other, parts):
    def kernel(own_ref, other_ref, *refs):
        total = own_ref[0].astype(jnp.float32) + other_ref[0].astype(jnp.float32)
        for ref in refs[:-1]:
            total = total + ref[...].astype(jnp.float32)
        refs[-1][...] = total

    return pl.pallas_call(
        kernel,
        out_shape=jax.ShapeDtypeStruct(parts[0].shape, jnp.float32),
        compiler_params=GRANT,
        name="base_sum",
    )(own, other, *parts)


def adapter_of(shape, first, group):
    slot = lax.broadcasted_iota(jnp.int32, shape, 0) + first
    return slot % group // MOST


def full_down(arrived, down):
    slots, width = arrived.shape
    here, rank, _ = down.shape
    group = here * MOST
    half = slots // 2
    tile = 192
    pair = 2 * rank

    def kernel(lo_ref, hi_ref, down_ref, out_ref):
        weight = down_ref[...].reshape(here * rank, width)
        lane = lax.broadcasted_iota(jnp.int32, (tile, pair), 1)

        def rows_of(ref):
            full = lax.dot_general(
                ref[...], weight, (((1,), (1,)), ((), ())), preferred_element_type=jnp.float32
            )
            mine = adapter_of((tile, pair), 0, group)
            kept = jnp.zeros((tile, pair), jnp.float32)
            for k in range(here // 2):
                holder = jnp.where(lane < rank, 2 * k, 2 * k + 1)
                kept = kept + jnp.where(mine == holder, full[:, k * pair : (k + 1) * pair], 0.0)
            return kept + pltpu.roll(kept, rank, 1)

        out_ref[...] = jnp.where(lane < rank, rows_of(lo_ref), rows_of(hi_ref)).astype(
            jnp.bfloat16
        )

    steps = half // tile
    return pl.pallas_call(
        kernel,
        grid=(steps,),
        in_specs=[
            pl.BlockSpec((tile, width), lambda i: (i, 0)),
            pl.BlockSpec((tile, width), lambda i: (i + steps, 0)),
            pl.BlockSpec((here, rank, width), lambda i: (0, 0, 0)),
        ],
        out_specs=pl.BlockSpec((tile, pair), lambda i: (i, 0)),
        out_shape=jax.ShapeDtypeStruct((half, pair), jnp.bfloat16),
        compiler_params=GRANT,
        name="full_down",
    )(arrived, arrived, down)


def full_up(low, up):
    half, pair = low.shape
    here, rank, cols = up.shape
    group = here * MOST

    def kernel(low_ref, up_ref, out_ref):
        weight = up_ref[...].reshape(here * rank, cols)
        low_wide = low_ref[...].astype(jnp.float32)
        turned = pltpu.roll(low_wide, rank, 1)
        lane = lax.broadcasted_iota(jnp.int32, (half, pair), 1)
        mine = adapter_of((half, pair), 0, group)
        for h in range(2):
            own = (lane < rank) == (h == 0)
            both = jnp.where(own, low_wide, turned)
            spread = []
            for k in range(here // 2):
                holder = jnp.where(lane < rank, 2 * k, 2 * k + 1)
                spread.append(jnp.where(mine == holder, both, 0.0).astype(jnp.bfloat16))
            acc = jnp.dot(
                jnp.concatenate(spread, axis=1), weight, preferred_element_type=jnp.float32
            )
            out_ref[h * half : (h + 1) * half, :] = (adapter_output_scale * acc).astype(
                jnp.bfloat16
            )

    return pl.pallas_call(
        kernel,
        out_shape=jax.ShapeDtypeStruct((2 * half, cols), jnp.bfloat16),
        compiler_params=GRANT,
        name="full_up",
    )(low, up)


def full_take(at_col, back, base):
    rows, cols = base.shape
    slots = back.shape[0]

    def kernel(at_ref, back_ref, base_ref, out_ref):
        slot = lax.broadcasted_iota(jnp.int32, (rows, slots), 1)
        pick = jnp.where(slot == at_ref[...], 1.0, 0.0).astype(jnp.bfloat16)
        mine = jnp.dot(pick, back_ref[...], preferred_element_type=jnp.float32)
        out_ref[...] = (base_ref[...] + mine).astype(jnp.bfloat16)

    return pl.pallas_call(
        kernel,
        out_shape=jax.ShapeDtypeStruct((rows, cols), jnp.bfloat16),
        compiler_params=GRANT,
        name="full_take",
    )(at_col, back, base)


def scalar_spec():
    return pl.BlockSpec(memory_space=pltpu.SMEM)


def count_before(row, col):
    n = row.shape[1]
    j = lax.broadcasted_iota(jnp.int32, (n, n), 0)
    i = lax.broadcasted_iota(jnp.int32, (n, n), 1)
    return jnp.sum(jnp.where((row == col) & (j < i), 1, 0), axis=0, keepdims=True)


def to_col(row):
    return jnp.broadcast_to(row, (128, row.shape[1])).T[:, :1]


def pick_rows(at_row, slots, first=0):
    n = at_row.shape[1]
    slot = lax.broadcasted_iota(jnp.int32, (slots, n), 0) + first
    return jnp.where(slot == at_row, 1.0, 0.0).astype(jnp.bfloat16)


def place_main(ids_row, seen, tokens, slots):
    rows, width = tokens.shape
    tile = 256

    def kernel(row_ref, seen_ref, tok_ref, out_ref):
        at_row = jnp.where(seen_ref[...] < MAIN, row_ref[...] * MAIN + seen_ref[...], -1)
        pick = pick_rows(at_row, tile, pl.program_id(0) * tile)
        out_ref[...] = jnp.dot(pick, tok_ref[...], preferred_element_type=jnp.float32).astype(
            jnp.bfloat16
        )

    return pl.pallas_call(
        kernel,
        grid=(slots // tile,),
        in_specs=[
            pl.BlockSpec((1, rows), lambda i: (0, 0)),
            pl.BlockSpec((1, rows), lambda i: (0, 0)),
            pl.BlockSpec((rows, width), lambda i: (0, 0)),
        ],
        out_specs=pl.BlockSpec((tile, width), lambda i: (i, 0)),
        out_shape=jax.ShapeDtypeStruct((slots, width), tokens.dtype),
        compiler_params=GRANT,
        name="place_main",
    )(ids_row, seen, tokens)


def bucket(rows_of, key, key_col, code, valid, flag, store):
    n = key.shape[1]
    width = rows_of.shape[1]
    q = count_before(key, key_col)
    fits = valid & (q < SIDE - 1)
    lost = jnp.max(jnp.where(valid & (q >= SIDE - 1), 1.0, 0.0), axis=1, keepdims=True)
    flag = jnp.maximum(flag, lost)
    pick = pick_rows(jnp.where(fits, key * SIDE + q, -1), 8 * SIDE)
    data = jnp.dot(pick, rows_of, preferred_element_type=jnp.float32)
    which = lax.broadcasted_iota(jnp.int32, (8, n), 0)
    owned = jnp.where(fits & (which == key), (code + 1).astype(jnp.float32), 0.0)
    place = lax.broadcasted_iota(jnp.int32, (128, n), 0)
    there = jnp.where(place == q, 1.0, 0.0)
    codes = lax.dot_general(
        owned.astype(jnp.bfloat16),
        there.astype(jnp.bfloat16),
        (((1,), (1,)), ((), ())),
        preferred_element_type=jnp.float32,
    )
    lane = lax.broadcasted_iota(jnp.int32, (8, 128), 1)
    codes = jnp.where(lane == 127, flag, codes)
    wide = jnp.concatenate([codes, jnp.zeros((8, width - 128), jnp.float32)], axis=1)
    row = lax.broadcasted_iota(jnp.int32, (SIDE, width), 0)
    for k in range(8):
        note = jnp.broadcast_to(wide[k : k + 1], (SIDE, width))
        block = jnp.where(row == SIDE - 1, note, data[k * SIDE : (k + 1) * SIDE])
        store(k, block.astype(jnp.bfloat16))


def read_codes(blocks):
    n = 8 * SIDE
    lane = lax.broadcasted_iota(jnp.int32, (8, n), 1)
    codes = jnp.zeros((8, n), jnp.float32)
    flag = jnp.zeros((1, 1), jnp.float32)
    for k in range(8):
        note = blocks[k].astype(jnp.float32)[SIDE - 1 : SIDE, :n]
        flag = jnp.maximum(flag, note[:, 127:128])
        own = jnp.where(lane < SIDE - 1, jnp.broadcast_to(note, (8, n)), 0.0)
        codes = codes + (pltpu.roll(own, k * SIDE, 1) if k else own)
    return codes[:1].astype(jnp.int32) - 1, flag


def side_first(ids_row, tokens):
    rows, width = tokens.shape

    def kernel(row_ref, tok_ref, out_ref, seen_ref, at_col_ref):
        row = row_ref[...]
        seen = count_before(row, to_col(row))
        seen_ref[...] = seen
        home = row // HERE
        spot = row % HERE
        back = home * (HERE * MOST) + jnp.where(
            seen < MAIN, spot * MAIN + seen, HERE * MAIN + spot
        )
        at_col_ref[...] = to_col(back)
        third = seen >= MAIN
        key = home % 8

        def store(k, block):
            out_ref[k * SIDE : (k + 1) * SIDE, :] = block

        bucket(
            tok_ref[...], key, to_col(jnp.where(third, key, -1)), home // 8 * 8 + spot, third,
            jnp.zeros((1, 1), jnp.float32), store,
        )

    return pl.pallas_call(
        kernel,
        out_shape=[
            jax.ShapeDtypeStruct((8 * SIDE, width), jnp.bfloat16),
            jax.ShapeDtypeStruct((1, rows), jnp.int32),
            jax.ShapeDtypeStruct((rows, 1), jnp.int32),
        ],
        compiler_params=GRANT,
        name="side_first",
    )(ids_row, tokens)


def side_second(at, arrived):
    n, width = arrived.shape

    def kernel(at_ref, in_ref, *refs):
        out_refs, block_ref = refs[:8], refs[8]
        blocks = [in_ref[k * SIDE : (k + 1) * SIDE, :] for k in range(8)]
        code, flag = read_codes(blocks)
        valid = code >= 0
        key = jnp.where(valid, code // 8, -1)
        from_y = lax.broadcasted_iota(jnp.int32, (1, n), 1) // SIDE

        def store(k, block):
            block_ref[k] = block

        bucket(in_ref[...], key, to_col(key), from_y * 8 + code % 8, valid, flag, store)
        for k in range(8):
            out_refs[k][...] = block_ref[at_ref[0] ^ k]

    return pl.pallas_call(
        kernel,
        in_specs=[scalar_spec(), pl.BlockSpec(memory_space=pltpu.VMEM)],
        out_shape=[jax.ShapeDtypeStruct((SIDE, width), jnp.bfloat16)] * 8,
        scratch_shapes=[pltpu.VMEM((8, SIDE, width), jnp.bfloat16)],
        compiler_params=GRANT,
        name="side_second",
    )(at, arrived)


def fold(full, mine, rank):
    pair = 2 * rank
    lane = lax.broadcasted_iota(jnp.int32, (full.shape[0], pair), 1)
    kept = jnp.zeros((full.shape[0], pair), jnp.float32)
    for k in range(HERE // 2):
        holder = jnp.where(lane < rank, 2 * k, 2 * k + 1)
        kept = kept + jnp.where(mine == holder, full[:, k * pair : (k + 1) * pair], 0.0)
    return kept + pltpu.roll(kept, rank, 1)


def contract_last(x, y):
    return lax.dot_general(x, y, (((1,), (1,)), ((), ())), preferred_element_type=jnp.float32)


def side_low(at, blocks, down):
    here, rank, width = down.shape
    n = 8 * SIDE
    thirds = 64 * here
    pair = 2 * rank

    def kernel(at_ref, *refs):
        down_ref, out_ref, flag_ref = refs[8:]
        blocks = [ref[...] for ref in refs[:8]]
        code, flag = read_codes(blocks)
        from_z = (lax.broadcasted_iota(jnp.int32, (1, n), 1) // SIDE) ^ at_ref[0]
        slot = jnp.where(code >= 0, from_z * 64 + code, -1)
        rows_of = jnp.concatenate(blocks, axis=0)
        full = contract_last(rows_of, down_ref[...].reshape(here * rank, width))
        mine = to_col(jnp.where(code >= 0, code % 8, -1))
        low = fold(full, mine, rank).astype(jnp.bfloat16)
        spread = jnp.dot(pick_rows(slot, thirds), low, preferred_element_type=jnp.float32)
        lane = lax.broadcasted_iota(jnp.int32, (thirds // 2, pair), 1)
        out_ref[...] = jnp.where(
            lane < rank, spread[: thirds // 2], spread[thirds // 2 :]
        ).astype(jnp.bfloat16)
        flag_ref[...] = jnp.broadcast_to(flag, (8, 128))

    return pl.pallas_call(
        kernel,
        in_specs=[scalar_spec()] + [pl.BlockSpec(memory_space=pltpu.VMEM)] * 9,
        out_shape=[
            jax.ShapeDtypeStruct((thirds // 2, pair), jnp.bfloat16),
            jax.ShapeDtypeStruct((8, 128), jnp.float32),
        ],
        compiler_params=GRANT,
        name="side_low",
    )(at, *blocks, down)


def down_main(arrived, thirds, down):
    slots, width = arrived.shape
    here, rank, _ = down.shape
    half = slots // 2
    tile = 256
    pair = 2 * rank

    def kernel(in_ref, thirds_ref, down_ref, out_ref):
        weight = down_ref[...].reshape(here * rank, width)
        lane = lax.broadcasted_iota(jnp.int32, (tile, pair), 1)
        slot = lax.broadcasted_iota(jnp.int32, (tile, pair), 0)
        mine = slot % (HERE * MAIN) // MAIN
        for first in range(0, half, tile):
            lo = fold(contract_last(in_ref[first : first + tile, :], weight), mine, rank)
            hi = fold(
                contract_last(in_ref[half + first : half + first + tile, :], weight), mine, rank
            )
            out_ref[first : first + tile, :] = jnp.where(lane < rank, lo, hi).astype(jnp.bfloat16)
        out_ref[half:, :] = thirds_ref[...]

    return pl.pallas_call(
        kernel,
        out_shape=jax.ShapeDtypeStruct((half + thirds.shape[0], pair), jnp.bfloat16),
        compiler_params=GRANT,
        name="down_main",
    )(arrived, thirds, down)


def up_main(low, flag, up):
    here, rank, cols = up.shape
    owners = 2 * low.shape[0] // (here * MOST)
    half = owners * here * MAIN // 2

    def kernel(low_ref, flag_ref, up_ref, out_ref):
        weight = up_ref[...].reshape(here * rank, cols)

        def mapped(part, per):
            wide = part.astype(jnp.float32)
            turned = pltpu.roll(wide, rank, 1)
            lane = lax.broadcasted_iota(jnp.int32, wide.shape, 1)
            slot = lax.broadcasted_iota(jnp.int32, wide.shape, 0)
            mine = slot % (here * per) // per
            halves = []
            for h in range(2):
                both = jnp.where((lane < rank) == (h == 0), wide, turned)
                spread = []
                for k in range(here // 2):
                    holder = jnp.where(lane < rank, 2 * k, 2 * k + 1)
                    spread.append(jnp.where(mine == holder, both, 0.0).astype(jnp.bfloat16))
                halves.append(
                    jnp.dot(
                        jnp.concatenate(spread, axis=1), weight, preferred_element_type=jnp.float32
                    )
                )
            acc = jnp.concatenate(halves, axis=0) * adapter_output_scale
            return acc.reshape(owners, here * per, cols)

        main = mapped(low_ref[:half, :], MAIN)
        thirds = mapped(low_ref[half:, :], MOST - MAIN)
        both = jnp.concatenate([main, thirds], axis=1).reshape(owners * here * MOST, cols)
        out_ref[...] = jnp.where(flag_ref[:1, :1] > 0.0, LOST, both).astype(jnp.bfloat16)

    return pl.pallas_call(
        kernel,
        out_shape=jax.ShapeDtypeStruct((owners * here * MOST, cols), jnp.bfloat16),
        compiler_params=GRANT,
        name="up_main",
    )(low, flag, up)


def take_main(at_col, back, base):
    rows, cols = base.shape
    slots = back.shape[0]

    def kernel(at_ref, back_ref, base_ref, out_ref, lost_ref):
        slot = lax.broadcasted_iota(jnp.int32, (rows, slots), 1)
        pick = jnp.where(slot == at_ref[...], 1.0, 0.0).astype(jnp.bfloat16)
        mine = jnp.dot(pick, back_ref[...], preferred_element_type=jnp.float32)
        out_ref[...] = (base_ref[...] + mine).astype(jnp.bfloat16)
        lost_ref[0] = (jnp.max(back_ref[...].astype(jnp.float32)) > LOST / 2).astype(jnp.int32)

    return pl.pallas_call(
        kernel,
        out_specs=[pl.BlockSpec(memory_space=pltpu.VMEM), pl.BlockSpec(memory_space=pltpu.SMEM)],
        out_shape=[
            jax.ShapeDtypeStruct((rows, cols), jnp.bfloat16),
            jax.ShapeDtypeStruct((1,), jnp.int32),
        ],
        compiler_params=GRANT,
        name="take_main",
    )(at_col, back, base)


def low_of_all(low_part, groups):
    rows, pair = low_part.shape
    parts = swap(low_part.reshape(groups, rows // groups, pair), TENSOR)
    share = parts.astype(jnp.float32).sum(axis=0).astype(jnp.bfloat16)
    copies = jnp.broadcast_to(share[None], (groups, *share.shape))
    return swap(copies, TENSOR).reshape(rows, pair)


def whole_exchange(tokens, adapter_down, adapter_up_weight, adapter_ids, base):
    rows, width = tokens.shape
    cols = adapter_up_weight.shape[2]
    share = HERE * MOST
    slots = 64 * share
    placed, at_col = full_place(adapter_ids.reshape(1, rows), tokens, slots)
    arrived = swap(placed.reshape(64, share, width), ADAPTER).reshape(slots, width)
    low = low_of_all(full_down(arrived, adapter_down), lax.axis_size(TENSOR))
    delta = full_up(low, adapter_up_weight)
    back = swap(delta.reshape(64, share, cols), ADAPTER).reshape(slots, cols)
    return full_take(at_col, back, base)


def layer(tokens, value_weight, adapter_down, adapter_up_weight, adapter_ids):
    groups = lax.axis_size(TENSOR)
    rows, width = tokens.shape
    cols = adapter_up_weight.shape[2]
    ids_row = adapter_ids.reshape(1, rows)
    at_z = lax.axis_index("z").astype(jnp.int32)

    blocks, seen, at_col = side_first(ids_row, tokens)
    blocks = swap(blocks.reshape(8, SIDE, width), "y").reshape(8 * SIDE, width)
    placed = place_main(ids_row, seen, tokens, 64 * HERE * MAIN)
    arrived = swap(placed.reshape(64, HERE * MAIN, width), ADAPTER)
    arrived = arrived.reshape(64 * HERE * MAIN, width)

    blocks = side_second(at_z.reshape(1), blocks)
    blocks = xor_sends(blocks, "z")
    thirds, flag = side_low(at_z.reshape(1), blocks, adapter_down)

    at = lax.axis_index(TENSOR).astype(jnp.int32).reshape(1)
    own, other = value_pieces(tokens, value_weight, at, groups)
    other = lax.ppermute(other, TENSOR[1], [(0, 1), (1, 0)])
    pairs = pair_sum(own, other)
    pairs = xor_sends([own, *pairs], TENSOR[0])[1:]
    base = base_sum(own, other, pairs)

    low = low_of_all(down_main(arrived, thirds, adapter_down), groups)
    delta = up_main(low, flag, adapter_up_weight)
    back = swap(delta.reshape(64, HERE * MOST, cols), ADAPTER).reshape(64 * HERE * MOST, cols)
    values, lost = take_main(at_col, back, base)
    return lax.cond(
        lost[0] > 0,
        lambda: whole_exchange(tokens, adapter_down, adapter_up_weight, adapter_ids, base),
        lambda: values,
    )


def xor_sends(pieces, axis):
    size = lax.axis_size(axis)
    parts = [pieces[0]]
    for k in range(1, size):
        parts.append(lax.ppermute(pieces[k], axis, [(i, i ^ k) for i in range(size)]))
    return parts


def solution(mesh):
    torus = Mesh(mesh.devices.reshape(8, 8, 4, 2), (*ADAPTER, *TENSOR))
    return jax.shard_map(
        layer,
        mesh=torus,
        in_specs=(
            P(ADAPTER, TENSOR),
            P(TENSOR, None),
            P(ADAPTER, None, TENSOR),
            P(ADAPTER, None, TENSOR),
            P(ADAPTER, None),
        ),
        out_specs=P(ADAPTER, TENSOR),
        check_vma=False,
    )
```

```python
import jax
import jax.numpy as jnp
from jax import lax
from jax.experimental import pallas as pl
from jax.experimental.pallas import tpu as pltpu
from jax.sharding import Mesh
from jax.sharding import PartitionSpec as P


TENSOR = ("tensor_0", "tensor_1")
ADAPTER = ("z", "y")
HERE = 8
MOST = 3
MAIN = 2
SIDE = 16
LOST = 3e38
GRANT = pltpu.CompilerParams(vmem_limit_bytes=16 * 2**20)

adapter_output_scale = 2.0


def swap(x, axes):
    return lax.all_to_all(x, axes, split_axis=0, concat_axis=0, tiled=True)


def full_place(ids_row, tokens, slots):
    rows, width = tokens.shape
    tile = 256

    def kernel(row_ref, tok_ref, out_ref, at_col_ref, at_row_ref):
        @pl.when(pl.program_id(0) == 0)
        def _():
            row = row_ref[...]
            col = jnp.broadcast_to(row, (128, rows)).T[:, :1]
            same = row == col
            i = lax.broadcasted_iota(jnp.int32, (rows, rows), 0)
            j = lax.broadcasted_iota(jnp.int32, (rows, rows), 1)
            before_row = jnp.sum(jnp.where(same & (i < j), 1, 0), axis=0, keepdims=True)
            before_col = jnp.sum(jnp.where(same & (j < i), 1, 0), axis=1, keepdims=True)
            at_row_ref[...] = row * MOST + before_row
            at_col_ref[...] = col * MOST + before_col

        first = pl.program_id(0) * tile
        slot = lax.broadcasted_iota(jnp.int32, (tile, rows), 0) + first
        pick = jnp.where(slot == at_row_ref[...], 1.0, 0.0).astype(jnp.bfloat16)
        out_ref[...] = jnp.dot(pick, tok_ref[...], preferred_element_type=jnp.float32).astype(
            jnp.bfloat16
        )

    return pl.pallas_call(
        kernel,
        grid=(slots // tile,),
        in_specs=[
            pl.BlockSpec((1, rows), lambda i: (0, 0)),
            pl.BlockSpec((rows, width), lambda i: (0, 0)),
        ],
        out_specs=[
            pl.BlockSpec((tile, width), lambda i: (i, 0)),
            pl.BlockSpec((rows, 1), lambda i: (0, 0)),
        ],
        out_shape=[
            jax.ShapeDtypeStruct((slots, width), tokens.dtype),
            jax.ShapeDtypeStruct((rows, 1), jnp.int32),
        ],
        scratch_shapes=[pltpu.VMEM((1, rows), jnp.int32)],
        compiler_params=GRANT,
        name="full_place",
    )(ids_row, tokens)


def value_pieces(tokens, weight, at, pieces):
    rows, width = tokens.shape
    cols = weight.shape[1] // pieces
    step = 2

    def kernel(at_ref, tok_ref, w_ref, own_ref, other_ref, part_ref):
        for first in range(0, pieces, step):
            part = jnp.dot(
                tok_ref[...],
                w_ref[:, first * cols : (first + step) * cols],
                preferred_element_type=jnp.float32,
            ).astype(jnp.bfloat16)
            for k in range(step):
                part_ref[first + k] = part[:, k * cols : (k + 1) * cols]
        for k in range(pieces // 2):
            own_ref[k] = part_ref[at_ref[0] ^ (2 * k)]
            other_ref[k] = part_ref[at_ref[0] ^ (2 * k + 1)]

    return pl.pallas_call(
        kernel,
        in_specs=[
            pl.BlockSpec(memory_space=pltpu.SMEM),
            pl.BlockSpec((rows, width), lambda: (0, 0)),
            pl.BlockSpec(weight.shape, lambda: (0, 0)),
        ],
        out_shape=[jax.ShapeDtypeStruct((pieces // 2, rows, cols), jnp.bfloat16)] * 2,
        scratch_shapes=[pltpu.VMEM((pieces, rows, cols), jnp.bfloat16)],
        compiler_params=GRANT,
        name="value_pieces",
    )(at, tokens, weight)


def pair_sum(own, other):
    count, rows, cols = own.shape

    def kernel(own_ref, other_ref, *out_refs):
        for k in range(1, count):
            total = own_ref[k].astype(jnp.float32) + other_ref[k].astype(jnp.float32)
            out_refs[k - 1][...] = total.astype(jnp.bfloat16)

    return pl.pallas_call(
        kernel,
        out_shape=[jax.ShapeDtypeStruct((rows, cols), jnp.bfloat16)] * (count - 1),
        compiler_params=GRANT,
        name="pair_sum",
    )(own, other)


def base_sum(own, other, parts):
    def kernel(own_ref, other_ref, *refs):
        total = own_ref[0].astype(jnp.float32) + other_ref[0].astype(jnp.float32)
        for ref in refs[:-1]:
            total = total + ref[...].astype(jnp.float32)
        refs[-1][...] = total

    return pl.pallas_call(
        kernel,
        out_shape=jax.ShapeDtypeStruct(parts[0].shape, jnp.float32),
        compiler_params=GRANT,
        name="base_sum",
    )(own, other, *parts)


def adapter_of(shape, first, group):
    slot = lax.broadcasted_iota(jnp.int32, shape, 0) + first
    return slot % group // MOST


def full_down(arrived, down):
    slots, width = arrived.shape
    here, rank, _ = down.shape
    group = here * MOST
    half = slots // 2
    tile = 192
    pair = 2 * rank

    def kernel(lo_ref, hi_ref, down_ref, out_ref):
        weight = down_ref[...].reshape(here * rank, width)
        lane = lax.broadcasted_iota(jnp.int32, (tile, pair), 1)

        def rows_of(ref):
            full = lax.dot_general(
                ref[...], weight, (((1,), (1,)), ((), ())), preferred_element_type=jnp.float32
            )
            mine = adapter_of((tile, pair), 0, group)
            kept = jnp.zeros((tile, pair), jnp.float32)
            for k in range(here // 2):
                holder = jnp.where(lane < rank, 2 * k, 2 * k + 1)
                kept = kept + jnp.where(mine == holder, full[:, k * pair : (k + 1) * pair], 0.0)
            return kept + pltpu.roll(kept, rank, 1)

        out_ref[...] = jnp.where(lane < rank, rows_of(lo_ref), rows_of(hi_ref)).astype(
            jnp.bfloat16
        )

    steps = half // tile
    return pl.pallas_call(
        kernel,
        grid=(steps,),
        in_specs=[
            pl.BlockSpec((tile, width), lambda i: (i, 0)),
            pl.BlockSpec((tile, width), lambda i: (i + steps, 0)),
            pl.BlockSpec((here, rank, width), lambda i: (0, 0, 0)),
        ],
        out_specs=pl.BlockSpec((tile, pair), lambda i: (i, 0)),
        out_shape=jax.ShapeDtypeStruct((half, pair), jnp.bfloat16),
        compiler_params=GRANT,
        name="full_down",
    )(arrived, arrived, down)


def full_up(low, up):
    half, pair = low.shape
    here, rank, cols = up.shape
    group = here * MOST

    def kernel(low_ref, up_ref, out_ref):
        weight = up_ref[...].reshape(here * rank, cols)
        low_wide = low_ref[...].astype(jnp.float32)
        turned = pltpu.roll(low_wide, rank, 1)
        lane = lax.broadcasted_iota(jnp.int32, (half, pair), 1)
        mine = adapter_of((half, pair), 0, group)
        for h in range(2):
            own = (lane < rank) == (h == 0)
            both = jnp.where(own, low_wide, turned)
            spread = []
            for k in range(here // 2):
                holder = jnp.where(lane < rank, 2 * k, 2 * k + 1)
                spread.append(jnp.where(mine == holder, both, 0.0).astype(jnp.bfloat16))
            acc = jnp.dot(
                jnp.concatenate(spread, axis=1), weight, preferred_element_type=jnp.float32
            )
            out_ref[h * half : (h + 1) * half, :] = (adapter_output_scale * acc).astype(
                jnp.bfloat16
            )

    return pl.pallas_call(
        kernel,
        out_shape=jax.ShapeDtypeStruct((2 * half, cols), jnp.bfloat16),
        compiler_params=GRANT,
        name="full_up",
    )(low, up)


def full_take(at_col, back, base):
    rows, cols = base.shape
    slots = back.shape[0]

    def kernel(at_ref, back_ref, base_ref, out_ref):
        slot = lax.broadcasted_iota(jnp.int32, (rows, slots), 1)
        pick = jnp.where(slot == at_ref[...], 1.0, 0.0).astype(jnp.bfloat16)
        mine = jnp.dot(pick, back_ref[...], preferred_element_type=jnp.float32)
        out_ref[...] = (base_ref[...] + mine).astype(jnp.bfloat16)

    return pl.pallas_call(
        kernel,
        out_shape=jax.ShapeDtypeStruct((rows, cols), jnp.bfloat16),
        compiler_params=GRANT,
        name="full_take",
    )(at_col, back, base)


def scalar_spec():
    return pl.BlockSpec(memory_space=pltpu.SMEM)


def count_before(row, col):
    n = row.shape[1]
    j = lax.broadcasted_iota(jnp.int32, (n, n), 0)
    i = lax.broadcasted_iota(jnp.int32, (n, n), 1)
    return jnp.sum(jnp.where((row == col) & (j < i), 1, 0), axis=0, keepdims=True)


def to_col(row):
    return jnp.broadcast_to(row, (128, row.shape[1])).T[:, :1]


def pick_rows(at_row, slots, first=0):
    n = at_row.shape[1]
    slot = lax.broadcasted_iota(jnp.int32, (slots, n), 0) + first
    return jnp.where(slot == at_row, 1.0, 0.0).astype(jnp.bfloat16)


def place_main(ids_row, seen, tokens, slots):
    rows, width = tokens.shape
    tile = 256

    def kernel(row_ref, seen_ref, tok_ref, out_ref):
        at_row = jnp.where(seen_ref[...] < MAIN, row_ref[...] * MAIN + seen_ref[...], -1)
        pick = pick_rows(at_row, tile, pl.program_id(0) * tile)
        out_ref[...] = jnp.dot(pick, tok_ref[...], preferred_element_type=jnp.float32).astype(
            jnp.bfloat16
        )

    return pl.pallas_call(
        kernel,
        grid=(slots // tile,),
        in_specs=[
            pl.BlockSpec((1, rows), lambda i: (0, 0)),
            pl.BlockSpec((1, rows), lambda i: (0, 0)),
            pl.BlockSpec((rows, width), lambda i: (0, 0)),
        ],
        out_specs=pl.BlockSpec((tile, width), lambda i: (i, 0)),
        out_shape=jax.ShapeDtypeStruct((slots, width), tokens.dtype),
        compiler_params=GRANT,
        name="place_main",
    )(ids_row, seen, tokens)


def bucket(rows_of, key, key_col, code, valid, flag, store):
    n = key.shape[1]
    width = rows_of.shape[1]
    q = count_before(key, key_col)
    fits = valid & (q < SIDE - 1)
    lost = jnp.max(jnp.where(valid & (q >= SIDE - 1), 1.0, 0.0), axis=1, keepdims=True)
    flag = jnp.maximum(flag, lost)
    pick = pick_rows(jnp.where(fits, key * SIDE + q, -1), 8 * SIDE)
    data = jnp.dot(pick, rows_of, preferred_element_type=jnp.float32)
    which = lax.broadcasted_iota(jnp.int32, (8, n), 0)
    owned = jnp.where(fits & (which == key), (code + 1).astype(jnp.float32), 0.0)
    place = lax.broadcasted_iota(jnp.int32, (128, n), 0)
    there = jnp.where(place == q, 1.0, 0.0)
    codes = lax.dot_general(
        owned.astype(jnp.bfloat16),
        there.astype(jnp.bfloat16),
        (((1,), (1,)), ((), ())),
        preferred_element_type=jnp.float32,
    )
    lane = lax.broadcasted_iota(jnp.int32, (8, 128), 1)
    codes = jnp.where(lane == 127, flag, codes)
    wide = jnp.concatenate([codes, jnp.zeros((8, width - 128), jnp.float32)], axis=1)
    row = lax.broadcasted_iota(jnp.int32, (SIDE, width), 0)
    for k in range(8):
        note = jnp.broadcast_to(wide[k : k + 1], (SIDE, width))
        block = jnp.where(row == SIDE - 1, note, data[k * SIDE : (k + 1) * SIDE])
        store(k, block.astype(jnp.bfloat16))


def read_codes(blocks):
    n = 8 * SIDE
    lane = lax.broadcasted_iota(jnp.int32, (8, n), 1)
    codes = jnp.zeros((8, n), jnp.float32)
    flag = jnp.zeros((1, 1), jnp.float32)
    for k in range(8):
        note = blocks[k].astype(jnp.float32)[SIDE - 1 : SIDE, :n]
        flag = jnp.maximum(flag, note[:, 127:128])
        own = jnp.where(lane < SIDE - 1, jnp.broadcast_to(note, (8, n)), 0.0)
        codes = codes + (pltpu.roll(own, k * SIDE, 1) if k else own)
    return codes[:1].astype(jnp.int32) - 1, flag


def side_first(ids_row, tokens):
    rows, width = tokens.shape

    def kernel(row_ref, tok_ref, out_ref, seen_ref, at_col_ref):
        row = row_ref[...]
        seen = count_before(row, to_col(row))
        seen_ref[...] = seen
        home = row // HERE
        spot = row % HERE
        back = home * (HERE * MOST) + jnp.where(
            seen < MAIN, spot * MAIN + seen, HERE * MAIN + spot
        )
        at_col_ref[...] = to_col(back)
        third = seen >= MAIN
        key = home % 8

        def store(k, block):
            out_ref[k * SIDE : (k + 1) * SIDE, :] = block

        bucket(
            tok_ref[...], key, to_col(jnp.where(third, key, -1)), home // 8 * 8 + spot, third,
            jnp.zeros((1, 1), jnp.float32), store,
        )

    return pl.pallas_call(
        kernel,
        out_shape=[
            jax.ShapeDtypeStruct((8 * SIDE, width), jnp.bfloat16),
            jax.ShapeDtypeStruct((1, rows), jnp.int32),
            jax.ShapeDtypeStruct((rows, 1), jnp.int32),
        ],
        compiler_params=GRANT,
        name="side_first",
    )(ids_row, tokens)


def side_second(at, arrived):
    n, width = arrived.shape

    def kernel(at_ref, in_ref, *refs):
        out_refs, block_ref = refs[:8], refs[8]
        blocks = [in_ref[k * SIDE : (k + 1) * SIDE, :] for k in range(8)]
        code, flag = read_codes(blocks)
        valid = code >= 0
        key = jnp.where(valid, code // 8, -1)
        from_y = lax.broadcasted_iota(jnp.int32, (1, n), 1) // SIDE

        def store(k, block):
            block_ref[k] = block

        bucket(in_ref[...], key, to_col(key), from_y * 8 + code % 8, valid, flag, store)
        for k in range(8):
            out_refs[k][...] = block_ref[at_ref[0] ^ k]

    return pl.pallas_call(
        kernel,
        in_specs=[scalar_spec(), pl.BlockSpec(memory_space=pltpu.VMEM)],
        out_shape=[jax.ShapeDtypeStruct((SIDE, width), jnp.bfloat16)] * 8,
        scratch_shapes=[pltpu.VMEM((8, SIDE, width), jnp.bfloat16)],
        compiler_params=GRANT,
        name="side_second",
    )(at, arrived)


def fold(full, mine, rank):
    pair = 2 * rank
    lane = lax.broadcasted_iota(jnp.int32, (full.shape[0], pair), 1)
    kept = jnp.zeros((full.shape[0], pair), jnp.float32)
    for k in range(HERE // 2):
        holder = jnp.where(lane < rank, 2 * k, 2 * k + 1)
        kept = kept + jnp.where(mine == holder, full[:, k * pair : (k + 1) * pair], 0.0)
    return kept + pltpu.roll(kept, rank, 1)


def contract_last(x, y):
    return lax.dot_general(x, y, (((1,), (1,)), ((), ())), preferred_element_type=jnp.float32)


def side_low(at, blocks, down):
    here, rank, width = down.shape
    n = 8 * SIDE
    thirds = 64 * here
    pair = 2 * rank

    def kernel(at_ref, *refs):
        down_ref, out_ref, flag_ref = refs[8:]
        blocks = [ref[...] for ref in refs[:8]]
        code, flag = read_codes(blocks)
        from_z = (lax.broadcasted_iota(jnp.int32, (1, n), 1) // SIDE) ^ at_ref[0]
        slot = jnp.where(code >= 0, from_z * 64 + code, -1)
        rows_of = jnp.concatenate(blocks, axis=0)
        full = contract_last(rows_of, down_ref[...].reshape(here * rank, width))
        mine = to_col(jnp.where(code >= 0, code % 8, -1))
        low = fold(full, mine, rank).astype(jnp.bfloat16)
        spread = jnp.dot(pick_rows(slot, thirds), low, preferred_element_type=jnp.float32)
        lane = lax.broadcasted_iota(jnp.int32, (thirds // 2, pair), 1)
        out_ref[...] = jnp.where(
            lane < rank, spread[: thirds // 2], spread[thirds // 2 :]
        ).astype(jnp.bfloat16)
        flag_ref[...] = jnp.broadcast_to(flag, (8, 128))

    return pl.pallas_call(
        kernel,
        in_specs=[scalar_spec()] + [pl.BlockSpec(memory_space=pltpu.VMEM)] * 9,
        out_shape=[
            jax.ShapeDtypeStruct((thirds // 2, pair), jnp.bfloat16),
            jax.ShapeDtypeStruct((8, 128), jnp.float32),
        ],
        compiler_params=GRANT,
        name="side_low",
    )(at, *blocks, down)


def down_main(at, arrived, thirds, down):
    slots, width = arrived.shape
    here, rank, _ = down.shape
    half = slots // 2
    tile = 256
    pair = 2 * rank
    share = (half + thirds.shape[0]) // 2

    def kernel(at_ref, in_ref, thirds_ref, down_ref, own_ref, other_ref, all_ref):
        weight = down_ref[...].reshape(here * rank, width)
        lane = lax.broadcasted_iota(jnp.int32, (tile, pair), 1)
        slot = lax.broadcasted_iota(jnp.int32, (tile, pair), 0)
        mine = slot % (HERE * MAIN) // MAIN
        parts = []
        for first in range(0, half, tile):
            lo = fold(contract_last(in_ref[first : first + tile, :], weight), mine, rank)
            hi = fold(
                contract_last(in_ref[half + first : half + first + tile, :], weight), mine, rank
            )
            parts.append(jnp.where(lane < rank, lo, hi).astype(jnp.bfloat16))
        rows = jnp.concatenate([*parts, thirds_ref[...]], axis=0)
        for k in range(2):
            all_ref[k] = rows[k * share : (k + 1) * share]
        own_ref[...] = all_ref[at_ref[0]]
        other_ref[...] = all_ref[1 - at_ref[0]]

    return pl.pallas_call(
        kernel,
        in_specs=[scalar_spec()] + [pl.BlockSpec(memory_space=pltpu.VMEM)] * 3,
        out_shape=[jax.ShapeDtypeStruct((share, pair), jnp.bfloat16)] * 2,
        scratch_shapes=[pltpu.VMEM((2, share, pair), jnp.bfloat16)],
        compiler_params=GRANT,
        name="down_main",
    )(at, arrived, thirds, down)


def up_main(low, flag, up):
    here, rank, cols = up.shape
    owners = 2 * low.shape[0] // (here * MOST)
    half = owners * here * MAIN // 2

    def kernel(low_ref, flag_ref, up_ref, out_ref):
        weight = up_ref[...].reshape(here * rank, cols)

        def mapped(part, per):
            wide = part.astype(jnp.float32)
            turned = pltpu.roll(wide, rank, 1)
            lane = lax.broadcasted_iota(jnp.int32, wide.shape, 1)
            slot = lax.broadcasted_iota(jnp.int32, wide.shape, 0)
            mine = slot % (here * per) // per
            halves = []
            for h in range(2):
                both = jnp.where((lane < rank) == (h == 0), wide, turned)
                spread = []
                for k in range(here // 2):
                    holder = jnp.where(lane < rank, 2 * k, 2 * k + 1)
                    spread.append(jnp.where(mine == holder, both, 0.0).astype(jnp.bfloat16))
                halves.append(
                    jnp.dot(
                        jnp.concatenate(spread, axis=1), weight, preferred_element_type=jnp.float32
                    )
                )
            acc = jnp.concatenate(halves, axis=0) * adapter_output_scale
            return acc.reshape(owners, here * per, cols)

        main = mapped(low_ref[:half, :], MAIN)
        thirds = mapped(low_ref[half:, :], MOST - MAIN)
        both = jnp.concatenate([main, thirds], axis=1).reshape(owners * here * MOST, cols)
        out_ref[...] = jnp.where(flag_ref[:1, :1] > 0.0, LOST, both).astype(jnp.bfloat16)

    return pl.pallas_call(
        kernel,
        out_shape=jax.ShapeDtypeStruct((owners * here * MOST, cols), jnp.bfloat16),
        compiler_params=GRANT,
        name="up_main",
    )(low, flag, up)


def take_main(at_col, back, base):
    rows, cols = base.shape
    slots = back.shape[0]

    def kernel(at_ref, back_ref, base_ref, out_ref, lost_ref):
        slot = lax.broadcasted_iota(jnp.int32, (rows, slots), 1)
        pick = jnp.where(slot == at_ref[...], 1.0, 0.0).astype(jnp.bfloat16)
        mine = jnp.dot(pick, back_ref[...], preferred_element_type=jnp.float32)
        out_ref[...] = (base_ref[...] + mine).astype(jnp.bfloat16)
        lost_ref[0] = (jnp.max(back_ref[...].astype(jnp.float32)) > LOST / 2).astype(jnp.int32)

    return pl.pallas_call(
        kernel,
        out_specs=[pl.BlockSpec(memory_space=pltpu.VMEM), pl.BlockSpec(memory_space=pltpu.SMEM)],
        out_shape=[
            jax.ShapeDtypeStruct((rows, cols), jnp.bfloat16),
            jax.ShapeDtypeStruct((1,), jnp.int32),
        ],
        compiler_params=GRANT,
        name="take_main",
    )(at_col, back, base)


def low_of_all(low_part, groups):
    rows, pair = low_part.shape
    parts = swap(low_part.reshape(groups, rows // groups, pair), TENSOR)
    share = parts.astype(jnp.float32).sum(axis=0).astype(jnp.bfloat16)
    copies = jnp.broadcast_to(share[None], (groups, *share.shape))
    return swap(copies, TENSOR).reshape(rows, pair)


def low_of_pairs(own, other):
    rounded = own.astype(jnp.float32)
    rounded = rounded + lax.ppermute(other, TENSOR[1], [(0, 1), (1, 0)]).astype(jnp.float32)
    chips = lax.axis_size(TENSOR[0])
    copies = jnp.broadcast_to(rounded.astype(jnp.bfloat16)[None], (chips, *own.shape))
    total = swap(copies, TENSOR[0]).astype(jnp.float32).sum(axis=0).astype(jnp.bfloat16)
    return lax.all_gather(total, TENSOR[1], axis=0, tiled=True)


def whole_exchange(tokens, adapter_down, adapter_up_weight, adapter_ids, base):
    rows, width = tokens.shape
    cols = adapter_up_weight.shape[2]
    share = HERE * MOST
    slots = 64 * share
    placed, at_col = full_place(adapter_ids.reshape(1, rows), tokens, slots)
    arrived = swap(placed.reshape(64, share, width), ADAPTER).reshape(slots, width)
    low = low_of_all(full_down(arrived, adapter_down), lax.axis_size(TENSOR))
    delta = full_up(low, adapter_up_weight)
    back = swap(delta.reshape(64, share, cols), ADAPTER).reshape(slots, cols)
    return full_take(at_col, back, base)


def layer(tokens, value_weight, adapter_down, adapter_up_weight, adapter_ids):
    groups = lax.axis_size(TENSOR)
    rows, width = tokens.shape
    cols = adapter_up_weight.shape[2]
    ids_row = adapter_ids.reshape(1, rows)
    at_z = lax.axis_index("z").astype(jnp.int32)

    blocks, seen, at_col = side_first(ids_row, tokens)
    blocks = swap(blocks.reshape(8, SIDE, width), "y").reshape(8 * SIDE, width)
    placed = place_main(ids_row, seen, tokens, 64 * HERE * MAIN)
    arrived = swap(placed.reshape(64, HERE * MAIN, width), ADAPTER)
    arrived = arrived.reshape(64 * HERE * MAIN, width)

    blocks = side_second(at_z.reshape(1), blocks)
    blocks = xor_sends(blocks, "z")
    thirds, flag = side_low(at_z.reshape(1), blocks, adapter_down)

    at = lax.axis_index(TENSOR).astype(jnp.int32).reshape(1)
    own, other = value_pieces(tokens, value_weight, at, groups)
    other = lax.ppermute(other, TENSOR[1], [(0, 1), (1, 0)])
    pairs = pair_sum(own, other)
    pairs = xor_sends([own, *pairs], TENSOR[0])[1:]
    base = base_sum(own, other, pairs)

    core = lax.axis_index(TENSOR[1]).astype(jnp.int32).reshape(1)
    low = low_of_pairs(*down_main(core, arrived, thirds, adapter_down))
    delta = up_main(low, flag, adapter_up_weight)
    back = swap(delta.reshape(64, HERE * MOST, cols), ADAPTER).reshape(64 * HERE * MOST, cols)
    back, *whole = lax.optimization_barrier(
        (back, tokens, adapter_down, adapter_up_weight, adapter_ids, base)
    )
    values, lost = take_main(at_col, back, base)
    return lax.cond(
        lost[0] > 0,
        lambda: whole_exchange(*whole),
        lambda: values,
    )


def xor_sends(pieces, axis):
    size = lax.axis_size(axis)
    parts = [pieces[0]]
    for k in range(1, size):
        parts.append(lax.ppermute(pieces[k], axis, [(i, i ^ k) for i in range(size)]))
    return parts


def solution(mesh):
    torus = Mesh(mesh.devices.reshape(8, 8, 4, 2), (*ADAPTER, *TENSOR))
    return jax.shard_map(
        layer,
        mesh=torus,
        in_specs=(
            P(ADAPTER, TENSOR),
            P(TENSOR, None),
            P(ADAPTER, None, TENSOR),
            P(ADAPTER, None, TENSOR),
            P(ADAPTER, None),
        ),
        out_specs=P(ADAPTER, TENSOR),
        check_vma=False,
    )
```

```python
import jax
import jax.numpy as jnp
from jax import lax
from jax.experimental import pallas as pl
from jax.experimental.pallas import tpu as pltpu
from jax.sharding import Mesh
from jax.sharding import PartitionSpec as P


TENSOR = ("tensor_0", "tensor_1")
ADAPTER = ("z", "y")
HERE = 8
MOST = 3
MAIN = 2
SIDE = 16
LOST = 3e38
GRANT = pltpu.CompilerParams(vmem_limit_bytes=16 * 2**20)

adapter_output_scale = 2.0


def swap(x, axes):
    return lax.all_to_all(x, axes, split_axis=0, concat_axis=0, tiled=True)


def full_place(ids_row, tokens, slots):
    rows, width = tokens.shape
    tile = 256

    def kernel(row_ref, tok_ref, out_ref, at_col_ref, at_row_ref):
        @pl.when(pl.program_id(0) == 0)
        def _():
            row = row_ref[...]
            col = jnp.broadcast_to(row, (128, rows)).T[:, :1]
            same = row == col
            i = lax.broadcasted_iota(jnp.int32, (rows, rows), 0)
            j = lax.broadcasted_iota(jnp.int32, (rows, rows), 1)
            before_row = jnp.sum(jnp.where(same & (i < j), 1, 0), axis=0, keepdims=True)
            before_col = jnp.sum(jnp.where(same & (j < i), 1, 0), axis=1, keepdims=True)
            at_row_ref[...] = row * MOST + before_row
            at_col_ref[...] = col * MOST + before_col

        first = pl.program_id(0) * tile
        slot = lax.broadcasted_iota(jnp.int32, (tile, rows), 0) + first
        pick = jnp.where(slot == at_row_ref[...], 1.0, 0.0).astype(jnp.bfloat16)
        out_ref[...] = jnp.dot(pick, tok_ref[...], preferred_element_type=jnp.float32).astype(
            jnp.bfloat16
        )

    return pl.pallas_call(
        kernel,
        grid=(slots // tile,),
        in_specs=[
            pl.BlockSpec((1, rows), lambda i: (0, 0)),
            pl.BlockSpec((rows, width), lambda i: (0, 0)),
        ],
        out_specs=[
            pl.BlockSpec((tile, width), lambda i: (i, 0)),
            pl.BlockSpec((rows, 1), lambda i: (0, 0)),
        ],
        out_shape=[
            jax.ShapeDtypeStruct((slots, width), tokens.dtype),
            jax.ShapeDtypeStruct((rows, 1), jnp.int32),
        ],
        scratch_shapes=[pltpu.VMEM((1, rows), jnp.int32)],
        compiler_params=GRANT,
        name="full_place",
    )(ids_row, tokens)


def value_pieces(tokens, weight, at, pieces):
    rows, width = tokens.shape
    cols = weight.shape[1] // pieces
    step = 2

    def kernel(at_ref, tok_ref, w_ref, own_ref, other_ref, part_ref):
        for first in range(0, pieces, step):
            part = jnp.dot(
                tok_ref[...],
                w_ref[:, first * cols : (first + step) * cols],
                preferred_element_type=jnp.float32,
            ).astype(jnp.bfloat16)
            for k in range(step):
                part_ref[first + k] = part[:, k * cols : (k + 1) * cols]
        for k in range(pieces // 2):
            own_ref[k] = part_ref[at_ref[0] ^ (2 * k)]
            other_ref[k] = part_ref[at_ref[0] ^ (2 * k + 1)]

    return pl.pallas_call(
        kernel,
        in_specs=[
            pl.BlockSpec(memory_space=pltpu.SMEM),
            pl.BlockSpec((rows, width), lambda: (0, 0)),
            pl.BlockSpec(weight.shape, lambda: (0, 0)),
        ],
        out_shape=[jax.ShapeDtypeStruct((pieces // 2, rows, cols), jnp.bfloat16)] * 2,
        scratch_shapes=[pltpu.VMEM((pieces, rows, cols), jnp.bfloat16)],
        compiler_params=GRANT,
        name="value_pieces",
    )(at, tokens, weight)


def pair_sum(own, other):
    count, rows, cols = own.shape

    def kernel(own_ref, other_ref, *out_refs):
        for k in range(1, count):
            total = own_ref[k].astype(jnp.float32) + other_ref[k].astype(jnp.float32)
            out_refs[k - 1][...] = total.astype(jnp.bfloat16)

    return pl.pallas_call(
        kernel,
        out_shape=[jax.ShapeDtypeStruct((rows, cols), jnp.bfloat16)] * (count - 1),
        compiler_params=GRANT,
        name="pair_sum",
    )(own, other)


def base_sum(own, other, parts):
    def kernel(own_ref, other_ref, *refs):
        total = own_ref[0].astype(jnp.float32) + other_ref[0].astype(jnp.float32)
        for ref in refs[:-1]:
            total = total + ref[...].astype(jnp.float32)
        refs[-1][...] = total

    return pl.pallas_call(
        kernel,
        out_shape=jax.ShapeDtypeStruct(parts[0].shape, jnp.float32),
        compiler_params=GRANT,
        name="base_sum",
    )(own, other, *parts)


def adapter_of(shape, first, group):
    slot = lax.broadcasted_iota(jnp.int32, shape, 0) + first
    return slot % group // MOST


def full_down(arrived, down):
    slots, width = arrived.shape
    here, rank, _ = down.shape
    group = here * MOST
    half = slots // 2
    tile = 192
    pair = 2 * rank

    def kernel(lo_ref, hi_ref, down_ref, out_ref):
        weight = down_ref[...].reshape(here * rank, width)
        lane = lax.broadcasted_iota(jnp.int32, (tile, pair), 1)

        def rows_of(ref):
            full = lax.dot_general(
                ref[...], weight, (((1,), (1,)), ((), ())), preferred_element_type=jnp.float32
            )
            mine = adapter_of((tile, pair), 0, group)
            kept = jnp.zeros((tile, pair), jnp.float32)
            for k in range(here // 2):
                holder = jnp.where(lane < rank, 2 * k, 2 * k + 1)
                kept = kept + jnp.where(mine == holder, full[:, k * pair : (k + 1) * pair], 0.0)
            return kept + pltpu.roll(kept, rank, 1)

        out_ref[...] = jnp.where(lane < rank, rows_of(lo_ref), rows_of(hi_ref)).astype(
            jnp.bfloat16
        )

    steps = half // tile
    return pl.pallas_call(
        kernel,
        grid=(steps,),
        in_specs=[
            pl.BlockSpec((tile, width), lambda i: (i, 0)),
            pl.BlockSpec((tile, width), lambda i: (i + steps, 0)),
            pl.BlockSpec((here, rank, width), lambda i: (0, 0, 0)),
        ],
        out_specs=pl.BlockSpec((tile, pair), lambda i: (i, 0)),
        out_shape=jax.ShapeDtypeStruct((half, pair), jnp.bfloat16),
        compiler_params=GRANT,
        name="full_down",
    )(arrived, arrived, down)


def full_up(low, up):
    half, pair = low.shape
    here, rank, cols = up.shape
    group = here * MOST

    def kernel(low_ref, up_ref, out_ref):
        weight = up_ref[...].reshape(here * rank, cols)
        low_wide = low_ref[...].astype(jnp.float32)
        turned = pltpu.roll(low_wide, rank, 1)
        lane = lax.broadcasted_iota(jnp.int32, (half, pair), 1)
        mine = adapter_of((half, pair), 0, group)
        for h in range(2):
            own = (lane < rank) == (h == 0)
            both = jnp.where(own, low_wide, turned)
            spread = []
            for k in range(here // 2):
                holder = jnp.where(lane < rank, 2 * k, 2 * k + 1)
                spread.append(jnp.where(mine == holder, both, 0.0).astype(jnp.bfloat16))
            acc = jnp.dot(
                jnp.concatenate(spread, axis=1), weight, preferred_element_type=jnp.float32
            )
            out_ref[h * half : (h + 1) * half, :] = (adapter_output_scale * acc).astype(
                jnp.bfloat16
            )

    return pl.pallas_call(
        kernel,
        out_shape=jax.ShapeDtypeStruct((2 * half, cols), jnp.bfloat16),
        compiler_params=GRANT,
        name="full_up",
    )(low, up)


def full_take(at_col, back, base):
    rows, cols = base.shape
    slots = back.shape[0]

    def kernel(at_ref, back_ref, base_ref, out_ref):
        slot = lax.broadcasted_iota(jnp.int32, (rows, slots), 1)
        pick = jnp.where(slot == at_ref[...], 1.0, 0.0).astype(jnp.bfloat16)
        mine = jnp.dot(pick, back_ref[...], preferred_element_type=jnp.float32)
        out_ref[...] = (base_ref[...] + mine).astype(jnp.bfloat16)

    return pl.pallas_call(
        kernel,
        out_shape=jax.ShapeDtypeStruct((rows, cols), jnp.bfloat16),
        compiler_params=GRANT,
        name="full_take",
    )(at_col, back, base)


def scalar_spec():
    return pl.BlockSpec(memory_space=pltpu.SMEM)


def count_before(row, col):
    n = row.shape[1]
    j = lax.broadcasted_iota(jnp.int32, (n, n), 0)
    i = lax.broadcasted_iota(jnp.int32, (n, n), 1)
    return jnp.sum(jnp.where((row == col) & (j < i), 1, 0), axis=0, keepdims=True)


def to_col(row):
    return jnp.broadcast_to(row, (128, row.shape[1])).T[:, :1]


def pick_rows(at_row, slots, first=0):
    n = at_row.shape[1]
    slot = lax.broadcasted_iota(jnp.int32, (slots, n), 0) + first
    return jnp.where(slot == at_row, 1.0, 0.0).astype(jnp.bfloat16)


def place_main(ids_row, seen, tokens, slots):
    rows, width = tokens.shape
    tile = 256

    def kernel(row_ref, seen_ref, tok_ref, out_ref):
        at_row = jnp.where(seen_ref[...] < MAIN, row_ref[...] * MAIN + seen_ref[...], -1)
        pick = pick_rows(at_row, tile, pl.program_id(0) * tile)
        out_ref[...] = jnp.dot(pick, tok_ref[...], preferred_element_type=jnp.float32).astype(
            jnp.bfloat16
        )

    return pl.pallas_call(
        kernel,
        grid=(slots // tile,),
        in_specs=[
            pl.BlockSpec((1, rows), lambda i: (0, 0)),
            pl.BlockSpec((1, rows), lambda i: (0, 0)),
            pl.BlockSpec((rows, width), lambda i: (0, 0)),
        ],
        out_specs=pl.BlockSpec((tile, width), lambda i: (i, 0)),
        out_shape=jax.ShapeDtypeStruct((slots, width), tokens.dtype),
        compiler_params=GRANT,
        name="place_main",
    )(ids_row, seen, tokens)


def bucket(rows_of, key, key_col, code, valid, flag, store):
    n = key.shape[1]
    width = rows_of.shape[1]
    q = count_before(key, key_col)
    fits = valid & (q < SIDE - 1)
    lost = jnp.max(jnp.where(valid & (q >= SIDE - 1), 1.0, 0.0), axis=1, keepdims=True)
    flag = jnp.maximum(flag, lost)
    pick = pick_rows(jnp.where(fits, key * SIDE + q, -1), 8 * SIDE)
    data = jnp.dot(pick, rows_of, preferred_element_type=jnp.float32)
    which = lax.broadcasted_iota(jnp.int32, (8, n), 0)
    owned = jnp.where(fits & (which == key), (code + 1).astype(jnp.float32), 0.0)
    place = lax.broadcasted_iota(jnp.int32, (128, n), 0)
    there = jnp.where(place == q, 1.0, 0.0)
    codes = lax.dot_general(
        owned.astype(jnp.bfloat16),
        there.astype(jnp.bfloat16),
        (((1,), (1,)), ((), ())),
        preferred_element_type=jnp.float32,
    )
    lane = lax.broadcasted_iota(jnp.int32, (8, 128), 1)
    codes = jnp.where(lane == 127, flag, codes)
    wide = jnp.concatenate([codes, jnp.zeros((8, width - 128), jnp.float32)], axis=1)
    row = lax.broadcasted_iota(jnp.int32, (SIDE, width), 0)
    for k in range(8):
        note = jnp.broadcast_to(wide[k : k + 1], (SIDE, width))
        block = jnp.where(row == SIDE - 1, note, data[k * SIDE : (k + 1) * SIDE])
        store(k, block.astype(jnp.bfloat16))


def read_codes(blocks):
    n = 8 * SIDE
    lane = lax.broadcasted_iota(jnp.int32, (8, n), 1)
    codes = jnp.zeros((8, n), jnp.float32)
    flag = jnp.zeros((1, 1), jnp.float32)
    for k in range(8):
        note = blocks[k].astype(jnp.float32)[SIDE - 1 : SIDE, :n]
        flag = jnp.maximum(flag, note[:, 127:128])
        own = jnp.where(lane < SIDE - 1, jnp.broadcast_to(note, (8, n)), 0.0)
        codes = codes + (pltpu.roll(own, k * SIDE, 1) if k else own)
    return codes[:1].astype(jnp.int32) - 1, flag


def side_first(ids_row, tokens):
    rows, width = tokens.shape

    def kernel(row_ref, tok_ref, out_ref, seen_ref, at_col_ref):
        row = row_ref[...]
        seen = count_before(row, to_col(row))
        seen_ref[...] = seen
        home = row // HERE
        spot = row % HERE
        back = home * (HERE * MOST) + jnp.where(
            seen < MAIN, spot * MAIN + seen, HERE * MAIN + spot
        )
        at_col_ref[...] = to_col(back)
        third = seen >= MAIN
        key = home % 8

        def store(k, block):
            out_ref[k * SIDE : (k + 1) * SIDE, :] = block

        bucket(
            tok_ref[...], key, to_col(jnp.where(third, key, -1)), home // 8 * 8 + spot, third,
            jnp.zeros((1, 1), jnp.float32), store,
        )

    return pl.pallas_call(
        kernel,
        out_shape=[
            jax.ShapeDtypeStruct((8 * SIDE, width), jnp.bfloat16),
            jax.ShapeDtypeStruct((1, rows), jnp.int32),
            jax.ShapeDtypeStruct((rows, 1), jnp.int32),
        ],
        compiler_params=GRANT,
        name="side_first",
    )(ids_row, tokens)


def side_second(at, arrived):
    n, width = arrived.shape

    def kernel(at_ref, in_ref, *refs):
        out_refs, block_ref = refs[:8], refs[8]
        blocks = [in_ref[k * SIDE : (k + 1) * SIDE, :] for k in range(8)]
        code, flag = read_codes(blocks)
        valid = code >= 0
        key = jnp.where(valid, code // 8, -1)
        from_y = lax.broadcasted_iota(jnp.int32, (1, n), 1) // SIDE

        def store(k, block):
            block_ref[k] = block

        bucket(in_ref[...], key, to_col(key), from_y * 8 + code % 8, valid, flag, store)
        for k in range(8):
            out_refs[k][...] = block_ref[at_ref[0] ^ k]

    return pl.pallas_call(
        kernel,
        in_specs=[scalar_spec(), pl.BlockSpec(memory_space=pltpu.VMEM)],
        out_shape=[jax.ShapeDtypeStruct((SIDE, width), jnp.bfloat16)] * 8,
        scratch_shapes=[pltpu.VMEM((8, SIDE, width), jnp.bfloat16)],
        compiler_params=GRANT,
        name="side_second",
    )(at, arrived)


def fold(full, mine, rank):
    pair = 2 * rank
    lane = lax.broadcasted_iota(jnp.int32, (full.shape[0], pair), 1)
    kept = jnp.zeros((full.shape[0], pair), jnp.float32)
    for k in range(HERE // 2):
        holder = jnp.where(lane < rank, 2 * k, 2 * k + 1)
        kept = kept + jnp.where(mine == holder, full[:, k * pair : (k + 1) * pair], 0.0)
    return kept + pltpu.roll(kept, rank, 1)


def contract_last(x, y):
    return lax.dot_general(x, y, (((1,), (1,)), ((), ())), preferred_element_type=jnp.float32)


def down_main(arrived, down):
    slots, width = arrived.shape
    here, rank, _ = down.shape
    half = slots // 2
    tile = 256
    pair = 2 * rank

    def kernel(in_ref, down_ref, out_ref):
        weight = down_ref[...].reshape(here * rank, width)
        lane = lax.broadcasted_iota(jnp.int32, (tile, pair), 1)
        slot = lax.broadcasted_iota(jnp.int32, (tile, pair), 0)
        mine = slot % (HERE * MAIN) // MAIN
        for first in range(0, half, tile):
            lo = fold(contract_last(in_ref[first : first + tile, :], weight), mine, rank)
            hi = fold(
                contract_last(in_ref[half + first : half + first + tile, :], weight), mine, rank
            )
            out_ref[first : first + tile, :] = jnp.where(lane < rank, lo, hi).astype(jnp.bfloat16)

    return pl.pallas_call(
        kernel,
        out_shape=jax.ShapeDtypeStruct((half, pair), jnp.bfloat16),
        compiler_params=GRANT,
        name="down_main",
    )(arrived, down)


def side_low(at, blocks, down, main):
    here, rank, width = down.shape
    n = 8 * SIDE
    pair = 2 * rank
    share = (main.shape[0] + n // 2) // 2

    def kernel(at_ref, *refs):
        down_ref, main_ref, own_ref, other_ref, slot_ref, flag_ref, all_ref = refs[8:]
        blocks = [ref[...] for ref in refs[:8]]
        code, flag = read_codes(blocks)
        from_z = (lax.broadcasted_iota(jnp.int32, (1, n), 1) // SIDE) ^ at_ref[0]
        slot_ref[...] = jnp.where(code >= 0, from_z * 64 + code, -1)
        flag_ref[...] = jnp.broadcast_to(flag, (8, 128))
        rows_of = jnp.concatenate(blocks, axis=0)
        full = contract_last(rows_of, down_ref[...].reshape(here * rank, width))
        low = fold(full, to_col(jnp.where(code >= 0, code % HERE, -1)), rank)
        lane = lax.broadcasted_iota(jnp.int32, (n // 2, pair), 1)
        packed = jnp.where(lane < rank, low[: n // 2], low[n // 2 :]).astype(jnp.bfloat16)
        rows = jnp.concatenate([main_ref[...], packed], axis=0)
        for k in range(2):
            all_ref[k] = rows[k * share : (k + 1) * share]
        own_ref[...] = all_ref[at_ref[1]]
        other_ref[...] = all_ref[1 - at_ref[1]]

    return pl.pallas_call(
        kernel,
        in_specs=[scalar_spec()] + [pl.BlockSpec(memory_space=pltpu.VMEM)] * 10,
        out_shape=[
            jax.ShapeDtypeStruct((share, pair), jnp.bfloat16),
            jax.ShapeDtypeStruct((share, pair), jnp.bfloat16),
            jax.ShapeDtypeStruct((1, n), jnp.int32),
            jax.ShapeDtypeStruct((8, 128), jnp.float32),
        ],
        scratch_shapes=[pltpu.VMEM((2, share, pair), jnp.bfloat16)],
        compiler_params=GRANT,
        name="side_low",
    )(at, *blocks, down, main)


def chip_sum(parts):
    def kernel(in_ref, out_ref):
        total = in_ref[0].astype(jnp.float32)
        for k in range(1, parts.shape[0]):
            total = total + in_ref[k].astype(jnp.float32)
        out_ref[...] = total.astype(jnp.bfloat16)

    return pl.pallas_call(
        kernel,
        out_shape=jax.ShapeDtypeStruct(parts.shape[1:], jnp.bfloat16),
        compiler_params=GRANT,
        name="chip_sum",
    )(parts)


def up_main(low, slot, flag, up):
    here, rank, cols = up.shape
    pair = 2 * rank
    n = slot.shape[1]
    half = low.shape[0] - n // 2
    owners = 2 * half // (here * MAIN)

    def kernel(low_ref, slot_ref, flag_ref, up_ref, out_ref):
        weight = up_ref[...].reshape(here * rank, cols)

        def mapped(part, holders):
            wide = part.astype(jnp.float32)
            turned = pltpu.roll(wide, rank, 1)
            lane = lax.broadcasted_iota(jnp.int32, wide.shape, 1)
            halves = []
            for h, mine in enumerate(holders):
                both = jnp.where((lane < rank) == (h == 0), wide, turned)
                spread = []
                for k in range(here // 2):
                    holder = jnp.where(lane < rank, 2 * k, 2 * k + 1)
                    spread.append(jnp.where(mine == holder, both, 0.0).astype(jnp.bfloat16))
                halves.append(
                    jnp.dot(
                        jnp.concatenate(spread, axis=1), weight, preferred_element_type=jnp.float32
                    )
                )
            return jnp.concatenate(halves, axis=0) * adapter_output_scale

        main_slot = lax.broadcasted_iota(jnp.int32, (half, pair), 0)
        spot = main_slot % (here * MAIN) // MAIN
        main = mapped(low_ref[:half, :], (spot, spot)).reshape(owners, here * MAIN, cols)
        at = slot_ref[...]
        spot = to_col(jnp.where(at >= 0, at % here, -1))
        thirds = mapped(low_ref[half:, :], (spot[: n // 2], spot[n // 2 :]))
        thirds = jnp.dot(
            pick_rows(at, owners * here),
            thirds.astype(jnp.bfloat16),
            preferred_element_type=jnp.float32,
        ).reshape(owners, here, cols)
        both = jnp.concatenate([main, thirds], axis=1).reshape(owners * here * MOST, cols)
        out_ref[...] = jnp.where(flag_ref[:1, :1] > 0.0, LOST, both).astype(jnp.bfloat16)

    return pl.pallas_call(
        kernel,
        out_shape=jax.ShapeDtypeStruct((owners * here * MOST, cols), jnp.bfloat16),
        compiler_params=GRANT,
        name="up_main",
    )(low, slot, flag, up)


def take_main(at_col, back, base):
    rows, cols = base.shape
    slots = back.shape[0]

    def kernel(at_ref, back_ref, base_ref, out_ref, lost_ref):
        slot = lax.broadcasted_iota(jnp.int32, (rows, slots), 1)
        pick = jnp.where(slot == at_ref[...], 1.0, 0.0).astype(jnp.bfloat16)
        mine = jnp.dot(pick, back_ref[...], preferred_element_type=jnp.float32)
        out_ref[...] = (base_ref[...] + mine).astype(jnp.bfloat16)
        lost_ref[0] = (jnp.max(back_ref[...].astype(jnp.float32)) > LOST / 2).astype(jnp.int32)

    return pl.pallas_call(
        kernel,
        out_specs=[pl.BlockSpec(memory_space=pltpu.VMEM), pl.BlockSpec(memory_space=pltpu.SMEM)],
        out_shape=[
            jax.ShapeDtypeStruct((rows, cols), jnp.bfloat16),
            jax.ShapeDtypeStruct((1,), jnp.int32),
        ],
        compiler_params=GRANT,
        name="take_main",
    )(at_col, back, base)


def low_of_all(low_part, groups):
    rows, pair = low_part.shape
    parts = swap(low_part.reshape(groups, rows // groups, pair), TENSOR)
    share = parts.astype(jnp.float32).sum(axis=0).astype(jnp.bfloat16)
    copies = jnp.broadcast_to(share[None], (groups, *share.shape))
    return swap(copies, TENSOR).reshape(rows, pair)


def low_of_pairs(own, other):
    rounded = own.astype(jnp.float32)
    rounded = rounded + lax.ppermute(other, TENSOR[1], [(0, 1), (1, 0)]).astype(jnp.float32)
    chips = lax.axis_size(TENSOR[0])
    copies = jnp.broadcast_to(rounded.astype(jnp.bfloat16)[None], (chips, *own.shape))
    total = chip_sum(swap(copies, TENSOR[0]))
    return lax.all_gather(total, TENSOR[1], axis=0, tiled=True)


def whole_exchange(tokens, adapter_down, adapter_up_weight, adapter_ids, base):
    rows, width = tokens.shape
    cols = adapter_up_weight.shape[2]
    share = HERE * MOST
    slots = 64 * share
    placed, at_col = full_place(adapter_ids.reshape(1, rows), tokens, slots)
    arrived = swap(placed.reshape(64, share, width), ADAPTER).reshape(slots, width)
    low = low_of_all(full_down(arrived, adapter_down), lax.axis_size(TENSOR))
    delta = full_up(low, adapter_up_weight)
    back = swap(delta.reshape(64, share, cols), ADAPTER).reshape(slots, cols)
    return full_take(at_col, back, base)


def layer(tokens, value_weight, adapter_down, adapter_up_weight, adapter_ids):
    groups = lax.axis_size(TENSOR)
    rows, width = tokens.shape
    cols = adapter_up_weight.shape[2]
    ids_row = adapter_ids.reshape(1, rows)
    at_z = lax.axis_index("z").astype(jnp.int32)

    blocks, seen, at_col = side_first(ids_row, tokens)
    blocks = swap(blocks.reshape(8, SIDE, width), "y").reshape(8 * SIDE, width)
    placed = place_main(ids_row, seen, tokens, 64 * HERE * MAIN)
    arrived = swap(placed.reshape(64, HERE * MAIN, width), ADAPTER)
    arrived = arrived.reshape(64 * HERE * MAIN, width)

    blocks = side_second(at_z.reshape(1), blocks)
    blocks = xor_sends(blocks, "z")
    at = lax.axis_index(TENSOR).astype(jnp.int32).reshape(1)
    own, other = value_pieces(tokens, value_weight, at, groups)
    other = lax.ppermute(other, TENSOR[1], [(0, 1), (1, 0)])
    pairs = pair_sum(own, other)
    pairs = xor_sends([own, *pairs], TENSOR[0])[1:]
    base = base_sum(own, other, pairs)

    main = down_main(arrived, adapter_down)
    core = lax.axis_index(TENSOR[1]).astype(jnp.int32)
    own, other, slot, flag = side_low(jnp.stack([at_z, core]), blocks, adapter_down, main)
    low = low_of_pairs(own, other)
    delta = up_main(low, slot, flag, adapter_up_weight)
    back = swap(delta.reshape(64, HERE * MOST, cols), ADAPTER).reshape(64 * HERE * MOST, cols)
    back, *whole = lax.optimization_barrier(
        (back, tokens, adapter_down, adapter_up_weight, adapter_ids, base)
    )
    values, lost = take_main(at_col, back, base)
    return lax.cond(
        lost[0] > 0,
        lambda: whole_exchange(*whole),
        lambda: values,
    )


def xor_sends(pieces, axis):
    size = lax.axis_size(axis)
    parts = [pieces[0]]
    for k in range(1, size):
        parts.append(lax.ppermute(pieces[k], axis, [(i, i ^ k) for i in range(size)]))
    return parts


def solution(mesh):
    torus = Mesh(mesh.devices.reshape(8, 8, 4, 2), (*ADAPTER, *TENSOR))
    return jax.shard_map(
        layer,
        mesh=torus,
        in_specs=(
            P(ADAPTER, TENSOR),
            P(TENSOR, None),
            P(ADAPTER, None, TENSOR),
            P(ADAPTER, None, TENSOR),
            P(ADAPTER, None),
        ),
        out_specs=P(ADAPTER, TENSOR),
        check_vma=False,
    )
```

```python
import jax
import jax.numpy as jnp
from jax import lax
from jax.experimental import pallas as pl
from jax.experimental.pallas import tpu as pltpu
from jax.sharding import Mesh
from jax.sharding import PartitionSpec as P


TENSOR = ("tensor_0", "tensor_1")
ADAPTER = ("z", "y")
HERE = 8
MOST = 3
MAIN = 2
SIDE = 16
LOST = 3e38
GRANT = pltpu.CompilerParams(vmem_limit_bytes=16 * 2**20)

adapter_output_scale = 2.0


def swap(x, axes):
    return lax.all_to_all(x, axes, split_axis=0, concat_axis=0, tiled=True)


def full_place(ids_row, tokens, slots):
    rows, width = tokens.shape
    tile = 256

    def kernel(row_ref, tok_ref, out_ref, at_col_ref, at_row_ref):
        @pl.when(pl.program_id(0) == 0)
        def _():
            row = row_ref[...]
            col = jnp.broadcast_to(row, (128, rows)).T[:, :1]
            same = row == col
            i = lax.broadcasted_iota(jnp.int32, (rows, rows), 0)
            j = lax.broadcasted_iota(jnp.int32, (rows, rows), 1)
            before_row = jnp.sum(jnp.where(same & (i < j), 1, 0), axis=0, keepdims=True)
            before_col = jnp.sum(jnp.where(same & (j < i), 1, 0), axis=1, keepdims=True)
            at_row_ref[...] = row * MOST + before_row
            at_col_ref[...] = col * MOST + before_col

        first = pl.program_id(0) * tile
        slot = lax.broadcasted_iota(jnp.int32, (tile, rows), 0) + first
        pick = jnp.where(slot == at_row_ref[...], 1.0, 0.0).astype(jnp.bfloat16)
        out_ref[...] = jnp.dot(pick, tok_ref[...], preferred_element_type=jnp.float32).astype(
            jnp.bfloat16
        )

    return pl.pallas_call(
        kernel,
        grid=(slots // tile,),
        in_specs=[
            pl.BlockSpec((1, rows), lambda i: (0, 0)),
            pl.BlockSpec((rows, width), lambda i: (0, 0)),
        ],
        out_specs=[
            pl.BlockSpec((tile, width), lambda i: (i, 0)),
            pl.BlockSpec((rows, 1), lambda i: (0, 0)),
        ],
        out_shape=[
            jax.ShapeDtypeStruct((slots, width), tokens.dtype),
            jax.ShapeDtypeStruct((rows, 1), jnp.int32),
        ],
        scratch_shapes=[pltpu.VMEM((1, rows), jnp.int32)],
        compiler_params=GRANT,
        name="full_place",
    )(ids_row, tokens)


def value_pieces(tokens, weight, at, pieces):
    rows, width = tokens.shape
    cols = weight.shape[1] // pieces
    step = 2

    def kernel(at_ref, tok_ref, w_ref, own_ref, other_ref, part_ref):
        for first in range(0, pieces, step):
            part = jnp.dot(
                tok_ref[...],
                w_ref[:, first * cols : (first + step) * cols],
                preferred_element_type=jnp.float32,
            ).astype(jnp.bfloat16)
            for k in range(step):
                part_ref[first + k] = part[:, k * cols : (k + 1) * cols]
        for k in range(pieces // 2):
            own_ref[k] = part_ref[at_ref[0] ^ (2 * k)]
            other_ref[k] = part_ref[at_ref[0] ^ (2 * k + 1)]

    return pl.pallas_call(
        kernel,
        in_specs=[
            pl.BlockSpec(memory_space=pltpu.SMEM),
            pl.BlockSpec((rows, width), lambda: (0, 0)),
            pl.BlockSpec(weight.shape, lambda: (0, 0)),
        ],
        out_shape=[jax.ShapeDtypeStruct((pieces // 2, rows, cols), jnp.bfloat16)] * 2,
        scratch_shapes=[pltpu.VMEM((pieces, rows, cols), jnp.bfloat16)],
        compiler_params=GRANT,
        name="value_pieces",
    )(at, tokens, weight)


def pair_sum(own, other):
    count, rows, cols = own.shape

    def kernel(own_ref, other_ref, *out_refs):
        for k in range(1, count):
            total = own_ref[k].astype(jnp.float32) + other_ref[k].astype(jnp.float32)
            out_refs[k - 1][...] = total.astype(jnp.bfloat16)

    return pl.pallas_call(
        kernel,
        out_shape=[jax.ShapeDtypeStruct((rows, cols), jnp.bfloat16)] * (count - 1),
        compiler_params=GRANT,
        name="pair_sum",
    )(own, other)


def base_sum(own, other, parts):
    def kernel(own_ref, other_ref, *refs):
        total = own_ref[0].astype(jnp.float32) + other_ref[0].astype(jnp.float32)
        for ref in refs[:-1]:
            total = total + ref[...].astype(jnp.float32)
        refs[-1][...] = total

    return pl.pallas_call(
        kernel,
        out_shape=jax.ShapeDtypeStruct(parts[0].shape, jnp.float32),
        compiler_params=GRANT,
        name="base_sum",
    )(own, other, *parts)


def adapter_of(shape, first, group):
    slot = lax.broadcasted_iota(jnp.int32, shape, 0) + first
    return slot % group // MOST


def full_down(arrived, down):
    slots, width = arrived.shape
    here, rank, _ = down.shape
    group = here * MOST
    half = slots // 2
    tile = 192
    pair = 2 * rank

    def kernel(lo_ref, hi_ref, down_ref, out_ref):
        weight = down_ref[...].reshape(here * rank, width)
        lane = lax.broadcasted_iota(jnp.int32, (tile, pair), 1)

        def rows_of(ref):
            full = lax.dot_general(
                ref[...], weight, (((1,), (1,)), ((), ())), preferred_element_type=jnp.float32
            )
            mine = adapter_of((tile, pair), 0, group)
            kept = jnp.zeros((tile, pair), jnp.float32)
            for k in range(here // 2):
                holder = jnp.where(lane < rank, 2 * k, 2 * k + 1)
                kept = kept + jnp.where(mine == holder, full[:, k * pair : (k + 1) * pair], 0.0)
            return kept + pltpu.roll(kept, rank, 1)

        out_ref[...] = jnp.where(lane < rank, rows_of(lo_ref), rows_of(hi_ref)).astype(
            jnp.bfloat16
        )

    steps = half // tile
    return pl.pallas_call(
        kernel,
        grid=(steps,),
        in_specs=[
            pl.BlockSpec((tile, width), lambda i: (i, 0)),
            pl.BlockSpec((tile, width), lambda i: (i + steps, 0)),
            pl.BlockSpec((here, rank, width), lambda i: (0, 0, 0)),
        ],
        out_specs=pl.BlockSpec((tile, pair), lambda i: (i, 0)),
        out_shape=jax.ShapeDtypeStruct((half, pair), jnp.bfloat16),
        compiler_params=GRANT,
        name="full_down",
    )(arrived, arrived, down)


def full_up(low, up):
    half, pair = low.shape
    here, rank, cols = up.shape
    group = here * MOST

    def kernel(low_ref, up_ref, out_ref):
        weight = up_ref[...].reshape(here * rank, cols)
        low_wide = low_ref[...].astype(jnp.float32)
        turned = pltpu.roll(low_wide, rank, 1)
        lane = lax.broadcasted_iota(jnp.int32, (half, pair), 1)
        mine = adapter_of((half, pair), 0, group)
        for h in range(2):
            own = (lane < rank) == (h == 0)
            both = jnp.where(own, low_wide, turned)
            spread = []
            for k in range(here // 2):
                holder = jnp.where(lane < rank, 2 * k, 2 * k + 1)
                spread.append(jnp.where(mine == holder, both, 0.0).astype(jnp.bfloat16))
            acc = jnp.dot(
                jnp.concatenate(spread, axis=1), weight, preferred_element_type=jnp.float32
            )
            out_ref[h * half : (h + 1) * half, :] = (adapter_output_scale * acc).astype(
                jnp.bfloat16
            )

    return pl.pallas_call(
        kernel,
        out_shape=jax.ShapeDtypeStruct((2 * half, cols), jnp.bfloat16),
        compiler_params=GRANT,
        name="full_up",
    )(low, up)


def full_take(at_col, back, base):
    rows, cols = base.shape
    slots = back.shape[0]

    def kernel(at_ref, back_ref, base_ref, out_ref):
        slot = lax.broadcasted_iota(jnp.int32, (rows, slots), 1)
        pick = jnp.where(slot == at_ref[...], 1.0, 0.0).astype(jnp.bfloat16)
        mine = jnp.dot(pick, back_ref[...], preferred_element_type=jnp.float32)
        out_ref[...] = (base_ref[...] + mine).astype(jnp.bfloat16)

    return pl.pallas_call(
        kernel,
        out_shape=jax.ShapeDtypeStruct((rows, cols), jnp.bfloat16),
        compiler_params=GRANT,
        name="full_take",
    )(at_col, back, base)


def scalar_spec():
    return pl.BlockSpec(memory_space=pltpu.SMEM)


def count_before(row, col):
    n = row.shape[1]
    j = lax.broadcasted_iota(jnp.int32, (n, n), 0)
    i = lax.broadcasted_iota(jnp.int32, (n, n), 1)
    return jnp.sum(jnp.where((row == col) & (j < i), 1, 0), axis=0, keepdims=True)


def to_col(row):
    return jnp.broadcast_to(row, (128, row.shape[1])).T[:, :1]


def pick_rows(at_row, slots, first=0):
    n = at_row.shape[1]
    slot = lax.broadcasted_iota(jnp.int32, (slots, n), 0) + first
    return jnp.where(slot == at_row, 1.0, 0.0).astype(jnp.bfloat16)


def place_main(ids_row, seen, tokens, slots):
    rows, width = tokens.shape
    tile = 256

    def kernel(row_ref, seen_ref, tok_ref, out_ref):
        at_row = jnp.where(seen_ref[...] < MAIN, row_ref[...] * MAIN + seen_ref[...], -1)
        pick = pick_rows(at_row, tile, pl.program_id(0) * tile)
        out_ref[...] = jnp.dot(pick, tok_ref[...], preferred_element_type=jnp.float32).astype(
            jnp.bfloat16
        )

    return pl.pallas_call(
        kernel,
        grid=(slots // tile,),
        in_specs=[
            pl.BlockSpec((1, rows), lambda i: (0, 0)),
            pl.BlockSpec((1, rows), lambda i: (0, 0)),
            pl.BlockSpec((rows, width), lambda i: (0, 0)),
        ],
        out_specs=pl.BlockSpec((tile, width), lambda i: (i, 0)),
        out_shape=jax.ShapeDtypeStruct((slots, width), tokens.dtype),
        compiler_params=GRANT,
        name="place_main",
    )(ids_row, seen, tokens)


def bucket(rows_of, key, key_col, code, valid, flag, store):
    n = key.shape[1]
    width = rows_of.shape[1]
    q = count_before(key, key_col)
    fits = valid & (q < SIDE - 1)
    lost = jnp.max(jnp.where(valid & (q >= SIDE - 1), 1.0, 0.0), axis=1, keepdims=True)
    flag = jnp.maximum(flag, lost)
    pick = pick_rows(jnp.where(fits, key * SIDE + q, -1), 8 * SIDE)
    data = jnp.dot(pick, rows_of, preferred_element_type=jnp.float32)
    which = lax.broadcasted_iota(jnp.int32, (8, n), 0)
    owned = jnp.where(fits & (which == key), (code + 1).astype(jnp.float32), 0.0)
    place = lax.broadcasted_iota(jnp.int32, (128, n), 0)
    there = jnp.where(place == q, 1.0, 0.0)
    codes = lax.dot_general(
        owned.astype(jnp.bfloat16),
        there.astype(jnp.bfloat16),
        (((1,), (1,)), ((), ())),
        preferred_element_type=jnp.float32,
    )
    lane = lax.broadcasted_iota(jnp.int32, (8, 128), 1)
    codes = jnp.where(lane == 127, flag, codes)
    wide = jnp.concatenate([codes, jnp.zeros((8, width - 128), jnp.float32)], axis=1)
    row = lax.broadcasted_iota(jnp.int32, (SIDE, width), 0)
    for k in range(8):
        note = jnp.broadcast_to(wide[k : k + 1], (SIDE, width))
        block = jnp.where(row == SIDE - 1, note, data[k * SIDE : (k + 1) * SIDE])
        store(k, block.astype(jnp.bfloat16))


def read_codes(blocks):
    n = 8 * SIDE
    lane = lax.broadcasted_iota(jnp.int32, (8, n), 1)
    codes = jnp.zeros((8, n), jnp.float32)
    flag = jnp.zeros((1, 1), jnp.float32)
    for k in range(8):
        note = blocks[k].astype(jnp.float32)[SIDE - 1 : SIDE, :n]
        flag = jnp.maximum(flag, note[:, 127:128])
        own = jnp.where(lane < SIDE - 1, jnp.broadcast_to(note, (8, n)), 0.0)
        codes = codes + (pltpu.roll(own, k * SIDE, 1) if k else own)
    return codes[:1].astype(jnp.int32) - 1, flag


def side_first(ids_row, tokens):
    rows, width = tokens.shape

    def kernel(row_ref, tok_ref, out_ref, seen_ref):
        row = row_ref[...]
        seen = count_before(row, to_col(row))
        seen_ref[...] = seen
        home = row // HERE
        spot = row % HERE
        third = seen >= MAIN
        key = home % 8

        def store(k, block):
            out_ref[k * SIDE : (k + 1) * SIDE, :] = block

        bucket(
            tok_ref[...], key, to_col(jnp.where(third, key, -1)), home // 8 * 8 + spot, third,
            jnp.zeros((1, 1), jnp.float32), store,
        )

    return pl.pallas_call(
        kernel,
        out_shape=[
            jax.ShapeDtypeStruct((8 * SIDE, width), jnp.bfloat16),
            jax.ShapeDtypeStruct((1, rows), jnp.int32),
        ],
        compiler_params=GRANT,
        name="side_first",
    )(ids_row, tokens)


def side_second(at, arrived):
    n, width = arrived.shape

    def kernel(at_ref, in_ref, *refs):
        out_refs, block_ref = refs[:8], refs[8]
        blocks = [in_ref[k * SIDE : (k + 1) * SIDE, :] for k in range(8)]
        code, flag = read_codes(blocks)
        valid = code >= 0
        key = jnp.where(valid, code // 8, -1)
        from_y = lax.broadcasted_iota(jnp.int32, (1, n), 1) // SIDE

        def store(k, block):
            block_ref[k] = block

        bucket(in_ref[...], key, to_col(key), from_y * 8 + code % 8, valid, flag, store)
        for k in range(8):
            out_refs[k][...] = block_ref[at_ref[0] ^ k]

    return pl.pallas_call(
        kernel,
        in_specs=[scalar_spec(), pl.BlockSpec(memory_space=pltpu.VMEM)],
        out_shape=[jax.ShapeDtypeStruct((SIDE, width), jnp.bfloat16)] * 8,
        scratch_shapes=[pltpu.VMEM((8, SIDE, width), jnp.bfloat16)],
        compiler_params=GRANT,
        name="side_second",
    )(at, arrived)


def fold(full, mine, rank):
    pair = 2 * rank
    lane = lax.broadcasted_iota(jnp.int32, (full.shape[0], pair), 1)
    kept = jnp.zeros((full.shape[0], pair), jnp.float32)
    for k in range(HERE // 2):
        holder = jnp.where(lane < rank, 2 * k, 2 * k + 1)
        kept = kept + jnp.where(mine == holder, full[:, k * pair : (k + 1) * pair], 0.0)
    return kept + pltpu.roll(kept, rank, 1)


def contract_last(x, y):
    return lax.dot_general(x, y, (((1,), (1,)), ((), ())), preferred_element_type=jnp.float32)


def down_main(arrived, down):
    slots, width = arrived.shape
    here, rank, _ = down.shape
    half = slots // 2
    tile = 256
    pair = 2 * rank

    def kernel(in_ref, down_ref, out_ref):
        weight = down_ref[...].reshape(here * rank, width)
        lane = lax.broadcasted_iota(jnp.int32, (tile, pair), 1)
        slot = lax.broadcasted_iota(jnp.int32, (tile, pair), 0)
        mine = slot % (HERE * MAIN) // MAIN
        for first in range(0, half, tile):
            lo = fold(contract_last(in_ref[first : first + tile, :], weight), mine, rank)
            hi = fold(
                contract_last(in_ref[half + first : half + first + tile, :], weight), mine, rank
            )
            out_ref[first : first + tile, :] = jnp.where(lane < rank, lo, hi).astype(jnp.bfloat16)

    return pl.pallas_call(
        kernel,
        out_shape=jax.ShapeDtypeStruct((half, pair), jnp.bfloat16),
        compiler_params=GRANT,
        name="down_main",
    )(arrived, down)


def side_low(at, blocks, down, main):
    here, rank, width = down.shape
    n = 8 * SIDE
    pair = 2 * rank
    share = (main.shape[0] + n // 2) // 2

    def kernel(at_ref, *refs):
        down_ref, main_ref, own_ref, other_ref, slot_ref, flag_ref, all_ref = refs[8:]
        blocks = [ref[...] for ref in refs[:8]]
        code, flag = read_codes(blocks)
        from_z = (lax.broadcasted_iota(jnp.int32, (1, n), 1) // SIDE) ^ at_ref[0]
        slot_ref[...] = jnp.where(code >= 0, from_z * 64 + code, -1)
        flag_ref[...] = jnp.broadcast_to(flag, (8, 128))
        rows_of = jnp.concatenate(blocks, axis=0)
        full = contract_last(rows_of, down_ref[...].reshape(here * rank, width))
        low = fold(full, to_col(jnp.where(code >= 0, code % HERE, -1)), rank)
        lane = lax.broadcasted_iota(jnp.int32, (n // 2, pair), 1)
        packed = jnp.where(lane < rank, low[: n // 2], low[n // 2 :]).astype(jnp.bfloat16)
        rows = jnp.concatenate([main_ref[...], packed], axis=0)
        for k in range(2):
            all_ref[k] = rows[k * share : (k + 1) * share]
        own_ref[...] = all_ref[at_ref[1]]
        other_ref[...] = all_ref[1 - at_ref[1]]

    return pl.pallas_call(
        kernel,
        in_specs=[scalar_spec()] + [pl.BlockSpec(memory_space=pltpu.VMEM)] * 10,
        out_shape=[
            jax.ShapeDtypeStruct((share, pair), jnp.bfloat16),
            jax.ShapeDtypeStruct((share, pair), jnp.bfloat16),
            jax.ShapeDtypeStruct((1, n), jnp.int32),
            jax.ShapeDtypeStruct((8, 128), jnp.float32),
        ],
        scratch_shapes=[pltpu.VMEM((2, share, pair), jnp.bfloat16)],
        compiler_params=GRANT,
        name="side_low",
    )(at, *blocks, down, main)


def chip_sum(parts):
    def kernel(in_ref, out_ref):
        total = in_ref[0].astype(jnp.float32)
        for k in range(1, parts.shape[0]):
            total = total + in_ref[k].astype(jnp.float32)
        out_ref[...] = total.astype(jnp.bfloat16)

    return pl.pallas_call(
        kernel,
        out_shape=jax.ShapeDtypeStruct(parts.shape[1:], jnp.bfloat16),
        compiler_params=GRANT,
        name="chip_sum",
    )(parts)


def up_main(low, slot, flag, up):
    here, rank, cols = up.shape
    pair = 2 * rank
    n = slot.shape[1]
    half = low.shape[0] - n // 2
    owners = 2 * half // (here * MAIN)

    def kernel(low_ref, slot_ref, flag_ref, up_ref, out_ref):
        weight = up_ref[...].reshape(here * rank, cols)

        def mapped(part, holders):
            wide = part.astype(jnp.float32)
            turned = pltpu.roll(wide, rank, 1)
            lane = lax.broadcasted_iota(jnp.int32, wide.shape, 1)
            halves = []
            for h, mine in enumerate(holders):
                both = jnp.where((lane < rank) == (h == 0), wide, turned)
                spread = []
                for k in range(here // 2):
                    holder = jnp.where(lane < rank, 2 * k, 2 * k + 1)
                    spread.append(jnp.where(mine == holder, both, 0.0).astype(jnp.bfloat16))
                halves.append(
                    jnp.dot(
                        jnp.concatenate(spread, axis=1), weight, preferred_element_type=jnp.float32
                    )
                )
            return jnp.concatenate(halves, axis=0) * adapter_output_scale

        main_slot = lax.broadcasted_iota(jnp.int32, (half, pair), 0)
        spot = main_slot % (here * MAIN) // MAIN
        main = mapped(low_ref[:half, :], (spot, spot)).reshape(owners, here * MAIN, cols)
        at = slot_ref[...]
        spot = to_col(jnp.where(at >= 0, at % here, -1))
        thirds = mapped(low_ref[half:, :], (spot[: n // 2], spot[n // 2 :]))
        thirds = jnp.dot(
            pick_rows(at, owners * here),
            thirds.astype(jnp.bfloat16),
            preferred_element_type=jnp.float32,
        ).reshape(owners, here, cols)
        both = jnp.concatenate([main, thirds], axis=1).reshape(owners * here * MOST, cols)
        out_ref[...] = jnp.where(flag_ref[:1, :1] > 0.0, LOST, both).astype(jnp.bfloat16)

    return pl.pallas_call(
        kernel,
        out_shape=jax.ShapeDtypeStruct((owners * here * MOST, cols), jnp.bfloat16),
        compiler_params=GRANT,
        name="up_main",
    )(low, slot, flag, up)


def pick_all(ids_row, seen, slots):
    rows = ids_row.shape[1]

    def kernel(row_ref, seen_ref, out_ref):
        row = row_ref[...]
        seen = seen_ref[...]
        spot = row % HERE
        back = row // HERE * (HERE * MOST) + jnp.where(
            seen < MAIN, spot * MAIN + seen, HERE * MAIN + spot
        )
        slot = lax.broadcasted_iota(jnp.int32, (rows, slots), 1)
        out_ref[...] = jnp.where(slot == to_col(back), 1.0, 0.0).astype(jnp.bfloat16)

    return pl.pallas_call(
        kernel,
        out_shape=jax.ShapeDtypeStruct((rows, slots), jnp.bfloat16),
        compiler_params=GRANT,
        name="pick_all",
    )(ids_row, seen)


def take_main(pick, back, base):
    rows, cols = base.shape

    def kernel(pick_ref, back_ref, base_ref, out_ref, lost_ref):
        mine = jnp.dot(pick_ref[...], back_ref[...], preferred_element_type=jnp.float32)
        out_ref[...] = (base_ref[...] + mine).astype(jnp.bfloat16)
        lost_ref[0] = (jnp.max(back_ref[...].astype(jnp.float32)) > LOST / 2).astype(jnp.int32)

    return pl.pallas_call(
        kernel,
        out_specs=[pl.BlockSpec(memory_space=pltpu.VMEM), pl.BlockSpec(memory_space=pltpu.SMEM)],
        out_shape=[
            jax.ShapeDtypeStruct((rows, cols), jnp.bfloat16),
            jax.ShapeDtypeStruct((1,), jnp.int32),
        ],
        compiler_params=GRANT,
        name="take_main",
    )(pick, back, base)


def low_of_all(low_part, groups):
    rows, pair = low_part.shape
    parts = swap(low_part.reshape(groups, rows // groups, pair), TENSOR)
    share = parts.astype(jnp.float32).sum(axis=0).astype(jnp.bfloat16)
    copies = jnp.broadcast_to(share[None], (groups, *share.shape))
    return swap(copies, TENSOR).reshape(rows, pair)


def low_of_pairs(own, other):
    rounded = own.astype(jnp.float32)
    rounded = rounded + lax.ppermute(other, TENSOR[1], [(0, 1), (1, 0)]).astype(jnp.float32)
    chips = lax.axis_size(TENSOR[0])
    copies = jnp.broadcast_to(rounded.astype(jnp.bfloat16)[None], (chips, *own.shape))
    total = chip_sum(swap(copies, TENSOR[0]))
    return lax.all_gather(total, TENSOR[1], axis=0, tiled=True)


def whole_exchange(tokens, adapter_down, adapter_up_weight, adapter_ids, base):
    rows, width = tokens.shape
    cols = adapter_up_weight.shape[2]
    share = HERE * MOST
    slots = 64 * share
    placed, at_col = full_place(adapter_ids.reshape(1, rows), tokens, slots)
    arrived = swap(placed.reshape(64, share, width), ADAPTER).reshape(slots, width)
    low = low_of_all(full_down(arrived, adapter_down), lax.axis_size(TENSOR))
    delta = full_up(low, adapter_up_weight)
    back = swap(delta.reshape(64, share, cols), ADAPTER).reshape(slots, cols)
    return full_take(at_col, back, base)


def layer(tokens, value_weight, adapter_down, adapter_up_weight, adapter_ids):
    groups = lax.axis_size(TENSOR)
    rows, width = tokens.shape
    cols = adapter_up_weight.shape[2]
    ids_row = adapter_ids.reshape(1, rows)
    at_z = lax.axis_index("z").astype(jnp.int32)

    blocks, seen = side_first(ids_row, tokens)
    blocks = swap(blocks.reshape(8, SIDE, width), "y").reshape(8 * SIDE, width)
    placed = place_main(ids_row, seen, tokens, 64 * HERE * MAIN)
    arrived = swap(placed.reshape(64, HERE * MAIN, width), ADAPTER)
    arrived = arrived.reshape(64 * HERE * MAIN, width)

    blocks = side_second(at_z.reshape(1), blocks)
    blocks = xor_sends(blocks, "z")
    at = lax.axis_index(TENSOR).astype(jnp.int32).reshape(1)
    own, other = value_pieces(tokens, value_weight, at, groups)
    other = lax.ppermute(other, TENSOR[1], [(0, 1), (1, 0)])
    pairs = pair_sum(own, other)
    pairs = xor_sends([own, *pairs], TENSOR[0])[1:]
    base = base_sum(own, other, pairs)

    main = down_main(arrived, adapter_down)
    core = lax.axis_index(TENSOR[1]).astype(jnp.int32)
    own, other, slot, flag = side_low(jnp.stack([at_z, core]), blocks, adapter_down, main)
    low = low_of_pairs(own, other)
    delta = up_main(low, slot, flag, adapter_up_weight)
    back = swap(delta.reshape(64, HERE * MOST, cols), ADAPTER)
    back = back.reshape(64 * HERE * MOST, cols)
    pick = pick_all(ids_row, seen, 64 * HERE * MOST)
    back, *whole = lax.optimization_barrier(
        (back, tokens, adapter_down, adapter_up_weight, adapter_ids, base)
    )
    values, lost = take_main(pick, back, base)
    return lax.cond(
        lost[0] > 0,
        lambda: whole_exchange(*whole),
        lambda: values,
    )


def xor_sends(pieces, axis):
    size = lax.axis_size(axis)
    parts = [pieces[0]]
    for k in range(1, size):
        parts.append(lax.ppermute(pieces[k], axis, [(i, i ^ k) for i in range(size)]))
    return parts


def solution(mesh):
    torus = Mesh(mesh.devices.reshape(8, 8, 4, 2), (*ADAPTER, *TENSOR))
    return jax.shard_map(
        layer,
        mesh=torus,
        in_specs=(
            P(ADAPTER, TENSOR),
            P(TENSOR, None),
            P(ADAPTER, None, TENSOR),
            P(ADAPTER, None, TENSOR),
            P(ADAPTER, None),
        ),
        out_specs=P(ADAPTER, TENSOR),
        check_vma=False,
    )
```

```python
import jax
import jax.numpy as jnp
from jax import lax
from jax.experimental import pallas as pl
from jax.experimental.pallas import tpu as pltpu
from jax.sharding import Mesh
from jax.sharding import PartitionSpec as P


TENSOR = ("tensor_0", "tensor_1")
ADAPTER = ("z", "y")
HERE = 8
MOST = 3
MAIN = 2
SIDE = 16
LOST = 3e38
GRANT = pltpu.CompilerParams(vmem_limit_bytes=16 * 2**20)

adapter_output_scale = 2.0


def swap(x, axes):
    return lax.all_to_all(x, axes, split_axis=0, concat_axis=0, tiled=True)


def full_place(ids_row, tokens, slots):
    rows, width = tokens.shape
    tile = 256

    def kernel(row_ref, tok_ref, out_ref, at_col_ref, at_row_ref):
        @pl.when(pl.program_id(0) == 0)
        def _():
            row = row_ref[...]
            col = jnp.broadcast_to(row, (128, rows)).T[:, :1]
            same = row == col
            i = lax.broadcasted_iota(jnp.int32, (rows, rows), 0)
            j = lax.broadcasted_iota(jnp.int32, (rows, rows), 1)
            before_row = jnp.sum(jnp.where(same & (i < j), 1, 0), axis=0, keepdims=True)
            before_col = jnp.sum(jnp.where(same & (j < i), 1, 0), axis=1, keepdims=True)
            at_row_ref[...] = row * MOST + before_row
            at_col_ref[...] = col * MOST + before_col

        first = pl.program_id(0) * tile
        slot = lax.broadcasted_iota(jnp.int32, (tile, rows), 0) + first
        pick = jnp.where(slot == at_row_ref[...], 1.0, 0.0).astype(jnp.bfloat16)
        out_ref[...] = jnp.dot(pick, tok_ref[...], preferred_element_type=jnp.float32).astype(
            jnp.bfloat16
        )

    return pl.pallas_call(
        kernel,
        grid=(slots // tile,),
        in_specs=[
            pl.BlockSpec((1, rows), lambda i: (0, 0)),
            pl.BlockSpec((rows, width), lambda i: (0, 0)),
        ],
        out_specs=[
            pl.BlockSpec((tile, width), lambda i: (i, 0)),
            pl.BlockSpec((rows, 1), lambda i: (0, 0)),
        ],
        out_shape=[
            jax.ShapeDtypeStruct((slots, width), tokens.dtype),
            jax.ShapeDtypeStruct((rows, 1), jnp.int32),
        ],
        scratch_shapes=[pltpu.VMEM((1, rows), jnp.int32)],
        compiler_params=GRANT,
        name="full_place",
    )(ids_row, tokens)


def value_pieces(tokens, weight, at, pieces):
    rows, width = tokens.shape
    cols = weight.shape[1] // pieces
    step = 2

    def kernel(at_ref, tok_ref, w_ref, own_ref, other_ref, part_ref):
        for first in range(0, pieces, step):
            part = jnp.dot(
                tok_ref[...],
                w_ref[:, first * cols : (first + step) * cols],
                preferred_element_type=jnp.float32,
            ).astype(jnp.bfloat16)
            for k in range(step):
                part_ref[first + k] = part[:, k * cols : (k + 1) * cols]
        for k in range(pieces // 2):
            own_ref[k] = part_ref[at_ref[0] ^ (2 * k)]
            other_ref[k] = part_ref[at_ref[0] ^ (2 * k + 1)]

    return pl.pallas_call(
        kernel,
        in_specs=[
            pl.BlockSpec(memory_space=pltpu.SMEM),
            pl.BlockSpec((rows, width), lambda: (0, 0)),
            pl.BlockSpec(weight.shape, lambda: (0, 0)),
        ],
        out_shape=[jax.ShapeDtypeStruct((pieces // 2, rows, cols), jnp.bfloat16)] * 2,
        scratch_shapes=[pltpu.VMEM((pieces, rows, cols), jnp.bfloat16)],
        compiler_params=GRANT,
        name="value_pieces",
    )(at, tokens, weight)


def pair_sum(own, other):
    count, rows, cols = own.shape

    def kernel(own_ref, other_ref, *out_refs):
        for k in range(1, count):
            total = own_ref[k].astype(jnp.float32) + other_ref[k].astype(jnp.float32)
            out_refs[k - 1][...] = total.astype(jnp.bfloat16)

    return pl.pallas_call(
        kernel,
        out_shape=[jax.ShapeDtypeStruct((rows, cols), jnp.bfloat16)] * (count - 1),
        compiler_params=GRANT,
        name="pair_sum",
    )(own, other)


def base_sum(own, other, parts):
    def kernel(own_ref, other_ref, *refs):
        total = own_ref[0].astype(jnp.float32) + other_ref[0].astype(jnp.float32)
        for ref in refs[:-1]:
            total = total + ref[...].astype(jnp.float32)
        refs[-1][...] = total

    return pl.pallas_call(
        kernel,
        out_shape=jax.ShapeDtypeStruct(parts[0].shape, jnp.float32),
        compiler_params=GRANT,
        name="base_sum",
    )(own, other, *parts)


def adapter_of(shape, first, group):
    slot = lax.broadcasted_iota(jnp.int32, shape, 0) + first
    return slot % group // MOST


def full_down(arrived, down):
    slots, width = arrived.shape
    here, rank, _ = down.shape
    group = here * MOST
    half = slots // 2
    tile = 192
    pair = 2 * rank

    def kernel(lo_ref, hi_ref, down_ref, out_ref):
        weight = down_ref[...].reshape(here * rank, width)
        lane = lax.broadcasted_iota(jnp.int32, (tile, pair), 1)

        def rows_of(ref):
            full = lax.dot_general(
                ref[...], weight, (((1,), (1,)), ((), ())), preferred_element_type=jnp.float32
            )
            mine = adapter_of((tile, pair), 0, group)
            kept = jnp.zeros((tile, pair), jnp.float32)
            for k in range(here // 2):
                holder = jnp.where(lane < rank, 2 * k, 2 * k + 1)
                kept = kept + jnp.where(mine == holder, full[:, k * pair : (k + 1) * pair], 0.0)
            return kept + pltpu.roll(kept, rank, 1)

        out_ref[...] = jnp.where(lane < rank, rows_of(lo_ref), rows_of(hi_ref)).astype(
            jnp.bfloat16
        )

    steps = half // tile
    return pl.pallas_call(
        kernel,
        grid=(steps,),
        in_specs=[
            pl.BlockSpec((tile, width), lambda i: (i, 0)),
            pl.BlockSpec((tile, width), lambda i: (i + steps, 0)),
            pl.BlockSpec((here, rank, width), lambda i: (0, 0, 0)),
        ],
        out_specs=pl.BlockSpec((tile, pair), lambda i: (i, 0)),
        out_shape=jax.ShapeDtypeStruct((half, pair), jnp.bfloat16),
        compiler_params=GRANT,
        name="full_down",
    )(arrived, arrived, down)


def full_up(low, up):
    half, pair = low.shape
    here, rank, cols = up.shape
    group = here * MOST

    def kernel(low_ref, up_ref, out_ref):
        weight = up_ref[...].reshape(here * rank, cols)
        low_wide = low_ref[...].astype(jnp.float32)
        turned = pltpu.roll(low_wide, rank, 1)
        lane = lax.broadcasted_iota(jnp.int32, (half, pair), 1)
        mine = adapter_of((half, pair), 0, group)
        for h in range(2):
            own = (lane < rank) == (h == 0)
            both = jnp.where(own, low_wide, turned)
            spread = []
            for k in range(here // 2):
                holder = jnp.where(lane < rank, 2 * k, 2 * k + 1)
                spread.append(jnp.where(mine == holder, both, 0.0).astype(jnp.bfloat16))
            acc = jnp.dot(
                jnp.concatenate(spread, axis=1), weight, preferred_element_type=jnp.float32
            )
            out_ref[h * half : (h + 1) * half, :] = (adapter_output_scale * acc).astype(
                jnp.bfloat16
            )

    return pl.pallas_call(
        kernel,
        out_shape=jax.ShapeDtypeStruct((2 * half, cols), jnp.bfloat16),
        compiler_params=GRANT,
        name="full_up",
    )(low, up)


def full_take(at_col, back, base):
    rows, cols = base.shape
    slots = back.shape[0]

    def kernel(at_ref, back_ref, base_ref, out_ref):
        slot = lax.broadcasted_iota(jnp.int32, (rows, slots), 1)
        pick = jnp.where(slot == at_ref[...], 1.0, 0.0).astype(jnp.bfloat16)
        mine = jnp.dot(pick, back_ref[...], preferred_element_type=jnp.float32)
        out_ref[...] = (base_ref[...] + mine).astype(jnp.bfloat16)

    return pl.pallas_call(
        kernel,
        out_shape=jax.ShapeDtypeStruct((rows, cols), jnp.bfloat16),
        compiler_params=GRANT,
        name="full_take",
    )(at_col, back, base)


def scalar_spec():
    return pl.BlockSpec(memory_space=pltpu.SMEM)


def count_before(row, col):
    n = row.shape[1]
    j = lax.broadcasted_iota(jnp.int32, (n, n), 0)
    i = lax.broadcasted_iota(jnp.int32, (n, n), 1)
    return jnp.sum(jnp.where((row == col) & (j < i), 1, 0), axis=0, keepdims=True)


def to_col(row):
    return jnp.broadcast_to(row, (128, row.shape[1])).T[:, :1]


def pick_rows(at_row, slots, first=0):
    n = at_row.shape[1]
    slot = lax.broadcasted_iota(jnp.int32, (slots, n), 0) + first
    return jnp.where(slot == at_row, 1.0, 0.0).astype(jnp.bfloat16)


def place_main(ids_row, seen, tokens, slots):
    rows, width = tokens.shape
    tile = 256

    def kernel(row_ref, seen_ref, tok_ref, out_ref):
        at_row = jnp.where(seen_ref[...] < MAIN, row_ref[...] * MAIN + seen_ref[...], -1)
        pick = pick_rows(at_row, tile, pl.program_id(0) * tile)
        out_ref[...] = jnp.dot(pick, tok_ref[...], preferred_element_type=jnp.float32).astype(
            jnp.bfloat16
        )

    return pl.pallas_call(
        kernel,
        grid=(slots // tile,),
        in_specs=[
            pl.BlockSpec((1, rows), lambda i: (0, 0)),
            pl.BlockSpec((1, rows), lambda i: (0, 0)),
            pl.BlockSpec((rows, width), lambda i: (0, 0)),
        ],
        out_specs=pl.BlockSpec((tile, width), lambda i: (i, 0)),
        out_shape=jax.ShapeDtypeStruct((slots, width), tokens.dtype),
        compiler_params=GRANT,
        name="place_main",
    )(ids_row, seen, tokens)


def bucket(rows_of, key, key_col, code, valid, flag, store):
    n = key.shape[1]
    width = rows_of.shape[1]
    q = count_before(key, key_col)
    fits = valid & (q < SIDE - 1)
    lost = jnp.max(jnp.where(valid & (q >= SIDE - 1), 1.0, 0.0), axis=1, keepdims=True)
    flag = jnp.maximum(flag, lost)
    pick = pick_rows(jnp.where(fits, key * SIDE + q, -1), 8 * SIDE)
    data = jnp.dot(pick, rows_of, preferred_element_type=jnp.float32)
    which = lax.broadcasted_iota(jnp.int32, (8, n), 0)
    owned = jnp.where(fits & (which == key), (code + 1).astype(jnp.float32), 0.0)
    place = lax.broadcasted_iota(jnp.int32, (128, n), 0)
    there = jnp.where(place == q, 1.0, 0.0)
    codes = lax.dot_general(
        owned.astype(jnp.bfloat16),
        there.astype(jnp.bfloat16),
        (((1,), (1,)), ((), ())),
        preferred_element_type=jnp.float32,
    )
    lane = lax.broadcasted_iota(jnp.int32, (8, 128), 1)
    codes = jnp.where(lane == 127, flag, codes)
    wide = jnp.concatenate([codes, jnp.zeros((8, width - 128), jnp.float32)], axis=1)
    row = lax.broadcasted_iota(jnp.int32, (SIDE, width), 0)
    for k in range(8):
        note = jnp.broadcast_to(wide[k : k + 1], (SIDE, width))
        block = jnp.where(row == SIDE - 1, note, data[k * SIDE : (k + 1) * SIDE])
        store(k, block.astype(jnp.bfloat16))


def read_codes(blocks):
    n = 8 * SIDE
    lane = lax.broadcasted_iota(jnp.int32, (8, n), 1)
    codes = jnp.zeros((8, n), jnp.float32)
    flag = jnp.zeros((1, 1), jnp.float32)
    for k in range(8):
        note = blocks[k].astype(jnp.float32)[SIDE - 1 : SIDE, :n]
        flag = jnp.maximum(flag, note[:, 127:128])
        own = jnp.where(lane < SIDE - 1, jnp.broadcast_to(note, (8, n)), 0.0)
        codes = codes + (pltpu.roll(own, k * SIDE, 1) if k else own)
    return codes[:1].astype(jnp.int32) - 1, flag


def side_first(ids_row, tokens):
    rows, width = tokens.shape

    def kernel(row_ref, tok_ref, out_ref, seen_ref):
        row = row_ref[...]
        seen = count_before(row, to_col(row))
        seen_ref[...] = seen
        home = row // HERE
        spot = row % HERE
        third = seen >= MAIN
        key = home % 8

        def store(k, block):
            out_ref[k * SIDE : (k + 1) * SIDE, :] = block

        bucket(
            tok_ref[...], key, to_col(jnp.where(third, key, -1)), home // 8 * 8 + spot, third,
            jnp.zeros((1, 1), jnp.float32), store,
        )

    return pl.pallas_call(
        kernel,
        out_shape=[
            jax.ShapeDtypeStruct((8 * SIDE, width), jnp.bfloat16),
            jax.ShapeDtypeStruct((1, rows), jnp.int32),
        ],
        compiler_params=GRANT,
        name="side_first",
    )(ids_row, tokens)


def side_second(at, arrived):
    n, width = arrived.shape

    def kernel(at_ref, in_ref, *refs):
        out_refs, block_ref = refs[:8], refs[8]
        blocks = [in_ref[k * SIDE : (k + 1) * SIDE, :] for k in range(8)]
        code, flag = read_codes(blocks)
        valid = code >= 0
        key = jnp.where(valid, code // 8, -1)
        from_y = lax.broadcasted_iota(jnp.int32, (1, n), 1) // SIDE

        def store(k, block):
            block_ref[k] = block

        bucket(in_ref[...], key, to_col(key), from_y * 8 + code % 8, valid, flag, store)
        for k in range(8):
            out_refs[k][...] = block_ref[at_ref[0] ^ k]

    return pl.pallas_call(
        kernel,
        in_specs=[scalar_spec(), pl.BlockSpec(memory_space=pltpu.VMEM)],
        out_shape=[jax.ShapeDtypeStruct((SIDE, width), jnp.bfloat16)] * 8,
        scratch_shapes=[pltpu.VMEM((8, SIDE, width), jnp.bfloat16)],
        compiler_params=GRANT,
        name="side_second",
    )(at, arrived)


def fold(full, mine, rank):
    pair = 2 * rank
    lane = lax.broadcasted_iota(jnp.int32, (full.shape[0], pair), 1)
    kept = jnp.zeros((full.shape[0], pair), jnp.float32)
    for k in range(HERE // 2):
        holder = jnp.where(lane < rank, 2 * k, 2 * k + 1)
        kept = kept + jnp.where(mine == holder, full[:, k * pair : (k + 1) * pair], 0.0)
    return kept + pltpu.roll(kept, rank, 1)


def contract_last(x, y):
    return lax.dot_general(x, y, (((1,), (1,)), ((), ())), preferred_element_type=jnp.float32)


def down_main(arrived, down):
    slots, width = arrived.shape
    here, rank, _ = down.shape
    half = slots // 2
    tile = 256
    pair = 2 * rank

    def kernel(in_ref, down_ref, out_ref):
        weight = down_ref[...].reshape(here * rank, width)
        lane = lax.broadcasted_iota(jnp.int32, (tile, pair), 1)
        slot = lax.broadcasted_iota(jnp.int32, (tile, pair), 0)
        mine = slot % (HERE * MAIN) // MAIN
        for first in range(0, half, tile):
            lo = fold(contract_last(in_ref[first : first + tile, :], weight), mine, rank)
            hi = fold(
                contract_last(in_ref[half + first : half + first + tile, :], weight), mine, rank
            )
            out_ref[first : first + tile, :] = jnp.where(lane < rank, lo, hi).astype(jnp.bfloat16)

    return pl.pallas_call(
        kernel,
        out_shape=jax.ShapeDtypeStruct((half, pair), jnp.bfloat16),
        compiler_params=GRANT,
        name="down_main",
    )(arrived, down)


def side_low(at, blocks, down, main):
    here, rank, width = down.shape
    n = 8 * SIDE
    pair = 2 * rank
    share = (main.shape[0] + n // 2) // 2

    def kernel(at_ref, *refs):
        down_ref, main_ref, own_ref, other_ref, slot_ref, flag_ref, all_ref = refs[8:]
        blocks = [ref[...] for ref in refs[:8]]
        code, flag = read_codes(blocks)
        from_z = (lax.broadcasted_iota(jnp.int32, (1, n), 1) // SIDE) ^ at_ref[0]
        slot_ref[...] = jnp.where(code >= 0, from_z * 64 + code, -1)
        flag_ref[...] = jnp.broadcast_to(flag, (8, 128))
        rows_of = jnp.concatenate(blocks, axis=0)
        full = contract_last(rows_of, down_ref[...].reshape(here * rank, width))
        low = fold(full, to_col(jnp.where(code >= 0, code % HERE, -1)), rank)
        lane = lax.broadcasted_iota(jnp.int32, (n // 2, pair), 1)
        packed = jnp.where(lane < rank, low[: n // 2], low[n // 2 :]).astype(jnp.bfloat16)
        rows = jnp.concatenate([main_ref[...], packed], axis=0)
        for k in range(2):
            all_ref[k] = rows[k * share : (k + 1) * share]
        own_ref[...] = all_ref[at_ref[1]]
        other_ref[...] = all_ref[1 - at_ref[1]]

    return pl.pallas_call(
        kernel,
        in_specs=[scalar_spec()] + [pl.BlockSpec(memory_space=pltpu.VMEM)] * 10,
        out_shape=[
            jax.ShapeDtypeStruct((share, pair), jnp.bfloat16),
            jax.ShapeDtypeStruct((share, pair), jnp.bfloat16),
            jax.ShapeDtypeStruct((1, n), jnp.int32),
            jax.ShapeDtypeStruct((8, 128), jnp.float32),
        ],
        scratch_shapes=[pltpu.VMEM((2, share, pair), jnp.bfloat16)],
        compiler_params=GRANT,
        name="side_low",
    )(at, *blocks, down, main)


def chip_sum(parts):
    def kernel(in_ref, out_ref):
        total = in_ref[0].astype(jnp.float32)
        for k in range(1, parts.shape[0]):
            total = total + in_ref[k].astype(jnp.float32)
        out_ref[...] = total.astype(jnp.bfloat16)

    return pl.pallas_call(
        kernel,
        out_shape=jax.ShapeDtypeStruct(parts.shape[1:], jnp.bfloat16),
        compiler_params=GRANT,
        name="chip_sum",
    )(parts)


def up_main(low, slot, flag, up):
    here, rank, cols = up.shape
    pair = 2 * rank
    n = slot.shape[1]
    half = low.shape[0] - n // 2
    owners = 2 * half // (here * MAIN)

    def kernel(low_ref, slot_ref, flag_ref, up_ref, out_ref):
        weight = up_ref[...].reshape(here * rank, cols)

        def mapped(part, holders):
            wide = part.astype(jnp.float32)
            turned = pltpu.roll(wide, rank, 1)
            lane = lax.broadcasted_iota(jnp.int32, wide.shape, 1)
            halves = []
            for h, mine in enumerate(holders):
                both = jnp.where((lane < rank) == (h == 0), wide, turned)
                spread = []
                for k in range(here // 2):
                    holder = jnp.where(lane < rank, 2 * k, 2 * k + 1)
                    spread.append(jnp.where(mine == holder, both, 0.0).astype(jnp.bfloat16))
                halves.append(
                    jnp.dot(
                        jnp.concatenate(spread, axis=1), weight, preferred_element_type=jnp.float32
                    )
                )
            return jnp.concatenate(halves, axis=0) * adapter_output_scale

        main_slot = lax.broadcasted_iota(jnp.int32, (half, pair), 0)
        spot = main_slot % (here * MAIN) // MAIN
        main = mapped(low_ref[:half, :], (spot, spot)).reshape(owners, here * MAIN, cols)
        at = slot_ref[...]
        spot = to_col(jnp.where(at >= 0, at % here, -1))
        thirds = mapped(low_ref[half:, :], (spot[: n // 2], spot[n // 2 :]))
        thirds = jnp.dot(
            pick_rows(at, owners * here),
            thirds.astype(jnp.bfloat16),
            preferred_element_type=jnp.float32,
        ).reshape(owners, here, cols)
        both = jnp.concatenate([main, thirds], axis=1).reshape(owners * here * MOST, cols)
        out_ref[...] = jnp.where(flag_ref[:1, :1] > 0.0, LOST, both).astype(jnp.bfloat16)

    return pl.pallas_call(
        kernel,
        out_shape=jax.ShapeDtypeStruct((owners * here * MOST, cols), jnp.bfloat16),
        compiler_params=GRANT,
        name="up_main",
    )(low, slot, flag, up)


def answer_slots(ids_row, seen):
    rows = ids_row.shape[1]

    def kernel(row_ref, seen_ref, out_ref):
        row = row_ref[...]
        seen = seen_ref[...]
        spot = row % HERE
        back = row // HERE * (HERE * MOST) + jnp.where(
            seen < MAIN, spot * MAIN + seen, HERE * MAIN + spot
        )
        out_ref[...] = to_col(back)

    return pl.pallas_call(
        kernel,
        out_shape=jax.ShapeDtypeStruct((rows, 1), jnp.int32),
        compiler_params=GRANT,
        name="answer_slots",
    )(ids_row, seen)


def take_main(at_col, back, base):
    rows, cols = base.shape
    slots = back.shape[0]

    def kernel(at_ref, back_ref, base_ref, out_ref, lost_ref):
        slot = lax.broadcasted_iota(jnp.int32, (rows, slots), 1)
        pick = jnp.where(slot == at_ref[...], 1.0, 0.0).astype(jnp.bfloat16)
        mine = jnp.dot(pick, back_ref[...], preferred_element_type=jnp.float32)
        out_ref[...] = (base_ref[...] + mine).astype(jnp.bfloat16)
        lost_ref[0] = (jnp.max(back_ref[...].astype(jnp.float32)) > LOST / 2).astype(jnp.int32)

    return pl.pallas_call(
        kernel,
        out_specs=[pl.BlockSpec(memory_space=pltpu.VMEM), pl.BlockSpec(memory_space=pltpu.SMEM)],
        out_shape=[
            jax.ShapeDtypeStruct((rows, cols), jnp.bfloat16),
            jax.ShapeDtypeStruct((1,), jnp.int32),
        ],
        compiler_params=GRANT,
        name="take_main",
    )(at_col, back, base)


def low_of_all(low_part, groups):
    rows, pair = low_part.shape
    parts = swap(low_part.reshape(groups, rows // groups, pair), TENSOR)
    share = parts.astype(jnp.float32).sum(axis=0).astype(jnp.bfloat16)
    copies = jnp.broadcast_to(share[None], (groups, *share.shape))
    return swap(copies, TENSOR).reshape(rows, pair)


def low_of_pairs(own, other):
    rounded = own.astype(jnp.float32)
    rounded = rounded + lax.ppermute(other, TENSOR[1], [(0, 1), (1, 0)]).astype(jnp.float32)
    chips = lax.axis_size(TENSOR[0])
    copies = jnp.broadcast_to(rounded.astype(jnp.bfloat16)[None], (chips, *own.shape))
    total = chip_sum(swap(copies, TENSOR[0]))
    return lax.all_gather(total, TENSOR[1], axis=0, tiled=True)


def whole_exchange(tokens, adapter_down, adapter_up_weight, adapter_ids, base):
    rows, width = tokens.shape
    cols = adapter_up_weight.shape[2]
    share = HERE * MOST
    slots = 64 * share
    placed, at_col = full_place(adapter_ids.reshape(1, rows), tokens, slots)
    arrived = swap(placed.reshape(64, share, width), ADAPTER).reshape(slots, width)
    low = low_of_all(full_down(arrived, adapter_down), lax.axis_size(TENSOR))
    delta = full_up(low, adapter_up_weight)
    back = swap(delta.reshape(64, share, cols), ADAPTER).reshape(slots, cols)
    return full_take(at_col, back, base)


def layer(tokens, value_weight, adapter_down, adapter_up_weight, adapter_ids):
    groups = lax.axis_size(TENSOR)
    rows, width = tokens.shape
    cols = adapter_up_weight.shape[2]
    ids_row = adapter_ids.reshape(1, rows)
    at_z = lax.axis_index("z").astype(jnp.int32)

    blocks, seen = side_first(ids_row, tokens)
    blocks = swap(blocks.reshape(8, SIDE, width), "y").reshape(8 * SIDE, width)
    placed = place_main(ids_row, seen, tokens, 64 * HERE * MAIN)
    at_col = answer_slots(ids_row, seen)
    arrived = swap(placed.reshape(64, HERE * MAIN, width), ADAPTER)
    arrived = arrived.reshape(64 * HERE * MAIN, width)

    blocks = side_second(at_z.reshape(1), blocks)
    blocks = xor_sends(blocks, "z")
    at = lax.axis_index(TENSOR).astype(jnp.int32).reshape(1)
    own, other = value_pieces(tokens, value_weight, at, groups)
    other = lax.ppermute(other, TENSOR[1], [(0, 1), (1, 0)])
    pairs = pair_sum(own, other)
    pairs = xor_sends([own, *pairs], TENSOR[0])[1:]
    base = base_sum(own, other, pairs)

    main = down_main(arrived, adapter_down)
    core = lax.axis_index(TENSOR[1]).astype(jnp.int32)
    own, other, slot, flag = side_low(jnp.stack([at_z, core]), blocks, adapter_down, main)
    low = low_of_pairs(own, other)
    delta = up_main(low, slot, flag, adapter_up_weight)
    back = swap(delta.reshape(64, HERE * MOST, cols), ADAPTER)
    back = back.reshape(64 * HERE * MOST, cols)
    back, *whole = lax.optimization_barrier(
        (back, tokens, adapter_down, adapter_up_weight, adapter_ids, base)
    )
    values, lost = take_main(at_col, back, base)
    return lax.cond(
        lost[0] > 0,
        lambda: whole_exchange(*whole),
        lambda: values,
    )


def xor_sends(pieces, axis):
    size = lax.axis_size(axis)
    parts = [pieces[0]]
    for k in range(1, size):
        parts.append(lax.ppermute(pieces[k], axis, [(i, i ^ k) for i in range(size)]))
    return parts


def solution(mesh):
    torus = Mesh(mesh.devices.reshape(8, 8, 4, 2), (*ADAPTER, *TENSOR))
    return jax.shard_map(
        layer,
        mesh=torus,
        in_specs=(
            P(ADAPTER, TENSOR),
            P(TENSOR, None),
            P(ADAPTER, None, TENSOR),
            P(ADAPTER, None, TENSOR),
            P(ADAPTER, None),
        ),
        out_specs=P(ADAPTER, TENSOR),
        check_vma=False,
    )
```

```python
import jax
import jax.numpy as jnp
from jax import lax
from jax.experimental import pallas as pl
from jax.experimental.pallas import tpu as pltpu
from jax.sharding import Mesh
from jax.sharding import PartitionSpec as P


TENSOR = ("tensor_0", "tensor_1")
ADAPTER = ("z", "y")
HERE = 8
MOST = 3
MAIN = 2
SIDE = 16
LOST = 3e38
GRANT = pltpu.CompilerParams(vmem_limit_bytes=16 * 2**20)

adapter_output_scale = 2.0


def swap(x, axes):
    return lax.all_to_all(x, axes, split_axis=0, concat_axis=0, tiled=True)


def full_place(ids_row, tokens, slots):
    rows, width = tokens.shape
    tile = 256

    def kernel(row_ref, tok_ref, out_ref, at_col_ref, at_row_ref):
        @pl.when(pl.program_id(0) == 0)
        def _():
            row = row_ref[...]
            col = jnp.broadcast_to(row, (128, rows)).T[:, :1]
            same = row == col
            i = lax.broadcasted_iota(jnp.int32, (rows, rows), 0)
            j = lax.broadcasted_iota(jnp.int32, (rows, rows), 1)
            before_row = jnp.sum(jnp.where(same & (i < j), 1, 0), axis=0, keepdims=True)
            before_col = jnp.sum(jnp.where(same & (j < i), 1, 0), axis=1, keepdims=True)
            at_row_ref[...] = row * MOST + before_row
            at_col_ref[...] = col * MOST + before_col

        first = pl.program_id(0) * tile
        slot = lax.broadcasted_iota(jnp.int32, (tile, rows), 0) + first
        pick = jnp.where(slot == at_row_ref[...], 1.0, 0.0).astype(jnp.bfloat16)
        out_ref[...] = jnp.dot(pick, tok_ref[...], preferred_element_type=jnp.float32).astype(
            jnp.bfloat16
        )

    return pl.pallas_call(
        kernel,
        grid=(slots // tile,),
        in_specs=[
            pl.BlockSpec((1, rows), lambda i: (0, 0)),
            pl.BlockSpec((rows, width), lambda i: (0, 0)),
        ],
        out_specs=[
            pl.BlockSpec((tile, width), lambda i: (i, 0)),
            pl.BlockSpec((rows, 1), lambda i: (0, 0)),
        ],
        out_shape=[
            jax.ShapeDtypeStruct((slots, width), tokens.dtype),
            jax.ShapeDtypeStruct((rows, 1), jnp.int32),
        ],
        scratch_shapes=[pltpu.VMEM((1, rows), jnp.int32)],
        compiler_params=GRANT,
        name="full_place",
    )(ids_row, tokens)


def value_pieces(tokens, weight, at, pieces):
    rows, width = tokens.shape
    cols = weight.shape[1] // pieces
    step = 2

    def kernel(at_ref, tok_ref, w_ref, own_ref, other_ref, part_ref):
        for first in range(0, pieces, step):
            part = jnp.dot(
                tok_ref[...],
                w_ref[:, first * cols : (first + step) * cols],
                preferred_element_type=jnp.float32,
            ).astype(jnp.bfloat16)
            for k in range(step):
                part_ref[first + k] = part[:, k * cols : (k + 1) * cols]
        for k in range(pieces // 2):
            own_ref[k] = part_ref[at_ref[0] ^ (2 * k)]
            other_ref[k] = part_ref[at_ref[0] ^ (2 * k + 1)]

    return pl.pallas_call(
        kernel,
        in_specs=[
            pl.BlockSpec(memory_space=pltpu.SMEM),
            pl.BlockSpec((rows, width), lambda: (0, 0)),
            pl.BlockSpec(weight.shape, lambda: (0, 0)),
        ],
        out_shape=[jax.ShapeDtypeStruct((pieces // 2, rows, cols), jnp.bfloat16)] * 2,
        scratch_shapes=[pltpu.VMEM((pieces, rows, cols), jnp.bfloat16)],
        compiler_params=GRANT,
        name="value_pieces",
    )(at, tokens, weight)


def pair_sum(own, other):
    count, rows, cols = own.shape

    def kernel(own_ref, other_ref, *out_refs):
        for k in range(1, count):
            total = own_ref[k].astype(jnp.float32) + other_ref[k].astype(jnp.float32)
            out_refs[k - 1][...] = total.astype(jnp.bfloat16)

    return pl.pallas_call(
        kernel,
        out_shape=[jax.ShapeDtypeStruct((rows, cols), jnp.bfloat16)] * (count - 1),
        compiler_params=GRANT,
        name="pair_sum",
    )(own, other)


def base_sum(own, other, parts):
    def kernel(own_ref, other_ref, *refs):
        total = own_ref[0].astype(jnp.float32) + other_ref[0].astype(jnp.float32)
        for ref in refs[:-1]:
            total = total + ref[...].astype(jnp.float32)
        refs[-1][...] = total

    return pl.pallas_call(
        kernel,
        out_shape=jax.ShapeDtypeStruct(parts[0].shape, jnp.float32),
        compiler_params=GRANT,
        name="base_sum",
    )(own, other, *parts)


def adapter_of(shape, first, group):
    slot = lax.broadcasted_iota(jnp.int32, shape, 0) + first
    return slot % group // MOST


def full_down(arrived, down):
    slots, width = arrived.shape
    here, rank, _ = down.shape
    group = here * MOST
    half = slots // 2
    tile = 192
    pair = 2 * rank

    def kernel(lo_ref, hi_ref, down_ref, out_ref):
        weight = down_ref[...].reshape(here * rank, width)
        lane = lax.broadcasted_iota(jnp.int32, (tile, pair), 1)

        def rows_of(ref):
            full = lax.dot_general(
                ref[...], weight, (((1,), (1,)), ((), ())), preferred_element_type=jnp.float32
            )
            mine = adapter_of((tile, pair), 0, group)
            kept = jnp.zeros((tile, pair), jnp.float32)
            for k in range(here // 2):
                holder = jnp.where(lane < rank, 2 * k, 2 * k + 1)
                kept = kept + jnp.where(mine == holder, full[:, k * pair : (k + 1) * pair], 0.0)
            return kept + pltpu.roll(kept, rank, 1)

        out_ref[...] = jnp.where(lane < rank, rows_of(lo_ref), rows_of(hi_ref)).astype(
            jnp.bfloat16
        )

    steps = half // tile
    return pl.pallas_call(
        kernel,
        grid=(steps,),
        in_specs=[
            pl.BlockSpec((tile, width), lambda i: (i, 0)),
            pl.BlockSpec((tile, width), lambda i: (i + steps, 0)),
            pl.BlockSpec((here, rank, width), lambda i: (0, 0, 0)),
        ],
        out_specs=pl.BlockSpec((tile, pair), lambda i: (i, 0)),
        out_shape=jax.ShapeDtypeStruct((half, pair), jnp.bfloat16),
        compiler_params=GRANT,
        name="full_down",
    )(arrived, arrived, down)


def full_up(low, up):
    half, pair = low.shape
    here, rank, cols = up.shape
    group = here * MOST

    def kernel(low_ref, up_ref, out_ref):
        weight = up_ref[...].reshape(here * rank, cols)
        low_wide = low_ref[...].astype(jnp.float32)
        turned = pltpu.roll(low_wide, rank, 1)
        lane = lax.broadcasted_iota(jnp.int32, (half, pair), 1)
        mine = adapter_of((half, pair), 0, group)
        for h in range(2):
            own = (lane < rank) == (h == 0)
            both = jnp.where(own, low_wide, turned)
            spread = []
            for k in range(here // 2):
                holder = jnp.where(lane < rank, 2 * k, 2 * k + 1)
                spread.append(jnp.where(mine == holder, both, 0.0).astype(jnp.bfloat16))
            acc = jnp.dot(
                jnp.concatenate(spread, axis=1), weight, preferred_element_type=jnp.float32
            )
            out_ref[h * half : (h + 1) * half, :] = (adapter_output_scale * acc).astype(
                jnp.bfloat16
            )

    return pl.pallas_call(
        kernel,
        out_shape=jax.ShapeDtypeStruct((2 * half, cols), jnp.bfloat16),
        compiler_params=GRANT,
        name="full_up",
    )(low, up)


def full_take(at_col, back, base):
    rows, cols = base.shape
    slots = back.shape[0]

    def kernel(at_ref, back_ref, base_ref, out_ref):
        slot = lax.broadcasted_iota(jnp.int32, (rows, slots), 1)
        pick = jnp.where(slot == at_ref[...], 1.0, 0.0).astype(jnp.bfloat16)
        mine = jnp.dot(pick, back_ref[...], preferred_element_type=jnp.float32)
        out_ref[...] = (base_ref[...] + mine).astype(jnp.bfloat16)

    return pl.pallas_call(
        kernel,
        out_shape=jax.ShapeDtypeStruct((rows, cols), jnp.bfloat16),
        compiler_params=GRANT,
        name="full_take",
    )(at_col, back, base)


def scalar_spec():
    return pl.BlockSpec(memory_space=pltpu.SMEM)


def count_before(row, col):
    n = row.shape[1]
    j = lax.broadcasted_iota(jnp.int32, (n, n), 0)
    i = lax.broadcasted_iota(jnp.int32, (n, n), 1)
    return jnp.sum(jnp.where((row == col) & (j < i), 1, 0), axis=0, keepdims=True)


def to_col(row):
    return jnp.broadcast_to(row, (128, row.shape[1])).T[:, :1]


def pick_rows(at_row, slots, first=0):
    n = at_row.shape[1]
    slot = lax.broadcasted_iota(jnp.int32, (slots, n), 0) + first
    return jnp.where(slot == at_row, 1.0, 0.0).astype(jnp.bfloat16)


def place_main(ids_row, seen, tokens, slots):
    rows, width = tokens.shape
    tile = 512

    def kernel(row_ref, seen_ref, tok_ref, out_ref):
        at_row = jnp.where(seen_ref[...] < MAIN, row_ref[...] * MAIN + seen_ref[...], -1)
        pick = pick_rows(at_row, tile, pl.program_id(0) * tile)
        out_ref[...] = jnp.dot(pick, tok_ref[...], preferred_element_type=jnp.float32).astype(
            jnp.bfloat16
        )

    return pl.pallas_call(
        kernel,
        grid=(slots // tile,),
        in_specs=[
            pl.BlockSpec((1, rows), lambda i: (0, 0)),
            pl.BlockSpec((1, rows), lambda i: (0, 0)),
            pl.BlockSpec((rows, width), lambda i: (0, 0)),
        ],
        out_specs=pl.BlockSpec((tile, width), lambda i: (i, 0)),
        out_shape=jax.ShapeDtypeStruct((slots, width), tokens.dtype),
        compiler_params=GRANT,
        name="place_main",
    )(ids_row, seen, tokens)


def bucket(rows_of, key, key_col, code, valid, flag, store):
    n = key.shape[1]
    q = count_before(key, key_col)
    fits = valid & (q < SIDE - 1)
    lost = jnp.max(jnp.where(valid & (q >= SIDE - 1), 1.0, 0.0), axis=1, keepdims=True)
    flag = jnp.maximum(flag, lost)
    pick = pick_rows(jnp.where(fits, key * SIDE + q, -1), 8 * SIDE)
    data = jnp.dot(pick, rows_of(), preferred_element_type=jnp.float32)
    width = data.shape[1]
    which = lax.broadcasted_iota(jnp.int32, (8, n), 0)
    owned = jnp.where(fits & (which == key), (code + 1).astype(jnp.float32), 0.0)
    place = lax.broadcasted_iota(jnp.int32, (128, n), 0)
    there = jnp.where(place == q, 1.0, 0.0)
    codes = lax.dot_general(
        owned.astype(jnp.bfloat16),
        there.astype(jnp.bfloat16),
        (((1,), (1,)), ((), ())),
        preferred_element_type=jnp.float32,
    )
    lane = lax.broadcasted_iota(jnp.int32, (8, 128), 1)
    codes = jnp.where(lane == 127, flag, codes)
    wide = jnp.concatenate([codes, jnp.zeros((8, width - 128), jnp.float32)], axis=1)
    row = lax.broadcasted_iota(jnp.int32, (SIDE, width), 0)
    for k in range(8):
        note = jnp.broadcast_to(wide[k : k + 1], (SIDE, width))
        block = jnp.where(row == SIDE - 1, note, data[k * SIDE : (k + 1) * SIDE])
        store(k, block.astype(jnp.bfloat16))


def read_codes(blocks):
    n = 8 * SIDE
    lane = lax.broadcasted_iota(jnp.int32, (8, n), 1)
    codes = jnp.zeros((8, n), jnp.float32)
    flag = jnp.zeros((1, 1), jnp.float32)
    for k in range(8):
        note = blocks[k].astype(jnp.float32)[SIDE - 1 : SIDE, :n]
        flag = jnp.maximum(flag, note[:, 127:128])
        own = jnp.where(lane < SIDE - 1, jnp.broadcast_to(note, (8, n)), 0.0)
        codes = codes + (pltpu.roll(own, k * SIDE, 1) if k else own)
    return codes[:1].astype(jnp.int32) - 1, flag


def side_first(ids_row, tokens):
    rows, width = tokens.shape

    def kernel(row_ref, tok_ref, out_ref, seen_ref, buffer_ref, sem):
        load = pltpu.make_async_copy(tok_ref, buffer_ref, sem)
        load.start()
        row = row_ref[...]
        seen = count_before(row, to_col(row))
        seen_ref[...] = seen
        home = row // HERE
        spot = row % HERE
        third = seen >= MAIN
        key = home % 8

        def rows_of():
            load.wait()
            return buffer_ref[...]

        def store(k, block):
            out_ref[k * SIDE : (k + 1) * SIDE, :] = block

        bucket(
            rows_of, key, to_col(jnp.where(third, key, -1)), home // 8 * 8 + spot, third,
            jnp.zeros((1, 1), jnp.float32), store,
        )

    return pl.pallas_call(
        kernel,
        in_specs=[pl.BlockSpec(memory_space=pltpu.VMEM), pl.BlockSpec(memory_space=pl.ANY)],
        scratch_shapes=[pltpu.VMEM((rows, width), tokens.dtype), pltpu.SemaphoreType.DMA],
        out_shape=[
            jax.ShapeDtypeStruct((8 * SIDE, width), jnp.bfloat16),
            jax.ShapeDtypeStruct((1, rows), jnp.int32),
        ],
        compiler_params=GRANT,
        name="side_first",
    )(ids_row, tokens)


def side_second(at, arrived):
    n, width = arrived.shape

    def kernel(at_ref, in_ref, *refs):
        out_refs, block_ref = refs[:8], refs[8]
        blocks = [in_ref[k * SIDE : (k + 1) * SIDE, :] for k in range(8)]
        code, flag = read_codes(blocks)
        valid = code >= 0
        key = jnp.where(valid, code // 8, -1)
        from_y = lax.broadcasted_iota(jnp.int32, (1, n), 1) // SIDE

        def store(k, block):
            block_ref[k] = block

        bucket(lambda: in_ref[...], key, to_col(key), from_y * 8 + code % 8, valid, flag, store)
        for k in range(8):
            out_refs[k][...] = block_ref[at_ref[0] ^ k]

    return pl.pallas_call(
        kernel,
        in_specs=[scalar_spec(), pl.BlockSpec(memory_space=pltpu.VMEM)],
        out_shape=[jax.ShapeDtypeStruct((SIDE, width), jnp.bfloat16)] * 8,
        scratch_shapes=[pltpu.VMEM((8, SIDE, width), jnp.bfloat16)],
        compiler_params=GRANT,
        name="side_second",
    )(at, arrived)


def fold(full, mine, rank):
    pair = 2 * rank
    lane = lax.broadcasted_iota(jnp.int32, (full.shape[0], pair), 1)
    kept = jnp.zeros((full.shape[0], pair), jnp.float32)
    for k in range(HERE // 2):
        holder = jnp.where(lane < rank, 2 * k, 2 * k + 1)
        kept = kept + jnp.where(mine == holder, full[:, k * pair : (k + 1) * pair], 0.0)
    return kept + pltpu.roll(kept, rank, 1)


def contract_last(x, y):
    return lax.dot_general(x, y, (((1,), (1,)), ((), ())), preferred_element_type=jnp.float32)


def down_main(arrived, down):
    slots, width = arrived.shape
    here, rank, _ = down.shape
    half = slots // 2
    tile = half
    pair = 2 * rank

    def kernel(in_ref, down_ref, out_ref):
        weight = down_ref[...].reshape(here * rank, width)
        lane = lax.broadcasted_iota(jnp.int32, (tile, pair), 1)
        slot = lax.broadcasted_iota(jnp.int32, (tile, pair), 0)
        mine = slot % (HERE * MAIN) // MAIN
        for first in range(0, half, tile):
            lo = fold(contract_last(in_ref[first : first + tile, :], weight), mine, rank)
            hi = fold(
                contract_last(in_ref[half + first : half + first + tile, :], weight), mine, rank
            )
            out_ref[first : first + tile, :] = jnp.where(lane < rank, lo, hi).astype(jnp.bfloat16)

    return pl.pallas_call(
        kernel,
        out_shape=jax.ShapeDtypeStruct((half, pair), jnp.bfloat16),
        compiler_params=GRANT,
        name="down_main",
    )(arrived, down)


def side_low(at, blocks, down, main):
    here, rank, width = down.shape
    n = 8 * SIDE
    pair = 2 * rank
    share = (main.shape[0] + n // 2) // 2

    def kernel(at_ref, *refs):
        down_ref, main_ref, own_ref, other_ref, slot_ref, flag_ref, all_ref = refs[8:]
        blocks = [ref[...] for ref in refs[:8]]
        code, flag = read_codes(blocks)
        from_z = (lax.broadcasted_iota(jnp.int32, (1, n), 1) // SIDE) ^ at_ref[0]
        slot_ref[...] = jnp.where(code >= 0, from_z * 64 + code, -1)
        flag_ref[...] = jnp.broadcast_to(flag, (8, 128))
        rows_of = jnp.concatenate(blocks, axis=0)
        full = contract_last(rows_of, down_ref[...].reshape(here * rank, width))
        low = fold(full, to_col(jnp.where(code >= 0, code % HERE, -1)), rank)
        lane = lax.broadcasted_iota(jnp.int32, (n // 2, pair), 1)
        packed = jnp.where(lane < rank, low[: n // 2], low[n // 2 :]).astype(jnp.bfloat16)
        rows = jnp.concatenate([main_ref[...], packed], axis=0)
        for k in range(2):
            all_ref[k] = rows[k * share : (k + 1) * share]
        own_ref[...] = all_ref[at_ref[1]]
        other_ref[...] = all_ref[1 - at_ref[1]]

    return pl.pallas_call(
        kernel,
        in_specs=[scalar_spec()] + [pl.BlockSpec(memory_space=pltpu.VMEM)] * 10,
        out_shape=[
            jax.ShapeDtypeStruct((share, pair), jnp.bfloat16),
            jax.ShapeDtypeStruct((share, pair), jnp.bfloat16),
            jax.ShapeDtypeStruct((1, n), jnp.int32),
            jax.ShapeDtypeStruct((8, 128), jnp.float32),
        ],
        scratch_shapes=[pltpu.VMEM((2, share, pair), jnp.bfloat16)],
        compiler_params=GRANT,
        name="side_low",
    )(at, *blocks, down, main)


def chip_sum(parts):
    def kernel(in_ref, out_ref):
        total = in_ref[0].astype(jnp.float32)
        for k in range(1, parts.shape[0]):
            total = total + in_ref[k].astype(jnp.float32)
        out_ref[...] = total.astype(jnp.bfloat16)

    return pl.pallas_call(
        kernel,
        out_shape=jax.ShapeDtypeStruct(parts.shape[1:], jnp.bfloat16),
        compiler_params=GRANT,
        name="chip_sum",
    )(parts)


def up_main(low, slot, flag, up):
    here, rank, cols = up.shape
    pair = 2 * rank
    n = slot.shape[1]
    half = low.shape[0] - n // 2
    owners = 2 * half // (here * MAIN)

    def kernel(low_ref, slot_ref, flag_ref, up_ref, out_ref):
        weight = up_ref[...].reshape(here * rank, cols)

        def mapped(part, holders):
            wide = part.astype(jnp.float32)
            turned = pltpu.roll(wide, rank, 1)
            lane = lax.broadcasted_iota(jnp.int32, wide.shape, 1)
            halves = []
            for h, mine in enumerate(holders):
                both = jnp.where((lane < rank) == (h == 0), wide, turned)
                spread = []
                for k in range(here // 2):
                    holder = jnp.where(lane < rank, 2 * k, 2 * k + 1)
                    spread.append(jnp.where(mine == holder, both, 0.0).astype(jnp.bfloat16))
                halves.append(
                    jnp.dot(
                        jnp.concatenate(spread, axis=1), weight, preferred_element_type=jnp.float32
                    )
                )
            return jnp.concatenate(halves, axis=0) * adapter_output_scale

        main_slot = lax.broadcasted_iota(jnp.int32, (half, pair), 0)
        spot = main_slot % (here * MAIN) // MAIN
        main = mapped(low_ref[:half, :], (spot, spot)).reshape(owners, here * MAIN, cols)
        at = slot_ref[...]
        spot = to_col(jnp.where(at >= 0, at % here, -1))
        thirds = mapped(low_ref[half:, :], (spot[: n // 2], spot[n // 2 :]))
        thirds = jnp.dot(
            pick_rows(at, owners * here),
            thirds.astype(jnp.bfloat16),
            preferred_element_type=jnp.float32,
        ).reshape(owners, here, cols)
        both = jnp.concatenate([main, thirds], axis=1).reshape(owners * here * MOST, cols)
        out_ref[...] = jnp.where(flag_ref[:1, :1] > 0.0, LOST, both).astype(jnp.bfloat16)

    return pl.pallas_call(
        kernel,
        out_shape=jax.ShapeDtypeStruct((owners * here * MOST, cols), jnp.bfloat16),
        compiler_params=GRANT,
        name="up_main",
    )(low, slot, flag, up)


def answer_slots(ids_row, seen):
    rows = ids_row.shape[1]

    def kernel(row_ref, seen_ref, out_ref):
        row = row_ref[...]
        seen = seen_ref[...]
        spot = row % HERE
        back = row // HERE * (HERE * MOST) + jnp.where(
            seen < MAIN, spot * MAIN + seen, HERE * MAIN + spot
        )
        out_ref[...] = to_col(back)

    return pl.pallas_call(
        kernel,
        out_shape=jax.ShapeDtypeStruct((rows, 1), jnp.int32),
        compiler_params=GRANT,
        name="answer_slots",
    )(ids_row, seen)


def take_main(at_col, back, base):
    rows, cols = base.shape
    slots = back.shape[0]

    def kernel(at_ref, back_ref, base_ref, out_ref, lost_ref):
        slot = lax.broadcasted_iota(jnp.int32, (rows, slots), 1)
        pick = jnp.where(slot == at_ref[...], 1.0, 0.0).astype(jnp.bfloat16)
        mine = jnp.dot(pick, back_ref[...], preferred_element_type=jnp.float32)
        out_ref[...] = (base_ref[...] + mine).astype(jnp.bfloat16)
        lost_ref[0] = (jnp.max(back_ref[...].astype(jnp.float32)) > LOST / 2).astype(jnp.int32)

    return pl.pallas_call(
        kernel,
        out_specs=[pl.BlockSpec(memory_space=pltpu.VMEM), pl.BlockSpec(memory_space=pltpu.SMEM)],
        out_shape=[
            jax.ShapeDtypeStruct((rows, cols), jnp.bfloat16),
            jax.ShapeDtypeStruct((1,), jnp.int32),
        ],
        compiler_params=GRANT,
        name="take_main",
    )(at_col, back, base)


def low_of_all(low_part, groups):
    rows, pair = low_part.shape
    parts = swap(low_part.reshape(groups, rows // groups, pair), TENSOR)
    share = parts.astype(jnp.float32).sum(axis=0).astype(jnp.bfloat16)
    copies = jnp.broadcast_to(share[None], (groups, *share.shape))
    return swap(copies, TENSOR).reshape(rows, pair)


def low_of_pairs(own, other):
    rounded = own.astype(jnp.float32)
    rounded = rounded + lax.ppermute(other, TENSOR[1], [(0, 1), (1, 0)]).astype(jnp.float32)
    chips = lax.axis_size(TENSOR[0])
    copies = jnp.broadcast_to(rounded.astype(jnp.bfloat16)[None], (chips, *own.shape))
    total = chip_sum(swap(copies, TENSOR[0]))
    return lax.all_gather(total, TENSOR[1], axis=0, tiled=True)


def whole_exchange(tokens, adapter_down, adapter_up_weight, adapter_ids, base):
    rows, width = tokens.shape
    cols = adapter_up_weight.shape[2]
    share = HERE * MOST
    slots = 64 * share
    placed, at_col = full_place(adapter_ids.reshape(1, rows), tokens, slots)
    arrived = swap(placed.reshape(64, share, width), ADAPTER).reshape(slots, width)
    low = low_of_all(full_down(arrived, adapter_down), lax.axis_size(TENSOR))
    delta = full_up(low, adapter_up_weight)
    back = swap(delta.reshape(64, share, cols), ADAPTER).reshape(slots, cols)
    return full_take(at_col, back, base)


def layer(tokens, value_weight, adapter_down, adapter_up_weight, adapter_ids):
    groups = lax.axis_size(TENSOR)
    rows, width = tokens.shape
    cols = adapter_up_weight.shape[2]
    ids_row = adapter_ids.reshape(1, rows)
    at_z = lax.axis_index("z").astype(jnp.int32)

    blocks, seen = side_first(ids_row, tokens)
    blocks = swap(blocks.reshape(8, SIDE, width), "y").reshape(8 * SIDE, width)
    placed = place_main(ids_row, seen, tokens, 64 * HERE * MAIN)
    at_col = answer_slots(ids_row, seen)
    arrived = swap(placed.reshape(64, HERE * MAIN, width), ADAPTER)
    arrived = arrived.reshape(64 * HERE * MAIN, width)

    blocks = side_second(at_z.reshape(1), blocks)
    blocks = xor_sends(blocks, "z")
    at = lax.axis_index(TENSOR).astype(jnp.int32).reshape(1)
    own, other = value_pieces(tokens, value_weight, at, groups)
    other = lax.ppermute(other, TENSOR[1], [(0, 1), (1, 0)])
    pairs = pair_sum(own, other)
    pairs = xor_sends([own, *pairs], TENSOR[0])[1:]
    base = base_sum(own, other, pairs)

    main = down_main(arrived, adapter_down)
    core = lax.axis_index(TENSOR[1]).astype(jnp.int32)
    own, other, slot, flag = side_low(jnp.stack([at_z, core]), blocks, adapter_down, main)
    low = low_of_pairs(own, other)
    delta = up_main(low, slot, flag, adapter_up_weight)
    back = swap(delta.reshape(64, HERE * MOST, cols), ADAPTER)
    back = back.reshape(64 * HERE * MOST, cols)
    back, *whole = lax.optimization_barrier(
        (back, tokens, adapter_down, adapter_up_weight, adapter_ids, base)
    )
    values, lost = take_main(at_col, back, base)
    return lax.cond(
        lost[0] > 0,
        lambda: whole_exchange(*whole),
        lambda: values,
    )


def xor_sends(pieces, axis):
    size = lax.axis_size(axis)
    parts = [pieces[0]]
    for k in range(1, size):
        parts.append(lax.ppermute(pieces[k], axis, [(i, i ^ k) for i in range(size)]))
    return parts


def solution(mesh):
    torus = Mesh(mesh.devices.reshape(8, 8, 4, 2), (*ADAPTER, *TENSOR))
    return jax.shard_map(
        layer,
        mesh=torus,
        in_specs=(
            P(ADAPTER, TENSOR),
            P(TENSOR, None),
            P(ADAPTER, None, TENSOR),
            P(ADAPTER, None, TENSOR),
            P(ADAPTER, None),
        ),
        out_specs=P(ADAPTER, TENSOR),
        check_vma=False,
    )
```
